32 devices in a mesh: dp: 2 (over x), fsdp: 16 (over z, y, core).
Axes of the slice: x: 2, y: 2, z: 4, core: 2. Of those that a mesh axis runs over, the one named last changes fastest.
Arguments:
- tokens: bfloat16 [18432, 768], P(('dp', 'fsdp')), may hold values from -6 to 6
- gain_attn: bfloat16 [768], P(('dp', 'fsdp')), may hold values from 0.25 to 1.75
- w_qkv: bfloat16 [768, 2304], P(('dp', 'fsdp')), may hold values from -0.21875 to 0.21875
- w_proj: bfloat16 [768, 768], P(('dp', 'fsdp')), may hold values from -2.5 to 2.5
- gain_moe: bfloat16 [768], P(('dp', 'fsdp')), may hold values from 0.25 to 1.75
- w_router: bfloat16 [768, 8], P(('dp', 'fsdp')), may hold values from -0.15625 to 0.15625
- w_in: bfloat16 [8, 768, 3072], P('dp', 'fsdp'), may hold values from -0.21875 to 0.21875
- w_out: bfloat16 [8, 3072, 768], P('dp', 'fsdp'), may hold values from -0.875 to 0.875
- routes: int32 [18432, 2], P(('dp', 'fsdp')), may hold values from 0 to 7, as said below
- slot_ids: int32 [18432, 2], P(('dp', 'fsdp')), may hold values from 0 to 152, as said below
- cotangent: bfloat16 [18432, 768], P(('dp', 'fsdp')), may hold values from -6 to 6
Outputs:
- output: bfloat16 [18432, 768], P(('dp', 'fsdp'))
- grad_tokens: float32 [18432, 768], P(('dp', 'fsdp'))
- d_gain_attn: float32 [768], P(('dp', 'fsdp'))
- d_qkv: float32 [768, 2304], P(('dp', 'fsdp'))
- d_proj: float32 [768, 768], P(('dp', 'fsdp'))
- d_gain_moe: float32 [768], P(('dp', 'fsdp'))
- d_router: float32 [768, 8], P(('dp', 'fsdp'))
- d_in: float32 [8, 768, 3072], P('dp', 'fsdp')
- d_out: float32 [8, 3072, 768], P('dp', 'fsdp')
The draws below stay inside these ranges and needn't reach their ends.
Inputs may be any that keep to these rules, and one draw needn't show every extreme that they name: `routes`: each row names two different experts. `slot_ids`: among the 576 patches of one device, the pairs routed to one expert hold the distinct slots 0, 1, 2, ... in some priority order; a pair beyond the 152 slots holds 152 and is dropped. On every device some expert gets more than 152 pairs.
All inputs are finite; a program needn't handle non-finite values.
Results may differ from the reference program's by a relative error of at most 0.017.
Values may be sent and summed in bfloat16 or wider, within the bound.
No kernel may reach another device: no remote copies, remote signals or barrier semaphores. Data moves between devices by JAX's collectives and lax.ppermute only.
A program may use at most 320 MiB of HBM per device.

```python
import jax
import jax.numpy as jnp
from jax import lax

D = 768
HEADS = 12
HEAD_DIM = 64
F = 3072
EXPERTS = 8
SEQ = 576
TOK_DEV = 576
TOKENS = 18432
CAP = 152


def route_tables(key):
    base_key = jax.random.fold_in(key, 7)
    device_count = TOKENS // TOK_DEV
    device_keys = jax.random.split(base_key, device_count)
    forced = min(TOK_DEV, CAP + 16)

    def one_device(device_key):
        pick_key, order_key, first_key, second_key, crowd_key = jax.random.split(device_key, 5)
        crowded = jax.random.randint(crowd_key, (), 0, EXPERTS)
        position_rank = jax.random.permutation(pick_key, TOK_DEV)
        first_choice = jax.random.randint(first_key, (TOK_DEV,), 0, EXPERTS)
        first_choice = jnp.where(position_rank < forced, crowded, first_choice).astype(jnp.int32)
        second = ((first_choice + jax.random.randint(second_key, (TOK_DEV,), 1, EXPERTS)) % EXPERTS).astype(jnp.int32)
        priority = jax.random.permutation(order_key, TOK_DEV)
        queued = jnp.concatenate([first_choice[priority], second[priority]])
        matches = (queued[:, None] == jnp.arange(EXPERTS, dtype=jnp.int32)[None, :]).astype(jnp.int32)
        before = jnp.cumsum(matches, axis=0) - matches
        slot_index = jnp.minimum(jnp.sum(before * matches, axis=1), CAP).astype(jnp.int32)
        slot_index = slot_index.reshape(2, TOK_DEV)
        table = jnp.zeros((TOK_DEV, 2), jnp.int32)
        table = table.at[priority, 0].set(slot_index[0]).at[priority, 1].set(slot_index[1])
        return (jnp.stack([first_choice, second], axis=1), table)
    route_rows, slot_rows = jax.vmap(one_device)(device_keys)
    return (route_rows.reshape(TOKENS, 2), slot_rows.reshape(TOKENS, 2))


def draw_routes(key, part):
    return route_tables(key)[0]


def draw_slot_ids(key, part):
    return route_tables(key)[1]


def raised(drawn, own_key, source, target, blocks, factor):
    owner, partner = [(jnp.arange(drawn.shape[position]) // (drawn.shape[position] // blocks)).reshape([-1 if axis == position else 1 for axis in range(drawn.ndim)]) for position in (source, target)]
    chosen = jax.random.permutation(own_key, blocks)[partner]
    strong = (owner == chosen) | (owner == (partner + blocks // 2) % blocks)
    return jnp.where(strong, factor * drawn, drawn)


def steps_of(key, shape, cuts, least, top_value):
    def one(axis_at, parts):
        steps = jax.random.uniform(jax.random.fold_in(jax.random.fold_in(key, 6), axis_at), (parts,), jnp.float32, least / len(cuts), top_value / len(cuts))
        return jnp.repeat(jnp.exp(steps), shape[axis_at] // parts).reshape((-1,) + (1,) * (len(shape) - axis_at - 1))

    loudness = one(*cuts[0])
    for cut in cuts[1:]:
        loudness = loudness * one(*cut)
    return loudness


def bell_draw(own_key, shape, spread, reach, pieces=(), kind=jnp.bfloat16):
    array = spread * jax.random.normal(own_key, shape, jnp.float32)
    if pieces:
        array = array * steps_of(own_key, shape, pieces, -0.22, 0.18)
    return jnp.clip(array, -reach, reach).astype(kind)


def noise_with(rng, extent, width, most, cuts, heavy, kind=jnp.bfloat16):
    drawn = width * jax.random.normal(rng, extent, jnp.float32)
    if cuts:
        drawn = drawn * steps_of(rng, extent, cuts, -0.22, 0.18)
    return jnp.clip(raised(drawn, jax.random.fold_in(rng, 3), *heavy), -most, most).astype(kind)


def setup_inputs(seed: int = 0) -> dict:
    streams_of = jax.random.split(jax.random.key(seed), 12)
    return {
        "tokens": noise_with(streams_of[0], (TOKENS, D), 1.0, 6.0, ((0, 32),), (0, 1, 32, 2.75)),
        "gain_attn": jnp.clip(1.0 + 0.15 * jax.random.normal(streams_of[1], (D,), jnp.float32), 0.25, 1.75).astype(jnp.bfloat16),
        "w_qkv": bell_draw(streams_of[2], (D, 3 * D), D ** -0.5, 0.21875, ((0, 32),)),
        "w_proj": bell_draw(streams_of[3], (D, D), (D // 128) ** -0.5, 2.5, ((0, 32),)),
        "gain_moe": jnp.clip(1.0 + 0.15 * jax.random.normal(streams_of[4], (D,), jnp.float32), 0.25, 1.75).astype(jnp.bfloat16),
        "w_router": bell_draw(streams_of[5], (D, EXPERTS), (2 * D) ** -0.5, 0.15625, ((0, 32),)),
        "w_in": bell_draw(streams_of[6], (EXPERTS, D, F), D ** -0.5, 0.21875, ((0, 2), (1, 16))),
        "w_out": bell_draw(streams_of[7], (EXPERTS, F, D), (F // 64) ** -0.5, 0.875, ((0, 2), (1, 16))),
        "routes": draw_routes(jax.random.fold_in(streams_of[11], 71), 0),
        "slot_ids": draw_slot_ids(jax.random.fold_in(streams_of[11], 71), 0),
        "cotangent": bell_draw(streams_of[10], (TOKENS, D), 1.0, 6.0, ((0, 32),)),
    }


highest = lax.Precision.HIGHEST
norm_epsilon = 1e-06

@jax.custom_vjp
def low(v):
    return lax.optimization_barrier(v.astype(jnp.bfloat16)).astype(jnp.float32)

@jax.custom_vjp
def low_back(v):
    return v

def low_keep(v):
    return (low(v), None)

def low_pass(kept, grad):
    return (grad,)

def back_keep(v):
    return (v, None)

def back_low(kept, grad):
    return (low(grad),)
low.defvjp(low_keep, low_pass)
low_back.defvjp(back_keep, back_low)

def layer_norm(values, gain):
    centre = values - lax.optimization_barrier(jnp.mean(values, axis=-1, keepdims=True))
    return centre * lax.rsqrt(lax.optimization_barrier(jnp.mean(centre * centre, axis=-1, keepdims=True)) + norm_epsilon) * gain

def block_forward(residual, gain_attn, w_qkv, w_proj, gain_moe, w_router, w_in, w_out, routes, slot_ids):
    images = residual.shape[0] // SEQ
    act_one = low(layer_norm(residual, gain_attn))
    qkv = low_back(low(jnp.dot(act_one, w_qkv, precision=highest)))
    split_qkv = qkv.reshape(images, SEQ, 3, HEADS, HEAD_DIM)
    scores = low_back(jnp.einsum('ishd,ithd->ihst', split_qkv[:, :, 0], split_qkv[:, :, 1], precision=highest) * HEAD_DIM ** (-0.5))
    attn_probs = low(jax.nn.softmax(scores, axis=-1))
    attended = low_back(low(jnp.einsum('ihst,ithd->ishd', attn_probs, split_qkv[:, :, 2], precision=highest)))
    attended = attended.reshape(residual.shape[0], -1)
    resid_mid = residual + low_back(jnp.dot(attended, w_proj, precision=highest))
    act_two = low(layer_norm(resid_mid, gain_moe))
    router = jax.nn.softmax(low_back(jnp.dot(act_two, w_router, precision=highest)), axis=-1)
    gate_values = low(jnp.take_along_axis(router, routes, axis=1))
    slot_count = EXPERTS * CAP
    columns = jnp.arange(slot_count, dtype=jnp.int32)
    targets = (routes * CAP + slot_ids).astype(jnp.int32)
    live_pair = slot_ids < CAP
    matches = jnp.where((targets[:, :, None] == columns[None, None, :]) & live_pair[:, :, None], 1.0, 0.0).astype(jnp.float32)
    dispatch = lax.optimization_barrier(jnp.sum(matches, axis=1))
    combine = jnp.einsum('tk,tkx->tx', gate_values, matches, precision=highest)
    slot_rows = low_back(low(jnp.einsum('tx,td->xd', dispatch, act_two, precision=highest))).reshape(EXPERTS, CAP, -1)
    pre_act = low_back(jnp.einsum('ecd,edf->ecf', slot_rows, w_in, precision=highest))
    hidden = low(jax.nn.gelu(pre_act, approximate=True))
    slot_result = low_back(low(jnp.einsum('ecf,efd->ecd', hidden, w_out, precision=highest)))
    return resid_mid + jnp.dot(combine, slot_result.reshape(slot_count, -1), precision=highest)

def reference(tokens, gain_attn, w_qkv, w_proj, gain_moe, w_router, w_in, w_out, routes, slot_ids, cotangent):
    weights = tuple((array_in.astype(jnp.float32) for array_in in (gain_attn, w_qkv, w_proj, gain_moe, w_router, w_in, w_out)))
    blocks = tokens.shape[0] // TOK_DEV
    resid_blocks = tokens.astype(jnp.float32).reshape(blocks, TOK_DEV, D)
    route_blocks = routes.reshape(blocks, TOK_DEV, 2)
    slot_blocks = slot_ids.reshape(blocks, TOK_DEV, 2)
    grad_blocks = cotangent.astype(jnp.float32).reshape(blocks, TOK_DEV, D)

    def one_block(totals, operands):
        residual, route_rows, slot_rows_in, grad_rows = operands

        def forward(resid_in, g_one, w_a, w_b, g_two, w_c, w_d, w_e):
            return block_forward(resid_in, g_one, w_a, w_b, g_two, w_c, w_d, w_e, route_rows, slot_rows_in)
        result, pull_back = jax.vjp(forward, residual, weights[0], weights[1], weights[2], weights[3], weights[4], weights[5], weights[6])
        gradients = pull_back(grad_rows)
        new_totals = tuple((total + grad for total, grad in zip(totals, gradients[1:])))
        return (new_totals, (result.astype(jnp.bfloat16), gradients[0]))
    zeros = tuple((jnp.zeros_like(array_in) for array_in in weights))
    totals, (outputs, grad_tokens) = lax.scan(one_block, zeros, (resid_blocks, route_blocks, slot_blocks, grad_blocks))
    return (outputs.reshape(-1, D), grad_tokens.reshape(-1, D), totals[0], totals[1], totals[2], totals[3], totals[4], totals[5], totals[6])
```

```python
import jax
import jax.numpy as jnp
from jax import lax
from jax.sharding import Mesh, PartitionSpec as P

HEADS = 12
HEAD_DIM = 64
EXPERTS = 8
SEQ = 576
CAP = 152
NORM_EPSILON = 1e-06
SCALE = HEAD_DIM ** (-0.5)
F32 = jnp.float32
BF16 = jnp.bfloat16


def norm_parts(values):
    centre = values - jnp.mean(values, axis=-1, keepdims=True)
    inverse = lax.rsqrt(jnp.mean(centre * centre, axis=-1, keepdims=True) + NORM_EPSILON)
    return centre * inverse, inverse


def norm_back(grad_normed, normed, inverse):
    mean_grad = jnp.mean(grad_normed, axis=-1, keepdims=True)
    mean_cross = jnp.mean(grad_normed * normed, axis=-1, keepdims=True)
    return (grad_normed - mean_grad - normed * mean_cross) * inverse


def gelu_tanh(values):
    return jax.nn.gelu(values, approximate=True)


def head_forward(operands):
    queries, keys_head, values_head = operands
    scores = jnp.einsum("isd,itd->ist", queries, keys_head, preferred_element_type=F32) * SCALE
    largest = jnp.max(scores, axis=-1, keepdims=True)
    powers = jnp.exp(scores - largest)
    totals = jnp.sum(powers, axis=-1, keepdims=True)
    attn_probs = (powers / totals).astype(BF16)
    head_out = jnp.einsum("ist,itd->isd", attn_probs, values_head, preferred_element_type=F32)
    return head_out.astype(BF16), (largest + jnp.log(totals))[..., 0]


def head_backward(operands):
    queries, keys_head, values_head, grad_head, log_total = operands
    scores = jnp.einsum("isd,itd->ist", queries, keys_head, preferred_element_type=F32) * SCALE
    attn_probs = jnp.exp(scores - log_total[..., None])
    grad_probs = jnp.einsum("isd,itd->ist", grad_head, values_head, preferred_element_type=F32)
    row_terms = jnp.sum(attn_probs * grad_probs, axis=-1, keepdims=True)
    grad_scores = (attn_probs * (grad_probs - row_terms)).astype(BF16)
    grad_query = jnp.einsum("ist,itd->isd", grad_scores, keys_head, preferred_element_type=F32) * SCALE
    grad_key = jnp.einsum("ist,isd->itd", grad_scores, queries, preferred_element_type=F32) * SCALE
    grad_value = jnp.einsum(
        "ist,isd->itd", attn_probs.astype(BF16), grad_head, preferred_element_type=F32
    )
    return grad_query, grad_key, grad_value


def attention_forward(qkv):
    rows = qkv.shape[0]
    split_qkv = qkv.reshape(rows // SEQ, SEQ, 3, HEADS, HEAD_DIM).transpose(2, 3, 0, 1, 4)
    head_out, head_lse = lax.map(head_forward, (split_qkv[0], split_qkv[1], split_qkv[2]))
    return head_out.transpose(1, 2, 0, 3).reshape(rows, -1), (split_qkv, head_lse)


def attention_backward(saved, grad_attended):
    split_qkv, head_lse = saved
    rows = grad_attended.shape[0]
    grad_heads = grad_attended.reshape(rows // SEQ, SEQ, HEADS, HEAD_DIM).transpose(2, 0, 1, 3)
    parts = lax.map(
        head_backward, (split_qkv[0], split_qkv[1], split_qkv[2], grad_heads, head_lse)
    )
    return jnp.stack(parts).transpose(2, 3, 0, 1, 4).reshape(rows, -1).astype(BF16)


class PairwiseLinks:
    def __init__(self, mesh):
        self.mesh = Mesh(mesh.devices.reshape(2, 2, 2, 2, 2), ("x", "zh", "zl", "y", "c"))
        self.data = ("x", "zh", "zl", "y", "c")
        self.fsdp = ("zh", "zl", "y", "c")
        self.dp = "x"
        self.hosts = ("x", "zl", "y")

    def swap(self, value, axis):
        return lax.ppermute(value, axis, [(0, 1), (1, 0)])

    def join(self, value, axis, at):
        other = self.swap(value, axis)
        first = lax.axis_index(axis) == 0
        return jnp.stack([jnp.where(first, value, other), jnp.where(first, other, value)], axis=at)

    def add_halves(self, value, axis, at):
        me = lax.axis_index(axis)
        mine = lax.dynamic_index_in_dim(value, me, at, keepdims=False)
        theirs = lax.dynamic_index_in_dim(value, 1 - me, at, keepdims=False)
        got = self.swap(theirs, axis)
        return (mine.astype(F32) + got.astype(F32)).astype(value.dtype)

    def gather_rows(self, shard):
        rows, columns = shard.shape
        copies = jnp.broadcast_to(shard[None], (4, rows, columns))
        over_z = lax.all_to_all(copies, ("zh", "zl"), 0, 0, tiled=True)
        over_y = self.join(over_z, "y", 1)
        over_x = self.join(over_y, "x", 0)
        whole = self.join(over_x, "c", 3)
        return whole.reshape(32 * rows, columns)

    def scatter_rows(self, value):
        rows, columns = value.shape
        part = value.reshape(2, 4, 2, 2, rows // 32, columns)
        part = self.add_halves(part, "c", 3)
        part = self.add_halves(part, "x", 0)
        part = self.add_halves(part, "y", 1)
        got = lax.all_to_all(part, ("zh", "zl"), 0, 0, tiled=True)
        return jnp.sum(got.astype(F32), axis=0)

    def send_slots(self, slots):
        return lax.all_to_all(slots, self.hosts, 0, 0, tiled=True)

    def return_slots(self, slots):
        return lax.all_to_all(slots, self.hosts, 0, 0, tiled=True)

    def gather_expert(self, shard):
        mine = lax.all_to_all(shard, ("zl", "y"), 0, 0, tiled=True)
        halves = self.join(mine, "zh", 0)
        whole = self.join(halves, "c", 2)
        return whole.reshape(1, -1, shard.shape[-1])

    def scatter_expert(self, grad):
        _, rows, columns = grad.shape
        part = grad.astype(BF16).reshape(2, 4, 2, rows // 16, columns)
        part = self.add_halves(part, "c", 2)
        part = self.add_halves(part, "zh", 0)
        return lax.all_to_all(part, ("zl", "y"), 0, 0, tiled=True).astype(F32)


class AxisLinks:
    def __init__(self, mesh):
        self.mesh = mesh
        self.data = ("dp", "fsdp")
        self.fsdp = "fsdp"
        self.dp = "dp"

    def gather_rows(self, shard):
        return lax.all_gather(shard, self.data, axis=0, tiled=True)

    def scatter_rows(self, value):
        return lax.psum_scatter(value.astype(F32), self.data, scatter_dimension=0, tiled=True)

    def send_slots(self, slots):
        return lax.all_to_all(slots, "dp", 0, 1, tiled=True)

    def return_slots(self, slots):
        return lax.all_to_all(slots, "dp", 1, 0, tiled=True)

    def gather_expert(self, shard):
        return lax.all_gather(shard, "fsdp", axis=1, tiled=True)

    def scatter_expert(self, grad):
        return lax.psum_scatter(
            grad.astype(BF16), "fsdp", scatter_dimension=1, tiled=True
        ).astype(F32)


def per_device(
    links, tokens, gain_attn, w_qkv, w_proj, gain_moe, w_router, w_in, w_out, routes, slot_ids, cotangent
):
    width = tokens.shape[1]
    small = jnp.concatenate(
        [w_router, gain_attn[:, None], gain_moe[:, None]], axis=1
    )
    small = jnp.pad(small, ((0, 0), (0, 128 - small.shape[1])))
    dense = links.gather_rows(jnp.concatenate([w_qkv, w_proj, small], axis=1))
    full_qkv = dense[:, : 3 * width]
    full_proj = dense[:, 3 * width : 4 * width]
    full_router = dense[:, 4 * width : 4 * width + EXPERTS]
    gain_one = dense[:, 4 * width + EXPERTS].astype(F32)
    gain_two = dense[:, 4 * width + EXPERTS + 1].astype(F32)
    expert_in = links.gather_expert(w_in)
    expert_out = links.gather_expert(w_out)

    residual = tokens.astype(F32)
    normed_one, inverse_one = norm_parts(residual)
    act_one = (normed_one * gain_one).astype(BF16)
    qkv = jnp.dot(act_one, full_qkv, preferred_element_type=F32).astype(BF16)
    attended, saved = attention_forward(qkv)
    resid_mid = residual + jnp.dot(attended, full_proj, preferred_element_type=F32)
    normed_two, inverse_two = norm_parts(resid_mid)
    act_two = (normed_two * gain_two).astype(BF16)
    logits = jnp.dot(act_two, full_router, preferred_element_type=F32)
    router = jax.nn.softmax(logits, axis=-1)
    expert_ids = lax.broadcasted_iota(jnp.int32, (1, 1, EXPERTS), 2)
    chosen = routes[:, :, None] == expert_ids
    gates_low = jnp.sum(jnp.where(chosen, router[:, None, :], 0.0), axis=-1).astype(BF16)
    slot_count = EXPERTS * CAP
    columns = lax.broadcasted_iota(jnp.int32, (1, slot_count), 1)
    live_pair = slot_ids < CAP
    targets = jnp.where(live_pair, routes * CAP + slot_ids, -1)
    match_a = targets[:, 0:1] == columns
    match_b = targets[:, 1:2] == columns
    dispatch = (match_a | match_b).astype(BF16)
    zero = jnp.zeros((), BF16)
    combine = jnp.where(match_a, gates_low[:, 0:1], jnp.where(match_b, gates_low[:, 1:2], zero))

    def to_slots(weights, values):
        rows = jnp.einsum("tx,td->xd", weights, values, preferred_element_type=F32)
        return rows.astype(BF16).reshape(EXPERTS, CAP, -1)

    slot_rows = links.send_slots(to_slots(dispatch, act_two))
    grad_slots = links.send_slots(to_slots(combine, cotangent))
    held = slot_rows.shape
    hosted = expert_in.shape[0]
    expert_rows = slot_rows.reshape(hosted, -1, width)
    grad_result = grad_slots.reshape(hosted, -1, width)

    pre_act = jnp.einsum("ecd,edf->ecf", expert_rows, expert_in, preferred_element_type=F32)
    hidden = gelu_tanh(pre_act).astype(BF16)
    result = jnp.einsum("ecf,efd->ecd", hidden, expert_out, preferred_element_type=F32)
    flat_result = links.return_slots(result.astype(BF16).reshape(held)).reshape(slot_count, -1)

    grad_down = jnp.einsum("ecf,ecd->efd", hidden, grad_result, preferred_element_type=F32)
    d_out = links.scatter_expert(grad_down)
    grad_hidden = jnp.einsum("ecd,efd->ecf", grad_result, expert_out, preferred_element_type=F32)
    grad_pre = jax.vjp(gelu_tanh, pre_act)[1](grad_hidden)[0].astype(BF16)
    grad_rows = jnp.einsum("ecf,edf->ecd", grad_pre, expert_in, preferred_element_type=F32)
    grad_rows = links.return_slots(grad_rows.astype(BF16).reshape(held)).reshape(slot_count, -1)
    grad_up = jnp.einsum("ecd,ecf->edf", expert_rows, grad_pre, preferred_element_type=F32)
    d_in = links.scatter_expert(grad_up)

    moe_sum = jnp.einsum("tx,xd->td", combine, flat_result, preferred_element_type=F32)
    output = (resid_mid + moe_sum).astype(BF16)
    crossed = jnp.einsum("td,xd->tx", cotangent, flat_result, preferred_element_type=F32)
    grad_gates = jnp.stack(
        [
            jnp.sum(jnp.where(match_a, crossed, 0.0), axis=1),
            jnp.sum(jnp.where(match_b, crossed, 0.0), axis=1),
        ],
        axis=1,
    )
    grad_router = jnp.sum(jnp.where(chosen, grad_gates[:, :, None], 0.0), axis=1)
    grad_logits = (
        router * (grad_router - jnp.sum(router * grad_router, axis=-1, keepdims=True))
    ).astype(BF16)
    d_router = jnp.einsum("td,te->de", act_two, grad_logits, preferred_element_type=F32)
    grad_act_two = jnp.einsum("te,de->td", grad_logits, full_router, preferred_element_type=F32)
    grad_act_two = grad_act_two + jnp.einsum(
        "tx,xd->td", dispatch, grad_rows, preferred_element_type=F32
    )
    d_gain_moe = jnp.sum(grad_act_two * normed_two, axis=0)
    grad_mid = cotangent.astype(F32) + norm_back(grad_act_two * gain_two, normed_two, inverse_two)
    grad_mid_low = grad_mid.astype(BF16)
    d_proj = jnp.einsum("td,te->de", attended, grad_mid_low, preferred_element_type=F32)
    grad_attended = jnp.einsum(
        "te,de->td", grad_mid_low, full_proj, preferred_element_type=F32
    ).astype(BF16)
    grad_qkv = attention_backward(saved, grad_attended)
    d_qkv = jnp.einsum("td,te->de", act_one, grad_qkv, preferred_element_type=F32)
    grad_act_one = jnp.einsum("te,de->td", grad_qkv, full_qkv, preferred_element_type=F32)
    d_gain_attn = jnp.sum(grad_act_one * normed_one, axis=0)
    grad_tokens = grad_mid + norm_back(grad_act_one * gain_one, normed_one, inverse_one)
    small_grads = jnp.concatenate([d_router, d_gain_attn[:, None], d_gain_moe[:, None]], axis=1)
    small_grads = jnp.pad(small_grads, ((0, 0), (0, 128 - small_grads.shape[1])))
    dense_grads = links.scatter_rows(
        jnp.concatenate([d_qkv, d_proj, small_grads], axis=1).astype(BF16)
    )
    return (
        output,
        grad_tokens,
        dense_grads[:, 4 * width + EXPERTS],
        dense_grads[:, : 3 * width],
        dense_grads[:, 3 * width : 4 * width],
        dense_grads[:, 4 * width + EXPERTS + 1],
        dense_grads[:, 4 * width : 4 * width + EXPERTS],
        d_in,
        d_out,
    )


def solution(mesh):
    pairwise = mesh.shape["dp"] == 2 and mesh.shape["fsdp"] == 16
    links = PairwiseLinks(mesh) if pairwise else AxisLinks(mesh)
    rows = P(links.data, None)
    flat = P(links.data)
    expert = P(links.dp, links.fsdp, None)
    return jax.shard_map(
        lambda *arrays: per_device(links, *arrays),
        mesh=links.mesh,
        in_specs=(rows, flat, rows, rows, flat, rows, expert, expert, rows, rows, rows),
        out_specs=(rows, rows, flat, rows, rows, flat, rows, expert, expert),
        check_vma=False,
    )
```

```python
import math

import jax
import jax.numpy as jnp
from jax import lax
from jax.experimental import pallas as pl
from jax.experimental.pallas import tpu as pltpu
from jax.sharding import Mesh, PartitionSpec as P

HEADS = 12
HEAD_DIM = 64
EXPERTS = 8
SEQ = 576
CAP = 152
SLOTS = EXPERTS * CAP
NORM_EPSILON = 1e-06
SCALE = HEAD_DIM ** (-0.5)
PAIR = 2 * HEAD_DIM
PAIRS = HEADS // 2
WIDTH = HEADS * HEAD_DIM
LANES = 128
GAIN_ONE = EXPERTS
GAIN_TWO = EXPERTS + 1
TOKEN_BLOCK = 192
ROW_BLOCK = 304
F_BLOCK = 512
F32 = jnp.float32
BF16 = jnp.bfloat16
QUICK = pl.CostEstimate(flops=1, bytes_accessed=1, transcendentals=0)


def dot_nn(left, right):
    return jnp.dot(left, right, preferred_element_type=F32)


def dot_nt(left, right):
    return lax.dot_general(left, right, (((1,), (1,)), ((), ())), preferred_element_type=F32)


def dot_tn(left, right):
    return lax.dot_general(left, right, (((0,), (0,)), ((), ())), preferred_element_type=F32)


def scaled(values):
    return values * jnp.asarray(SCALE, BF16)


def norm_parts(values):
    centre = values - jnp.mean(values, axis=-1, keepdims=True)
    inverse = lax.rsqrt(jnp.mean(centre * centre, axis=-1, keepdims=True) + NORM_EPSILON)
    return centre * inverse, inverse


def norm_back(grad_normed, normed, inverse):
    mean_grad = jnp.mean(grad_normed, axis=-1, keepdims=True)
    mean_cross = jnp.mean(grad_normed * normed, axis=-1, keepdims=True)
    return (grad_normed - mean_grad - normed * mean_cross) * inverse


def whole(*shape):
    return pl.BlockSpec(shape, lambda *at: (0,) * len(shape))


def call(name, kernel, grid, in_specs, out_specs, out_shape, scratch=(), scalars=0):
    return pl.pallas_call(
        kernel,
        grid_spec=pltpu.PrefetchScalarGridSpec(
            num_scalar_prefetch=scalars,
            grid=grid,
            in_specs=in_specs,
            out_specs=out_specs,
            scratch_shapes=scratch,
        ),
        out_shape=out_shape,
        cost_estimate=QUICK,
        name=name,
    )


def struct(shape, dtype):
    return jax.ShapeDtypeStruct(shape, dtype)


def attention_kernel(qkv_ref, out_ref, log_ref):
    values_t = qkv_ref[:, 2 * PAIR :].T
    outs = []
    for head in range(2):
        at = head * HEAD_DIM
        queries = scaled(qkv_ref[:, at : at + HEAD_DIM])
        keys = qkv_ref[:, PAIR + at : PAIR + at + HEAD_DIM]
        scores = dot_nt(keys, queries)
        largest = jnp.max(scores, axis=0, keepdims=True)
        powers = jnp.exp(scores - largest)
        totals = jnp.sum(powers, axis=0, keepdims=True)
        mixed = dot_nn(values_t[at : at + HEAD_DIM], powers.astype(BF16))
        outs.append((mixed / totals).astype(BF16))
        log_ref[0, 0, head : head + 1, :] = largest + jnp.log(totals)
    out_ref[...] = jnp.concatenate(outs, axis=0).T


def attention_back_kernel(qkv_ref, out_ref, log_ref, grad_ref, result_ref):
    products = out_ref[...].T.astype(F32) * grad_ref[...].T.astype(F32)
    keys_t = scaled(qkv_ref[:, PAIR : 2 * PAIR]).T
    grad_queries = []
    for head in range(2):
        at = head * HEAD_DIM
        span = slice(at, at + HEAD_DIM)
        queries = scaled(qkv_ref[:, span])
        keys = qkv_ref[:, PAIR + at : PAIR + at + HEAD_DIM]
        values = qkv_ref[:, 2 * PAIR + at : 2 * PAIR + at + HEAD_DIM]
        grads = grad_ref[:, span]
        row_terms = jnp.sum(products[span], axis=0, keepdims=True)
        probs = jnp.exp(dot_nt(keys, queries) - log_ref[0, 0, head : head + 1, :])
        grad_scores = (probs * (dot_nt(values, grads) - row_terms)).astype(BF16)
        grad_values = dot_nn(probs.astype(BF16), grads)
        grad_keys = dot_nn(grad_scores, queries)
        result_ref[:, 2 * PAIR + at : 2 * PAIR + at + HEAD_DIM] = grad_values.astype(BF16)
        result_ref[:, PAIR + at : PAIR + at + HEAD_DIM] = grad_keys.astype(BF16)
        grad_queries.append(dot_nn(keys_t[span], grad_scores).astype(BF16))
    result_ref[:, :PAIR] = jnp.concatenate(grad_queries, axis=0).T


def attention_specs():
    return (
        pl.BlockSpec((SEQ, 3 * PAIR), lambda image, pair: (image, pair)),
        pl.BlockSpec((SEQ, PAIR), lambda image, pair: (image, pair)),
        pl.BlockSpec((1, 1, 2, SEQ), lambda image, pair: (image, pair, 0, 0)),
    )


def attention_forward(qkv):
    rows = qkv.shape[0]
    images = rows // SEQ
    wide, narrow, logs = attention_specs()
    return call(
        "attention_forward",
        attention_kernel,
        (images, PAIRS),
        [wide],
        [narrow, logs],
        [struct((rows, WIDTH), BF16), struct((images, PAIRS, 2, SEQ), F32)],
    )(qkv)


def attention_backward(qkv, attended, logs_saved, grad_attended):
    wide, narrow, logs = attention_specs()
    return call(
        "attention_backward",
        attention_back_kernel,
        (qkv.shape[0] // SEQ, PAIRS),
        [wide, narrow, logs, narrow],
        wide,
        struct(qkv.shape, BF16),
    )(qkv, attended, logs_saved, grad_attended)


QKV_SPEC = pl.BlockSpec((WIDTH, 3 * WIDTH), lambda *at: (0, 0))
PROJ_SPEC = pl.BlockSpec((WIDTH, WIDTH), lambda *at: (0, 3))
SMALL_SPEC = pl.BlockSpec((WIDTH, LANES), lambda *at: (0, 4 * WIDTH // LANES))


def project_kernel(tokens_ref, weight_ref, small_ref, qkv_ref, act_ref, table_ref):
    @pl.when(pl.program_id(0) == 0)
    def _():
        table = small_ref[...].T
        table_ref[...] = table
        gain = table[GAIN_ONE : GAIN_ONE + 1].astype(F32)
        normed, _ = norm_parts(tokens_ref[...].astype(F32))
        act_ref[...] = (normed * gain).astype(BF16)

    qkv_ref[...] = dot_nn(act_ref[...], weight_ref[...]).astype(BF16)


def project(tokens, dense):
    rows = tokens.shape[0]
    return call(
        "project",
        project_kernel,
        (PAIRS,),
        [
            whole(rows, WIDTH),
            pl.BlockSpec((WIDTH, 3 * PAIR), lambda pair: (0, pair)),
            SMALL_SPEC,
        ],
        [
            pl.BlockSpec((rows, 3 * PAIR), lambda pair: (0, pair)),
            whole(rows, WIDTH),
            whole(LANES, WIDTH),
        ],
        [
            struct((rows, 3 * WIDTH), BF16),
            struct((rows, WIDTH), BF16),
            struct((LANES, WIDTH), BF16),
        ],
    )(tokens, dense, dense)


def slot_hits(routes_ref, slots_ref):
    rows = routes_ref.shape[1]
    places = lax.broadcasted_iota(jnp.int32, (CAP, rows), 0)
    expert = pl.program_id(0)
    return [
        (routes_ref[k : k + 1, :] == expert) & (slots_ref[k : k + 1, :] == places)
        for k in range(2)
    ]


def middle_kernel(
    routes_ref, slots_ref, tokens_ref, attended_ref, proj_ref, table_ref,
    mid_ref, act_ref, columns_ref, gates_ref, slot_rows_ref,
):
    @pl.when(pl.program_id(0) == 0)
    def _():
        mid = tokens_ref[...].astype(F32) + dot_nn(attended_ref[...], proj_ref[...])
        mid_ref[...] = mid
        normed, _ = norm_parts(mid)
        gain = table_ref[GAIN_TWO : GAIN_TWO + 1, :].astype(F32)
        act = (normed * gain).astype(BF16)
        act_ref[...] = act
        logits = dot_nt(table_ref[:16, :], act)[:EXPERTS]
        powers = jnp.exp(logits - jnp.max(logits, axis=0, keepdims=True))
        router = powers / jnp.sum(powers, axis=0, keepdims=True)
        names = lax.broadcasted_iota(jnp.int32, router.shape, 0)
        gates = [
            jnp.sum(jnp.where(names == routes_ref[k : k + 1, :], router, 0.0), axis=0, keepdims=True)
            .astype(BF16)
            .astype(F32)
            for k in range(2)
        ]
        rows = router.shape[1]
        gates = jnp.concatenate(gates + [jnp.zeros((EXPERTS - 2, rows), F32)], axis=0)
        gates_ref[...] = gates
        spare = jnp.zeros((LANES - 2 * EXPERTS, rows), F32)
        columns_ref[...] = jnp.concatenate([router, gates, spare], axis=0).T

    first, second = slot_hits(routes_ref, slots_ref)
    dispatch = jnp.where(first | second, 1.0, 0.0).astype(BF16)
    slot_rows_ref[0] = dot_nn(dispatch, act_ref[...]).astype(BF16)


def middle(routes_t, slots_t, tokens, attended, dense, table):
    rows = tokens.shape[0]
    return call(
        "middle",
        middle_kernel,
        (EXPERTS,),
        [
            whole(2, rows),
            whole(2, rows),
            whole(rows, WIDTH),
            whole(rows, WIDTH),
            PROJ_SPEC,
            whole(LANES, WIDTH),
        ],
        [
            whole(rows, WIDTH),
            whole(rows, WIDTH),
            whole(rows, LANES),
            whole(EXPERTS, rows),
            pl.BlockSpec((1, CAP, WIDTH), lambda expert: (expert, 0, 0)),
        ],
        [
            struct((rows, WIDTH), F32),
            struct((rows, WIDTH), BF16),
            struct((rows, LANES), F32),
            struct((EXPERTS, rows), F32),
            struct((EXPERTS, CAP, WIDTH), BF16),
        ],
    )(routes_t, slots_t, tokens, attended, dense, table)


def slot_grads_kernel(routes_ref, slots_ref, gates_ref, grad_ref, result_ref):
    first, second = slot_hits(routes_ref, slots_ref)
    combine = jnp.where(first, gates_ref[0:1, :], jnp.where(second, gates_ref[1:2, :], 0.0))
    result_ref[0] = dot_nn(combine.astype(BF16), grad_ref[...]).astype(BF16)


def slot_grads(routes_t, slots_t, gates, cotangent):
    rows = cotangent.shape[0]
    return call(
        "slot_grads",
        slot_grads_kernel,
        (EXPERTS,),
        [whole(2, rows), whole(2, rows), whole(EXPERTS, rows), whole(rows, WIDTH)],
        pl.BlockSpec((1, CAP, WIDTH), lambda expert: (expert, 0, 0)),
        struct((EXPERTS, CAP, WIDTH), BF16),
    )(routes_t, slots_t, gates, cotangent)


def expert_up_kernel(rows_ref, weight_ref, hidden_ref, slope_ref):
    root = math.sqrt(2.0 / math.pi)
    value = dot_nn(rows_ref[...], weight_ref[...])
    square = value * value
    curve = jnp.tanh(value * (root + (root * 0.044715) * square))
    upper = 0.5 + 0.5 * curve
    hidden_ref[...] = (value * upper).astype(BF16)
    inner = value * (root + (3.0 * root * 0.044715) * square)
    slope_ref[...] = (upper + (0.5 - 0.5 * curve * curve) * inner).astype(BF16)


def expert_up(rows, weight):
    count, depth = rows.shape[0], weight.shape[1]
    wide = pl.BlockSpec((count, F_BLOCK), lambda f: (0, f))
    return call(
        "expert_up",
        expert_up_kernel,
        (depth // F_BLOCK,),
        [whole(count, WIDTH), pl.BlockSpec((WIDTH, F_BLOCK), lambda f: (0, f))],
        [wide, wide],
        [struct((count, depth), BF16)] * 2,
    )(rows, weight)


def expert_down_kernel(hidden_ref, weight_ref, result_ref):
    result_ref[...] = dot_nn(hidden_ref[...], weight_ref[...]).astype(BF16)


def expert_down(hidden, weight):
    count, depth = hidden.shape
    return call(
        "expert_down",
        expert_down_kernel,
        (count // ROW_BLOCK,),
        [pl.BlockSpec((ROW_BLOCK, depth), lambda r: (r, 0)), whole(depth, WIDTH)],
        pl.BlockSpec((ROW_BLOCK, WIDTH), lambda r: (r, 0)),
        struct((count, WIDTH), BF16),
    )(hidden, weight)


def expert_back_kernel(grad_ref, slope_ref, out_ref, in_ref, grad_pre_ref, grad_rows_ref):
    grad_hidden = dot_nt(grad_ref[...], out_ref[...])
    grad_pre = (grad_hidden * slope_ref[...].astype(F32)).astype(BF16)
    grad_pre_ref[...] = grad_pre
    grad_rows_ref[...] = dot_nt(grad_pre, in_ref[...]).astype(BF16)


def expert_back(grad_result, slope, weight_out, weight_in):
    count, depth = slope.shape
    wide = pl.BlockSpec((ROW_BLOCK, depth), lambda r: (r, 0))
    narrow = pl.BlockSpec((ROW_BLOCK, WIDTH), lambda r: (r, 0))
    return call(
        "expert_back",
        expert_back_kernel,
        (count // ROW_BLOCK,),
        [narrow, wide, whole(depth, WIDTH), whole(WIDTH, depth)],
        [wide, narrow],
        [struct((count, depth), BF16), struct((count, WIDTH), BF16)],
    )(grad_result, slope, weight_out, weight_in)


def out_grad_kernel(me_ref, hidden_ref, grad_ref, mine_ref, theirs_ref):
    value = dot_tn(hidden_ref[...], grad_ref[...]).astype(BF16)
    half = value.shape[0] // 2
    first = me_ref[0] == 0
    mine_ref[0, 0] = jnp.where(first, value[:half], value[half:])
    theirs_ref[0, 0] = jnp.where(first, value[half:], value[:half])


def out_grad(me, hidden, grad_result):
    count, depth = hidden.shape
    rest = depth // 16
    half = pl.BlockSpec((1, 1, rest, WIDTH), lambda f, me: (f // 4, lax.rem(f, 4), 0, 0))
    return call(
        "out_grad",
        out_grad_kernel,
        (8,),
        [pl.BlockSpec((count, 2 * rest), lambda f, me: (0, f)), whole(count, WIDTH)],
        [half, half],
        [struct((2, 4, rest, WIDTH), BF16)] * 2,
        scalars=1,
    )(me, hidden, grad_result)


def in_grad_kernel(me_ref, rows_ref, grad_ref, mine_ref, theirs_ref, turned_ref):
    @pl.when(pl.program_id(0) == 0)
    def _():
        turned_ref[...] = rows_ref[...].T

    value = dot_nn(turned_ref[...], grad_ref[...]).astype(BF16)
    value = value.reshape(8, 2, WIDTH // 16, F_BLOCK)
    first = me_ref[0] == 0
    shape = mine_ref.shape
    mine_ref[...] = jnp.where(first, value[:, 0], value[:, 1]).reshape(shape)
    theirs_ref[...] = jnp.where(first, value[:, 1], value[:, 0]).reshape(shape)


def in_grad(me, rows, grad_pre):
    count, depth = grad_pre.shape
    rest = WIDTH // 16
    half = pl.BlockSpec((2, 4, rest, F_BLOCK), lambda f, me: (0, 0, 0, f))
    return call(
        "in_grad",
        in_grad_kernel,
        (depth // F_BLOCK,),
        [whole(count, WIDTH), pl.BlockSpec((count, F_BLOCK), lambda f, me: (0, f))],
        [half, half],
        [struct((2, 4, rest, depth), BF16)] * 2,
        scratch=[pltpu.VMEM((WIDTH, count), BF16)],
        scalars=1,
    )(me, rows, grad_pre)


def token_hits(targets_ref):
    columns = lax.broadcasted_iota(jnp.int32, (targets_ref.shape[0], SLOTS), 1)
    return [targets_ref[:, k : k + 1] == columns for k in range(2)]


def combine_kernel(
    routes_ref, targets_ref, columns_ref, mid_ref, grad_ref, result_ref, output_ref, logits_ref
):
    first, second = token_hits(targets_ref)
    gates = columns_ref[:, EXPERTS : EXPERTS + 2]
    combine = jnp.where(first, gates[:, 0:1], jnp.where(second, gates[:, 1:2], 0.0)).astype(BF16)
    output_ref[...] = (mid_ref[...] + dot_nn(combine, result_ref[...])).astype(BF16)
    crossed = dot_nt(grad_ref[...], result_ref[...])
    lanes = lax.broadcasted_iota(jnp.int32, columns_ref.shape, 1)
    grad_router = jnp.zeros(columns_ref.shape, F32)
    for k, hits in enumerate((first, second)):
        grad_gate = jnp.sum(jnp.where(hits, crossed, 0.0), axis=1, keepdims=True)
        grad_router += jnp.where(lanes == routes_ref[:, k : k + 1], grad_gate, 0.0)
    router = jnp.where(lanes < EXPERTS, columns_ref[...], 0.0)
    total = jnp.sum(router * grad_router, axis=1, keepdims=True)
    logits_ref[...] = (router * (grad_router - total)).astype(BF16)


def token_spec(columns):
    return pl.BlockSpec((TOKEN_BLOCK, columns), lambda t: (t, 0))


def combine_results(routes, targets, columns, mid, cotangent, result):
    rows = mid.shape[0]
    return call(
        "combine",
        combine_kernel,
        (rows // TOKEN_BLOCK,),
        [
            token_spec(2),
            token_spec(2),
            token_spec(LANES),
            token_spec(WIDTH),
            token_spec(WIDTH),
            whole(SLOTS, WIDTH),
        ],
        [token_spec(WIDTH), token_spec(LANES)],
        [struct((rows, WIDTH), BF16), struct((rows, LANES), BF16)],
    )(routes, targets, columns, mid, cotangent, result)


def middle_back_kernel(
    targets_ref, logits_ref, mid_ref, grad_ref, rows_ref, proj_ref, table_ref,
    grad_mid_ref, low_ref, attended_ref, gain_ref,
):
    first, second = token_hits(targets_ref)
    dispatch = jnp.where(first | second, 1.0, 0.0).astype(BF16)
    grad_act = dot_nn(dispatch, rows_ref[...]) + dot_nn(logits_ref[...], table_ref[...])
    normed, inverse = norm_parts(mid_ref[...])
    gain = table_ref[GAIN_TWO : GAIN_TWO + 1, :].astype(F32)
    part = jnp.sum(grad_act * normed, axis=0, keepdims=True)

    @pl.when(pl.program_id(0) == 0)
    def _():
        gain_ref[...] = jnp.zeros_like(gain_ref)

    gain_ref[0:1, :] += part
    grad_mid = grad_ref[...].astype(F32) + norm_back(grad_act * gain, normed, inverse)
    grad_mid_ref[...] = grad_mid
    low = grad_mid.astype(BF16)
    low_ref[...] = low
    attended_ref[...] = dot_nt(low, proj_ref[...]).astype(BF16)


def middle_back(targets, logits, mid, cotangent, grad_rows, dense, table):
    rows = mid.shape[0]
    return call(
        "middle_back",
        middle_back_kernel,
        (rows // TOKEN_BLOCK,),
        [
            token_spec(2),
            token_spec(LANES),
            token_spec(WIDTH),
            token_spec(WIDTH),
            whole(SLOTS, WIDTH),
            PROJ_SPEC,
            whole(LANES, WIDTH),
        ],
        [token_spec(WIDTH), token_spec(WIDTH), token_spec(WIDTH), whole(8, WIDTH)],
        [
            struct((rows, WIDTH), F32),
            struct((rows, WIDTH), BF16),
            struct((rows, WIDTH), BF16),
            struct((8, WIDTH), F32),
        ],
    )(targets, logits, mid, cotangent, grad_rows, dense, table)


def proj_grads_kernel(attended_ref, low_ref, act_ref, logits_ref, gain_ref, result_ref):
    result_ref[:, :WIDTH] = dot_tn(attended_ref[...], low_ref[...]).astype(BF16)
    small = dot_tn(act_ref[...], logits_ref[...])
    lanes = lax.broadcasted_iota(jnp.int32, small.shape, 1)
    gain = gain_ref[...].T[:, 0:1]
    result_ref[:, WIDTH:] = jnp.where(lanes == GAIN_TWO, gain, small).astype(BF16)


def proj_grads(attended, low, act_two, logits, gain):
    rows = low.shape[0]
    return call(
        "proj_grads",
        proj_grads_kernel,
        (1,),
        [whole(rows, WIDTH)] * 3 + [whole(rows, LANES), whole(8, WIDTH)],
        whole(WIDTH, WIDTH + LANES),
        struct((WIDTH, WIDTH + LANES), BF16),
    )(attended, low, act_two, logits, gain)


def qkv_grads_kernel(act_ref, grad_ref, result_ref, turned_ref):
    @pl.when(pl.program_id(0) == 0)
    def _():
        turned_ref[...] = act_ref[...].T

    result_ref[...] = dot_nn(turned_ref[...], grad_ref[...]).astype(BF16)


def qkv_grads(act_one, grad_qkv):
    rows = act_one.shape[0]
    return call(
        "qkv_grads",
        qkv_grads_kernel,
        (PAIRS,),
        [whole(rows, WIDTH), pl.BlockSpec((rows, 3 * PAIR), lambda pair: (0, pair))],
        pl.BlockSpec((WIDTH, 3 * PAIR), lambda pair: (0, pair)),
        struct((WIDTH, 3 * WIDTH), BF16),
        scratch=[pltpu.VMEM((WIDTH, rows), BF16)],
    )(act_one, grad_qkv)


def token_grads_kernel(grad_ref, weight_ref, tokens_ref, grad_mid_ref, table_ref, result_ref):
    grad_act = dot_nt(grad_ref[...], weight_ref[...])
    normed, inverse = norm_parts(tokens_ref[...].astype(F32))
    gain = table_ref[GAIN_ONE : GAIN_ONE + 1, :].astype(F32)
    result_ref[...] = grad_mid_ref[...] + norm_back(grad_act * gain, normed, inverse)


def token_grads(grad_qkv, dense, tokens, grad_mid, table):
    rows = tokens.shape[0]
    return call(
        "token_grads",
        token_grads_kernel,
        (rows // TOKEN_BLOCK,),
        [token_spec(3 * WIDTH), QKV_SPEC, token_spec(WIDTH), token_spec(WIDTH), whole(LANES, WIDTH)],
        token_spec(WIDTH),
        struct((rows, WIDTH), F32),
    )(grad_qkv, dense, tokens, grad_mid, table)


def by_pair(columns):
    rows = columns.shape[0]
    return columns.reshape(rows, 3, PAIRS, PAIR).transpose(0, 2, 1, 3).reshape(rows, -1)


def by_part(columns):
    rows = columns.shape[0]
    return columns.reshape(rows, PAIRS, 3, PAIR).transpose(0, 2, 1, 3).reshape(rows, -1)


def place_kernel(count, me_ref, *refs):
    pieces, result_ref = refs[:-1], refs[-1]
    at = 0
    for axis in range(count):
        at = 2 * at + lax.rem(pl.program_id(axis) + me_ref[axis], 2)
    for index, piece in enumerate(pieces):

        @pl.when(at == index)
        def _():
            result_ref[...] = piece[...].reshape(result_ref.shape)


def place(me, pieces, axes):
    count = len(axes)
    shape = list(pieces[0].shape)
    for axis in axes:
        shape.insert(axis, 2)
    block = [1 if axis in axes else size for axis, size in enumerate(shape)]

    def index(*at):
        return tuple(at[axes.index(a)] if a in axes else 0 for a in range(len(shape)))

    return call(
        "place",
        lambda *refs: place_kernel(count, *refs),
        (2,) * count,
        [whole(*piece.shape) for piece in pieces],
        pl.BlockSpec(tuple(block), index),
        struct(tuple(shape), pieces[0].dtype),
        scalars=1,
    )(me, *pieces)


def together(*values):
    return lax.optimization_barrier(values)


def add(mine, got):
    return (mine.astype(F32) + got.astype(F32)).astype(BF16)


class PairwiseLinks:
    def __init__(self, mesh):
        self.mesh = Mesh(mesh.devices.reshape(2, 2, 2, 2, 2), ("x", "zh", "zl", "y", "c"))
        self.data = ("x", "zh", "zl", "y", "c")
        self.fsdp = ("zh", "zl", "y", "c")
        self.dp = "x"

    def swap(self, value, axis):
        return lax.ppermute(value, axis, [(0, 1), (1, 0)])

    def trade(self, value, axes):
        return lax.all_to_all(value, axes, 0, 0, tiled=True)

    def place_of(self, *axes):
        return jnp.stack([lax.axis_index(axis) for axis in axes]).astype(jnp.int32)

    def half(self, value, axis, at, other):
        first = lax.axis_index(axis) == (1 if other else 0)
        low = lax.index_in_dim(value, 0, at, keepdims=False)
        high = lax.index_in_dim(value, 1, at, keepdims=False)
        return jnp.where(first, low, high)

    def add_halves(self, value, axis, at):
        got = self.swap(self.half(value, axis, at, True), axis)
        return add(self.half(value, axis, at, False), got)

    def gather_all(self, dense, w_in, w_out):
        rows, columns = dense.shape
        in_raw = self.swap(w_in, "zh")
        copies = jnp.broadcast_to(dense[None], (4, rows, columns))
        own = self.trade(copies, ("zh", "zl"))
        in_near = self.trade(w_in, ("zl", "y"))
        over_y = self.swap(own, "y")
        over_x = self.swap(own, "x")
        over_xy = self.swap(over_y, "x")
        pieces = [own, over_y, over_x, over_xy]
        pieces = [piece for near in pieces for piece in (near, self.swap(near, "c"))]
        full = place(self.place_of("x", "y", "c"), pieces, (0, 2, 3)).reshape(32 * rows, columns)

        def finish(near, far):
            pieces = [near, self.swap(near, "c"), far, self.swap(far, "c")]
            joined = place(self.place_of("zh", "c"), pieces, (0, 2))
            return joined.reshape(-1, near.shape[-1])

        def finish_in(signal):
            signal, raw = together(signal, in_raw)
            return signal, finish(in_near, self.trade(raw, ("zl", "y")))

        out_near = self.trade(w_out, ("zl", "y"))
        out_far = self.swap(out_near, "zh")

        def finish_out(signal):
            signal, far = together(signal, out_far)
            return signal, finish(out_near, far)

        return full, finish_in, finish_out

    def send_slots(self, slots):
        return self.trade(slots, ("x", "zl", "y"))

    def return_slots(self, slots):
        return self.trade(slots, ("x", "zl", "y"))

    def core(self):
        return self.place_of("c")

    def expert_cores(self, mine, theirs):
        return add(mine, self.swap(theirs, "c"))

    def expert_far(self, part):
        got = self.swap(self.half(part, "zh", 0, True), "zh")
        return self.half(part, "zh", 0, False), got

    def expert_end(self, mine, got):
        return self.trade(add(mine, got), ("zl", "y")).astype(F32)

    def scatter_rows(self, value):
        rows, columns = value.shape
        part = value.reshape(2, 4, 2, 2, rows // 32, columns)
        part = self.add_halves(part, "c", 3)
        part = self.add_halves(part, "x", 0)
        part = self.add_halves(part, "y", 1)
        return jnp.sum(self.trade(part, ("zh", "zl")).astype(F32), axis=0)


class AxisLinks:
    def __init__(self, mesh):
        self.mesh = mesh
        self.data = ("dp", "fsdp")
        self.fsdp = "fsdp"
        self.dp = "dp"

    def gather_all(self, dense, w_in, w_out):
        def finish(shard):
            return lambda signal: (
                signal,
                lax.all_gather(shard, "fsdp", axis=1, tiled=True).reshape(-1, shard.shape[-1]),
            )

        return lax.all_gather(dense, self.data, axis=0, tiled=True), finish(w_in), finish(w_out)

    def send_slots(self, slots):
        return lax.all_to_all(slots, "dp", 0, 0, tiled=True)

    def return_slots(self, slots):
        return lax.all_to_all(slots, "dp", 0, 0, tiled=True)

    def core(self):
        return jnp.zeros((1,), jnp.int32)

    def expert_cores(self, mine, theirs):
        return jnp.stack([mine, theirs], axis=2)

    def expert_far(self, part):
        return part, None

    def expert_end(self, part, got):
        grad = part.reshape(1, -1, part.shape[-1])
        return lax.psum_scatter(grad, "fsdp", scatter_dimension=1, tiled=True).astype(F32)

    def scatter_rows(self, value):
        return lax.psum_scatter(value.astype(F32), self.data, scatter_dimension=0, tiled=True)


def per_device(
    links, tokens, gain_attn, w_qkv, w_proj, gain_moe, w_router, w_in, w_out, routes, slot_ids, cotangent
):
    small = jnp.concatenate([w_router, gain_attn[:, None], gain_moe[:, None]], axis=1)
    small = jnp.pad(small, ((0, 0), (0, LANES - small.shape[1])))
    own_qkv = by_pair(w_qkv)
    dense, finish_in, finish_out = links.gather_all(
        jnp.concatenate([own_qkv, w_proj, small], axis=1), w_in, w_out
    )
    routes_t = routes.T
    slots_t = slot_ids.T
    targets = jnp.where(slot_ids < CAP, routes * CAP + slot_ids, -1)

    qkv, act_one, table = project(tokens, dense)
    attended, logs = attention_forward(qkv)
    mid, act_two, columns, gates, rows_sent = middle(
        routes_t, slots_t, tokens, attended, dense, table
    )
    rows_sent, expert_in = finish_in(rows_sent)
    slot_rows = links.send_slots(rows_sent)
    grads_sent, slot_rows = together(slot_grads(routes_t, slots_t, gates, cotangent), slot_rows)
    grad_slots = links.send_slots(grads_sent)
    held = slot_rows.shape
    expert_rows = slot_rows.reshape(-1, WIDTH)
    hidden, slope = expert_up(expert_rows, expert_in)
    hidden, expert_out = finish_out(hidden)
    result, grad_slots = together(expert_down(hidden, expert_out), grad_slots)
    flat_result = links.return_slots(result.reshape(held)).reshape(SLOTS, WIDTH)
    grad_result = grad_slots.reshape(-1, WIDTH)

    core = links.core()
    out_part = links.expert_cores(*out_grad(core, hidden, grad_result))
    grad_pre, grad_rows = expert_back(grad_result, slope, expert_out, expert_in)
    grad_rows, flat_result = together(grad_rows, flat_result)
    rows_back = links.return_slots(grad_rows.reshape(held)).reshape(SLOTS, WIDTH)
    out_mine, out_got = links.expert_far(out_part)
    in_part = links.expert_cores(*in_grad(core, expert_rows, grad_pre))
    in_mine, in_got = links.expert_far(in_part)

    output, grad_logits = combine_results(routes, targets, columns, mid, cotangent, flat_result)
    grad_mid, low, grad_attended, d_gain = middle_back(
        targets, grad_logits, mid, cotangent, rows_back, dense, table
    )
    grad_qkv = attention_backward(qkv, attended, logs, grad_attended)
    d_qkv = qkv_grads(act_one, grad_qkv)
    d_rest = proj_grads(attended, low, act_two, grad_logits, d_gain)
    grad_tokens = token_grads(grad_qkv, dense, tokens, grad_mid, table)
    d_out = links.expert_end(out_mine, out_got)
    d_in = links.expert_end(in_mine, in_got)
    d_rest = links.scatter_rows(d_rest)
    d_qkv = links.scatter_rows(d_qkv)
    d_gain_attn = jnp.sum(d_qkv * own_qkv.astype(F32), axis=1) / gain_attn.astype(F32)
    return (
        output,
        grad_tokens,
        d_gain_attn,
        by_part(d_qkv),
        d_rest[:, :WIDTH],
        d_rest[:, WIDTH + GAIN_TWO],
        d_rest[:, WIDTH : WIDTH + EXPERTS],
        d_in,
        d_out,
    )


def solution(mesh):
    pairwise = mesh.shape["dp"] == 2 and mesh.shape["fsdp"] == 16
    links = PairwiseLinks(mesh) if pairwise else AxisLinks(mesh)
    rows = P(links.data, None)
    flat = P(links.data)
    expert = P(links.dp, links.fsdp, None)
    return jax.shard_map(
        lambda *arrays: per_device(links, *arrays),
        mesh=links.mesh,
        in_specs=(rows, flat, rows, rows, flat, rows, expert, expert, rows, rows, rows),
        out_specs=(rows, rows, flat, rows, rows, flat, rows, expert, expert),
        check_vma=False,
    )
```

```python
import math

import jax
import jax.numpy as jnp
from jax import lax
from jax.experimental import pallas as pl
from jax.experimental.pallas import tpu as pltpu
from jax.sharding import Mesh, PartitionSpec as P

HEADS = 12
HEAD_DIM = 64
EXPERTS = 8
SEQ = 576
CAP = 152
SLOTS = EXPERTS * CAP
NORM_EPSILON = 1e-06
SCALE = HEAD_DIM ** (-0.5)
PAIR = 2 * HEAD_DIM
PAIRS = HEADS // 2
WIDTH = HEADS * HEAD_DIM
LANES = 128
GAIN_ONE = EXPERTS
GAIN_TWO = EXPERTS + 1
TOKEN_BLOCK = 192
ROW_BLOCK = 304
F_BLOCK = 512
F32 = jnp.float32
BF16 = jnp.bfloat16
QUICK = pl.CostEstimate(flops=1, bytes_accessed=1, transcendentals=0)


def dot_nn(left, right):
    return jnp.dot(left, right, preferred_element_type=F32)


def dot_nt(left, right):
    return lax.dot_general(left, right, (((1,), (1,)), ((), ())), preferred_element_type=F32)


def dot_tn(left, right):
    return lax.dot_general(left, right, (((0,), (0,)), ((), ())), preferred_element_type=F32)


def scaled(values):
    return values * jnp.asarray(SCALE, BF16)


def norm_parts(values):
    centre = values - jnp.mean(values, axis=-1, keepdims=True)
    inverse = lax.rsqrt(jnp.mean(centre * centre, axis=-1, keepdims=True) + NORM_EPSILON)
    return centre * inverse, inverse


def norm_back(grad_normed, normed, inverse):
    mean_grad = jnp.mean(grad_normed, axis=-1, keepdims=True)
    mean_cross = jnp.mean(grad_normed * normed, axis=-1, keepdims=True)
    return (grad_normed - mean_grad - normed * mean_cross) * inverse


def whole(*shape):
    return pl.BlockSpec(shape, lambda *at: (0,) * len(shape))


def call(name, kernel, grid, in_specs, out_specs, out_shape, scratch=(), scalars=0):
    return pl.pallas_call(
        kernel,
        grid_spec=pltpu.PrefetchScalarGridSpec(
            num_scalar_prefetch=scalars,
            grid=grid,
            in_specs=in_specs,
            out_specs=out_specs,
            scratch_shapes=scratch,
        ),
        out_shape=out_shape,
        cost_estimate=QUICK,
        name=name,
    )


def struct(shape, dtype):
    return jax.ShapeDtypeStruct(shape, dtype)


def attention_kernel(qkv_ref, out_ref, log_ref):
    values_t = qkv_ref[:, 2 * PAIR :].T
    outs = []
    for head in range(2):
        at = head * HEAD_DIM
        queries = scaled(qkv_ref[:, at : at + HEAD_DIM])
        keys = qkv_ref[:, PAIR + at : PAIR + at + HEAD_DIM]
        scores = dot_nt(keys, queries)
        largest = jnp.max(scores, axis=0, keepdims=True)
        powers = jnp.exp(scores - largest)
        totals = jnp.sum(powers, axis=0, keepdims=True)
        mixed = dot_nn(values_t[at : at + HEAD_DIM], powers.astype(BF16))
        outs.append((mixed / totals).astype(BF16))
        log_ref[0, 0, head : head + 1, :] = largest + jnp.log(totals)
    out_ref[...] = jnp.concatenate(outs, axis=0).T


def attention_back_kernel(qkv_ref, out_ref, log_ref, grad_ref, result_ref):
    products = out_ref[...].T.astype(F32) * grad_ref[...].T.astype(F32)
    keys_t = scaled(qkv_ref[:, PAIR : 2 * PAIR]).T
    grad_queries = []
    for head in range(2):
        at = head * HEAD_DIM
        span = slice(at, at + HEAD_DIM)
        queries = scaled(qkv_ref[:, span])
        keys = qkv_ref[:, PAIR + at : PAIR + at + HEAD_DIM]
        values = qkv_ref[:, 2 * PAIR + at : 2 * PAIR + at + HEAD_DIM]
        grads = grad_ref[:, span]
        row_terms = jnp.sum(products[span], axis=0, keepdims=True)
        probs = jnp.exp(dot_nt(keys, queries) - log_ref[0, 0, head : head + 1, :])
        grad_scores = (probs * (dot_nt(values, grads) - row_terms)).astype(BF16)
        grad_values = dot_nn(probs.astype(BF16), grads)
        grad_keys = dot_nn(grad_scores, queries)
        result_ref[:, 2 * PAIR + at : 2 * PAIR + at + HEAD_DIM] = grad_values.astype(BF16)
        result_ref[:, PAIR + at : PAIR + at + HEAD_DIM] = grad_keys.astype(BF16)
        grad_queries.append(dot_nn(keys_t[span], grad_scores).astype(BF16))
    result_ref[:, :PAIR] = jnp.concatenate(grad_queries, axis=0).T


def attention_specs():
    return (
        pl.BlockSpec((SEQ, 3 * PAIR), lambda image, pair: (image, pair)),
        pl.BlockSpec((SEQ, PAIR), lambda image, pair: (image, pair)),
        pl.BlockSpec((1, 1, 2, SEQ), lambda image, pair: (image, pair, 0, 0)),
    )


def attention_forward(qkv):
    rows = qkv.shape[0]
    images = rows // SEQ
    wide, narrow, logs = attention_specs()
    return call(
        "attention_forward",
        attention_kernel,
        (images, PAIRS),
        [wide],
        [narrow, logs],
        [struct((rows, WIDTH), BF16), struct((images, PAIRS, 2, SEQ), F32)],
    )(qkv)


def attention_backward(qkv, attended, logs_saved, grad_attended):
    wide, narrow, logs = attention_specs()
    return call(
        "attention_backward",
        attention_back_kernel,
        (qkv.shape[0] // SEQ, PAIRS),
        [wide, narrow, logs, narrow],
        wide,
        struct(qkv.shape, BF16),
    )(qkv, attended, logs_saved, grad_attended)


QKV_SPEC = pl.BlockSpec((WIDTH, 3 * WIDTH), lambda *at: (0, 0))
PROJ_SPEC = pl.BlockSpec((WIDTH, WIDTH), lambda *at: (0, 3))
SMALL_SPEC = pl.BlockSpec((WIDTH, LANES), lambda *at: (0, 4 * WIDTH // LANES))


def project_kernel(tokens_ref, weight_ref, small_ref, qkv_ref, act_ref, table_ref):
    @pl.when(pl.program_id(0) == 0)
    def _():
        table = small_ref[...].T
        table_ref[...] = table
        gain = table[GAIN_ONE : GAIN_ONE + 1].astype(F32)
        normed, _ = norm_parts(tokens_ref[...].astype(F32))
        act_ref[...] = (normed * gain).astype(BF16)

    qkv_ref[...] = dot_nn(act_ref[...], weight_ref[...]).astype(BF16)


def project(tokens, dense):
    rows = tokens.shape[0]
    return call(
        "project",
        project_kernel,
        (PAIRS,),
        [
            whole(rows, WIDTH),
            pl.BlockSpec((WIDTH, 3 * PAIR), lambda pair: (0, pair)),
            SMALL_SPEC,
        ],
        [
            pl.BlockSpec((rows, 3 * PAIR), lambda pair: (0, pair)),
            whole(rows, WIDTH),
            whole(LANES, WIDTH),
        ],
        [
            struct((rows, 3 * WIDTH), BF16),
            struct((rows, WIDTH), BF16),
            struct((LANES, WIDTH), BF16),
        ],
    )(tokens, dense, dense)


def slot_hits(routes_ref, slots_ref):
    rows = routes_ref.shape[1]
    places = lax.broadcasted_iota(jnp.int32, (CAP, rows), 0)
    expert = pl.program_id(0)
    return [
        (routes_ref[k : k + 1, :] == expert) & (slots_ref[k : k + 1, :] == places)
        for k in range(2)
    ]


def middle_kernel(
    routes_ref, slots_ref, tokens_ref, attended_ref, proj_ref, table_ref,
    mid_ref, act_ref, columns_ref, gates_ref, slot_rows_ref,
):
    @pl.when(pl.program_id(0) == 0)
    def _():
        mid = tokens_ref[...].astype(F32) + dot_nn(attended_ref[...], proj_ref[...])
        mid_ref[...] = mid
        normed, _ = norm_parts(mid)
        gain = table_ref[GAIN_TWO : GAIN_TWO + 1, :].astype(F32)
        act = (normed * gain).astype(BF16)
        act_ref[...] = act
        logits = dot_nt(table_ref[:16, :], act)[:EXPERTS]
        powers = jnp.exp(logits - jnp.max(logits, axis=0, keepdims=True))
        router = powers / jnp.sum(powers, axis=0, keepdims=True)
        names = lax.broadcasted_iota(jnp.int32, router.shape, 0)
        gates = [
            jnp.sum(jnp.where(names == routes_ref[k : k + 1, :], router, 0.0), axis=0, keepdims=True)
            .astype(BF16)
            .astype(F32)
            for k in range(2)
        ]
        rows = router.shape[1]
        gates = jnp.concatenate(gates + [jnp.zeros((EXPERTS - 2, rows), F32)], axis=0)
        gates_ref[...] = gates
        spare = jnp.zeros((LANES - 2 * EXPERTS, rows), F32)
        columns_ref[...] = jnp.concatenate([router, gates, spare], axis=0).T

    first, second = slot_hits(routes_ref, slots_ref)
    dispatch = jnp.where(first | second, 1.0, 0.0).astype(BF16)
    slot_rows_ref[0] = dot_nn(dispatch, act_ref[...]).astype(BF16)


def middle(routes_t, slots_t, tokens, attended, dense, table):
    rows = tokens.shape[0]
    return call(
        "middle",
        middle_kernel,
        (EXPERTS,),
        [
            whole(2, rows),
            whole(2, rows),
            whole(rows, WIDTH),
            whole(rows, WIDTH),
            PROJ_SPEC,
            whole(LANES, WIDTH),
        ],
        [
            whole(rows, WIDTH),
            whole(rows, WIDTH),
            whole(rows, LANES),
            whole(EXPERTS, rows),
            pl.BlockSpec((1, CAP, WIDTH), lambda expert: (expert, 0, 0)),
        ],
        [
            struct((rows, WIDTH), F32),
            struct((rows, WIDTH), BF16),
            struct((rows, LANES), F32),
            struct((EXPERTS, rows), F32),
            struct((EXPERTS, CAP, WIDTH), BF16),
        ],
    )(routes_t, slots_t, tokens, attended, dense, table)


def slot_grads_kernel(routes_ref, slots_ref, gates_ref, grad_ref, result_ref):
    first, second = slot_hits(routes_ref, slots_ref)
    combine = jnp.where(first, gates_ref[0:1, :], jnp.where(second, gates_ref[1:2, :], 0.0))
    result_ref[0] = dot_nn(combine.astype(BF16), grad_ref[...]).astype(BF16)


def slot_grads(routes_t, slots_t, gates, cotangent):
    rows = cotangent.shape[0]
    return call(
        "slot_grads",
        slot_grads_kernel,
        (EXPERTS,),
        [whole(2, rows), whole(2, rows), whole(EXPERTS, rows), whole(rows, WIDTH)],
        pl.BlockSpec((1, CAP, WIDTH), lambda expert: (expert, 0, 0)),
        struct((EXPERTS, CAP, WIDTH), BF16),
    )(routes_t, slots_t, gates, cotangent)


def expert_up_kernel(rows_ref, weight_ref, hidden_ref, slope_ref):
    root = math.sqrt(2.0 / math.pi)
    value = dot_nn(rows_ref[...], weight_ref[...])
    square = value * value
    curve = jnp.tanh(value * (root + (root * 0.044715) * square))
    upper = 0.5 + 0.5 * curve
    hidden_ref[...] = (value * upper).astype(BF16)
    inner = value * (root + (3.0 * root * 0.044715) * square)
    slope_ref[...] = (upper + (0.5 - 0.5 * curve * curve) * inner).astype(BF16)


def expert_up(rows, weight):
    count, depth = rows.shape[0], weight.shape[1]
    wide = pl.BlockSpec((count, F_BLOCK), lambda f: (0, f))
    return call(
        "expert_up",
        expert_up_kernel,
        (depth // F_BLOCK,),
        [whole(count, WIDTH), pl.BlockSpec((WIDTH, F_BLOCK), lambda f: (0, f))],
        [wide, wide],
        [struct((count, depth), BF16)] * 2,
    )(rows, weight)


def expert_down_kernel(hidden_ref, weight_ref, result_ref):
    result_ref[...] = dot_nn(hidden_ref[...], weight_ref[...]).astype(BF16)


def expert_down(hidden, weight):
    count, depth = hidden.shape
    return call(
        "expert_down",
        expert_down_kernel,
        (count // ROW_BLOCK,),
        [pl.BlockSpec((ROW_BLOCK, depth), lambda r: (r, 0)), whole(depth, WIDTH)],
        pl.BlockSpec((ROW_BLOCK, WIDTH), lambda r: (r, 0)),
        struct((count, WIDTH), BF16),
    )(hidden, weight)


def expert_back_kernel(grad_ref, slope_ref, out_ref, in_ref, grad_pre_ref, grad_rows_ref):
    grad_hidden = dot_nt(grad_ref[...], out_ref[...])
    grad_pre = (grad_hidden * slope_ref[...].astype(F32)).astype(BF16)
    grad_pre_ref[...] = grad_pre
    grad_rows_ref[...] = dot_nt(grad_pre, in_ref[...]).astype(BF16)


def expert_back(grad_result, slope, weight_out, weight_in):
    count, depth = slope.shape
    wide = pl.BlockSpec((ROW_BLOCK, depth), lambda r: (r, 0))
    narrow = pl.BlockSpec((ROW_BLOCK, WIDTH), lambda r: (r, 0))
    return call(
        "expert_back",
        expert_back_kernel,
        (count // ROW_BLOCK,),
        [narrow, wide, whole(depth, WIDTH), whole(WIDTH, depth)],
        [wide, narrow],
        [struct((count, depth), BF16), struct((count, WIDTH), BF16)],
    )(grad_result, slope, weight_out, weight_in)


def out_grad_kernel(me_ref, hidden_ref, grad_ref, mine_ref, theirs_ref):
    value = dot_tn(hidden_ref[...], grad_ref[...]).astype(BF16)
    half = value.shape[0] // 2
    first = me_ref[0] == 0
    mine_ref[0, 0] = jnp.where(first, value[:half], value[half:])
    theirs_ref[0, 0] = jnp.where(first, value[half:], value[:half])


def out_grad(me, hidden, grad_result):
    count, depth = hidden.shape
    rest = depth // 16
    half = pl.BlockSpec((1, 1, rest, WIDTH), lambda f, me: (f // 4, lax.rem(f, 4), 0, 0))
    return call(
        "out_grad",
        out_grad_kernel,
        (8,),
        [pl.BlockSpec((count, 2 * rest), lambda f, me: (0, f)), whole(count, WIDTH)],
        [half, half],
        [struct((2, 4, rest, WIDTH), BF16)] * 2,
        scalars=1,
    )(me, hidden, grad_result)


def in_grad_kernel(me_ref, rows_ref, grad_ref, mine_ref, theirs_ref, turned_ref):
    @pl.when(pl.program_id(0) == 0)
    def _():
        turned_ref[...] = rows_ref[...].T

    value = dot_nn(turned_ref[...], grad_ref[...]).astype(BF16)
    value = value.reshape(8, 2, WIDTH // 16, F_BLOCK)
    first = me_ref[0] == 0
    shape = mine_ref.shape
    mine_ref[...] = jnp.where(first, value[:, 0], value[:, 1]).reshape(shape)
    theirs_ref[...] = jnp.where(first, value[:, 1], value[:, 0]).reshape(shape)


def in_grad(me, rows, grad_pre):
    count, depth = grad_pre.shape
    rest = WIDTH // 16
    half = pl.BlockSpec((2, 4, rest, F_BLOCK), lambda f, me: (0, 0, 0, f))
    return call(
        "in_grad",
        in_grad_kernel,
        (depth // F_BLOCK,),
        [whole(count, WIDTH), pl.BlockSpec((count, F_BLOCK), lambda f, me: (0, f))],
        [half, half],
        [struct((2, 4, rest, depth), BF16)] * 2,
        scratch=[pltpu.VMEM((WIDTH, count), BF16)],
        scalars=1,
    )(me, rows, grad_pre)


def token_hits(targets_ref):
    columns = lax.broadcasted_iota(jnp.int32, (targets_ref.shape[0], SLOTS), 1)
    return [targets_ref[:, k : k + 1] == columns for k in range(2)]


def combine_kernel(
    routes_ref, targets_ref, columns_ref, mid_ref, grad_ref, result_ref, output_ref, logits_ref
):
    first, second = token_hits(targets_ref)
    gates = columns_ref[:, EXPERTS : EXPERTS + 2]
    combine = jnp.where(first, gates[:, 0:1], jnp.where(second, gates[:, 1:2], 0.0)).astype(BF16)
    output_ref[...] = (mid_ref[...] + dot_nn(combine, result_ref[...])).astype(BF16)
    crossed = dot_nt(grad_ref[...], result_ref[...])
    lanes = lax.broadcasted_iota(jnp.int32, columns_ref.shape, 1)
    grad_router = jnp.zeros(columns_ref.shape, F32)
    for k, hits in enumerate((first, second)):
        grad_gate = jnp.sum(jnp.where(hits, crossed, 0.0), axis=1, keepdims=True)
        grad_router += jnp.where(lanes == routes_ref[:, k : k + 1], grad_gate, 0.0)
    router = jnp.where(lanes < EXPERTS, columns_ref[...], 0.0)
    total = jnp.sum(router * grad_router, axis=1, keepdims=True)
    logits_ref[...] = (router * (grad_router - total)).astype(BF16)


def token_spec(columns):
    return pl.BlockSpec((TOKEN_BLOCK, columns), lambda t: (t, 0))


def combine_results(routes, targets, columns, mid, cotangent, result):
    rows = mid.shape[0]
    return call(
        "combine",
        combine_kernel,
        (rows // TOKEN_BLOCK,),
        [
            token_spec(2),
            token_spec(2),
            token_spec(LANES),
            token_spec(WIDTH),
            token_spec(WIDTH),
            whole(SLOTS, WIDTH),
        ],
        [token_spec(WIDTH), token_spec(LANES)],
        [struct((rows, WIDTH), BF16), struct((rows, LANES), BF16)],
    )(routes, targets, columns, mid, cotangent, result)


def middle_back_kernel(
    targets_ref, logits_ref, mid_ref, grad_ref, rows_ref, proj_ref, table_ref,
    grad_mid_ref, low_ref, attended_ref, gain_ref,
):
    first, second = token_hits(targets_ref)
    dispatch = jnp.where(first | second, 1.0, 0.0).astype(BF16)
    grad_act = dot_nn(dispatch, rows_ref[...]) + dot_nn(logits_ref[...], table_ref[...])
    normed, inverse = norm_parts(mid_ref[...])
    gain = table_ref[GAIN_TWO : GAIN_TWO + 1, :].astype(F32)
    part = jnp.sum(grad_act * normed, axis=0, keepdims=True)

    @pl.when(pl.program_id(0) == 0)
    def _():
        gain_ref[...] = jnp.zeros_like(gain_ref)

    gain_ref[0:1, :] += part
    grad_mid = grad_ref[...].astype(F32) + norm_back(grad_act * gain, normed, inverse)
    grad_mid_ref[...] = grad_mid
    low = grad_mid.astype(BF16)
    low_ref[...] = low
    attended_ref[...] = dot_nt(low, proj_ref[...]).astype(BF16)


def middle_back(targets, logits, mid, cotangent, grad_rows, dense, table):
    rows = mid.shape[0]
    return call(
        "middle_back",
        middle_back_kernel,
        (rows // TOKEN_BLOCK,),
        [
            token_spec(2),
            token_spec(LANES),
            token_spec(WIDTH),
            token_spec(WIDTH),
            whole(SLOTS, WIDTH),
            PROJ_SPEC,
            whole(LANES, WIDTH),
        ],
        [token_spec(WIDTH), token_spec(WIDTH), token_spec(WIDTH), whole(8, WIDTH)],
        [
            struct((rows, WIDTH), F32),
            struct((rows, WIDTH), BF16),
            struct((rows, WIDTH), BF16),
            struct((8, WIDTH), F32),
        ],
    )(targets, logits, mid, cotangent, grad_rows, dense, table)


def write_halves(value, first, mine_ref, theirs_ref):
    value = value.reshape(2, 4, 2, 2, value.shape[0] // 32, value.shape[1])
    for x, y, z in ((x, y, z) for x in range(2) for y in range(2) for z in range(4)):
        low, high = value[x, z, y, 0], value[x, z, y, 1]
        mine_ref[x, y, z] = jnp.where(first, low, high).astype(BF16)
        theirs_ref[x, y, z] = jnp.where(first, high, low).astype(BF16)


def proj_grads_kernel(
    me_ref, attended_ref, low_ref, act_ref, logits_ref, gain_ref, mine_ref, theirs_ref
):
    wide = dot_tn(attended_ref[...], low_ref[...])
    small = dot_tn(act_ref[...], logits_ref[...])
    lanes = lax.broadcasted_iota(jnp.int32, small.shape, 1)
    gain = gain_ref[...].T[:, 0:1]
    value = jnp.concatenate([wide, jnp.where(lanes == GAIN_TWO, gain, small)], axis=1)
    write_halves(value, me_ref[0] == 0, mine_ref, theirs_ref)


def proj_grads(me, attended, low, act_two, logits, gain):
    rows = low.shape[0]
    half = (2, 2, 4, WIDTH // 32, WIDTH + LANES)
    return call(
        "proj_grads",
        proj_grads_kernel,
        (1,),
        [whole(rows, WIDTH)] * 3 + [whole(rows, LANES), whole(8, WIDTH)],
        [whole(*half)] * 2,
        [struct(half, BF16)] * 2,
        scalars=1,
    )(me, attended, low, act_two, logits, gain)


def qkv_grads_kernel(me_ref, act_ref, grad_ref, mine_ref, theirs_ref, turned_ref):
    @pl.when(pl.program_id(0) == 0)
    def _():
        turned_ref[...] = act_ref[...].T

    value = dot_nn(turned_ref[...], grad_ref[...])
    write_halves(value, me_ref[0] == 0, mine_ref, theirs_ref)


def qkv_grads(me, act_one, grad_qkv):
    rows = act_one.shape[0]
    half = (2, 2, 4, WIDTH // 32)
    spec = pl.BlockSpec(half + (3 * PAIR,), lambda pair, me: (0, 0, 0, 0, pair))
    return call(
        "qkv_grads",
        qkv_grads_kernel,
        (PAIRS,),
        [whole(rows, WIDTH), pl.BlockSpec((rows, 3 * PAIR), lambda pair, me: (0, pair))],
        [spec, spec],
        [struct(half + (3 * WIDTH,), BF16)] * 2,
        scratch=[pltpu.VMEM((WIDTH, rows), BF16)],
        scalars=1,
    )(me, act_one, grad_qkv)


def token_grads_kernel(grad_ref, weight_ref, tokens_ref, grad_mid_ref, table_ref, result_ref):
    grad_act = dot_nt(grad_ref[...], weight_ref[...])
    normed, inverse = norm_parts(tokens_ref[...].astype(F32))
    gain = table_ref[GAIN_ONE : GAIN_ONE + 1, :].astype(F32)
    result_ref[...] = grad_mid_ref[...] + norm_back(grad_act * gain, normed, inverse)


def token_grads(grad_qkv, dense, tokens, grad_mid, table):
    rows = tokens.shape[0]
    return call(
        "token_grads",
        token_grads_kernel,
        (rows // TOKEN_BLOCK,),
        [token_spec(3 * WIDTH), QKV_SPEC, token_spec(WIDTH), token_spec(WIDTH), whole(LANES, WIDTH)],
        token_spec(WIDTH),
        struct((rows, WIDTH), F32),
    )(grad_qkv, dense, tokens, grad_mid, table)


def by_pair(columns):
    rows = columns.shape[0]
    return columns.reshape(rows, 3, PAIRS, PAIR).transpose(0, 2, 1, 3).reshape(rows, -1)


def by_part(columns):
    rows = columns.shape[0]
    return columns.reshape(rows, PAIRS, 3, PAIR).transpose(0, 2, 1, 3).reshape(rows, -1)


def place_kernel(count, me_ref, *refs):
    pieces, result_ref = refs[:-1], refs[-1]
    at = 0
    for axis in range(count):
        at = 2 * at + lax.rem(pl.program_id(axis) + me_ref[axis], 2)
    for index, piece in enumerate(pieces):

        @pl.when(at == index)
        def _():
            result_ref[...] = piece[...].reshape(result_ref.shape)


def place(me, pieces, axes):
    count = len(axes)
    shape = list(pieces[0].shape)
    for axis in axes:
        shape.insert(axis, 2)
    block = [1 if axis in axes else size for axis, size in enumerate(shape)]

    def index(*at):
        return tuple(at[axes.index(a)] if a in axes else 0 for a in range(len(shape)))

    return call(
        "place",
        lambda *refs: place_kernel(count, *refs),
        (2,) * count,
        [whole(*piece.shape) for piece in pieces],
        pl.BlockSpec(tuple(block), index),
        struct(tuple(shape), pieces[0].dtype),
        scalars=1,
    )(me, *pieces)


def join_kernel(bounds, me_ref, near_ref, near_core_ref, *refs):
    zh, core = me_ref[0], me_ref[1]
    result_ref = refs[-1]
    result_ref[zh, 0, core] = near_ref[0]
    result_ref[zh, 0, 1 - core] = near_core_ref[0]
    for part, (begin, end) in enumerate(bounds):

        @pl.when((pl.program_id(0) >= begin) & (pl.program_id(0) < end))
        def _():
            result_ref[1 - zh, 0, core] = refs[part][0]
            result_ref[1 - zh, 0, 1 - core] = refs[len(bounds) + part][0]


def join(me, near, near_core, far, far_core):
    blocks, rest, columns = near.shape
    bounds, end = [], 0
    for part in far:
        bounds.append((end, end + part.shape[0]))
        end += part.shape[0]

    def piece(begin, end):
        return pl.BlockSpec(
            (1, rest, columns), lambda b, me: (jnp.clip(b - begin, 0, end - begin - 1), 0, 0)
        )

    return call(
        "join",
        lambda *refs: join_kernel(bounds, *refs),
        (blocks,),
        [piece(0, blocks)] * 2 + [piece(*at) for at in bounds] * 2,
        pl.BlockSpec((2, 1, 2, rest, columns), lambda b, me: (0, b, 0, 0, 0)),
        struct((2, blocks, 2, rest, columns), near.dtype),
        scalars=1,
    )(me, near, near_core, *far, *far_core).reshape(-1, columns)


def parts_of(columns):
    return 3 if columns % (3 * LANES) == 0 else 1


def columns_of(shape):
    block = tuple(shape[:-1]) + (shape[-1] // parts_of(shape[-1]),)
    return pl.BlockSpec(block, lambda i, me: (0,) * (len(shape) - 1) + (i,))


def pick_kernel(count, me_ref, *refs):
    parts, outs = refs[:-count], refs[-count:]
    places = [(ref, at) for ref in parts for at in range(ref.shape[0])]
    for place_at, (part, at) in enumerate(places):
        for k, ref in enumerate(outs):

            @pl.when((me_ref[0] ^ k) == place_at)
            def _():
                ref[...] = part[at]


def pick(me, *parts):
    count, shape = sum(part.shape[0] for part in parts), parts[0].shape[1:]
    return call(
        "pick",
        lambda *refs: pick_kernel(count, *refs),
        (parts_of(shape[-1]),),
        [columns_of(part.shape) for part in parts],
        [columns_of(shape)] * count,
        [struct(shape, BF16)] * count,
        scalars=1,
    )(me, *parts)


def pack_kernel(me_ref, *refs):
    for k, ref in enumerate(refs[:-1]):
        refs[-1][me_ref[0] ^ k] = ref[...].astype(refs[-1].dtype)


def pack(me, pieces, dtype=BF16):
    shape = (len(pieces),) + pieces[0].shape
    return call(
        "pack",
        pack_kernel,
        (parts_of(shape[-1]),),
        [columns_of(shape[1:])] * len(pieces),
        columns_of(shape),
        struct(shape, dtype),
        scalars=1,
    )(me, *pieces)


def add_halves_kernel(me_ref, mine_ref, got_ref, keep_ref, *send_refs):
    def total(at):
        return (mine_ref[at].astype(F32) + got_ref[at].astype(F32)).astype(BF16)

    keep_ref[...] = total(me_ref[0])
    send = total(1 - me_ref[0])
    begin = 0
    for ref in send_refs:
        ref[...] = send[begin : begin + ref.shape[0]]
        begin += ref.shape[0]


def add_halves(me, mine, got, counts):
    shapes = [(count,) + mine.shape[2:] for count in (mine.shape[1],) + counts]
    return call(
        "add_halves",
        add_halves_kernel,
        (parts_of(mine.shape[-1]),),
        [columns_of(mine.shape)] * 2,
        [columns_of(shape) for shape in shapes],
        [struct(shape, BF16) for shape in shapes],
        scalars=1,
    )(me, mine, got)


def add_pick_kernel(me_ref, mine_ref, *refs):
    gots, outs = refs[: -mine_ref.shape[0]], refs[-mine_ref.shape[0] :]
    got = jnp.concatenate([ref[...] for ref in gots], axis=0).astype(F32)
    for at in range(mine_ref.shape[0]):
        value = (mine_ref[at].astype(F32) + got[at]).astype(BF16)
        for k, ref in enumerate(outs):

            @pl.when((me_ref[0] ^ k) == at)
            def _():
                ref[...] = value


def add_pick(me, mine, gots):
    count, shape = mine.shape[0], mine.shape[1:]
    return call(
        "add_pick",
        add_pick_kernel,
        (parts_of(shape[-1]),),
        [columns_of(mine.shape)] + [columns_of(got.shape) for got in gots],
        [columns_of(shape)] * count,
        [struct(shape, BF16)] * count,
        scalars=1,
    )(me, mine, *gots)


def dense_pick_kernel(me_ref, *refs):
    outs = refs[-4:]
    begin = 0
    for mine_ref, got_ref in zip(refs[:-4:2], refs[1:-4:2]):
        end = begin + mine_ref.shape[-1]
        for at in range(4):
            value = (mine_ref[at].astype(F32) + got_ref[at].astype(F32)).astype(BF16)
            for k, ref in enumerate(outs):

                @pl.when((me_ref[0] ^ k) == at)
                def _():
                    ref[:, begin:end] = value

        begin = end


def dense_pick(me, pairs):
    arrays = [array.reshape(4, -1, array.shape[-1]) for pair in pairs for array in pair]
    shape = (arrays[0].shape[1], sum(array.shape[-1] for array in arrays[::2]))
    half = shape[0] // 2
    return call(
        "dense_pick",
        dense_pick_kernel,
        (2,),
        [pl.BlockSpec((4, half, array.shape[-1]), lambda i, me: (0, i, 0)) for array in arrays],
        [pl.BlockSpec((half, shape[1]), lambda i, me: (i, 0))] * 4,
        [struct(shape, BF16)] * 4,
        scalars=1,
    )(me, *arrays)


def turn_kernel(me_ref, *refs):
    outs = refs[-4:]
    total = sum(ref[...].astype(F32) for ref in refs[:-4])
    total = total.reshape(4, total.shape[0] // 4, total.shape[1])
    for at in range(4):
        value = total[at].astype(BF16)
        for k, ref in enumerate(outs):

            @pl.when((me_ref[0] ^ k) == at)
            def _():
                ref[...] = value


def turn(me, pieces):
    shape = (pieces[0].shape[0] // 4, pieces[0].shape[1])
    return call(
        "turn",
        turn_kernel,
        (1,),
        [whole(*piece.shape) for piece in pieces],
        [whole(*shape)] * 4,
        [struct(shape, BF16)] * 4,
        scalars=1,
    )(me, *pieces)


def together(*values):
    return lax.optimization_barrier(values)


def add(mine, got):
    return (mine.astype(F32) + got.astype(F32)).astype(BF16)


class PairwiseLinks:
    def __init__(self, mesh):
        self.mesh = Mesh(mesh.devices.reshape(2, 2, 2, 2, 2), ("x", "zh", "zl", "y", "c"))
        self.data = ("x", "zh", "zl", "y", "c")
        self.fsdp = ("zh", "zl", "y", "c")
        self.dp = "x"

    def swap(self, value, axis):
        return lax.ppermute(value, axis, [(0, 1), (1, 0)])

    def trade(self, value, axes):
        return lax.all_to_all(value, axes, 0, 0, tiled=True)

    def place_of(self, *axes):
        return jnp.stack([lax.axis_index(axis) for axis in axes]).astype(jnp.int32)

    def core(self):
        return self.place_of("c")

    def number(self, *axes):
        index = 0
        for axis in axes:
            index = 2 * index + lax.axis_index(axis)
        return index.astype(jnp.int32)[None]

    def moved(self, pieces, *axes):
        count = len(pieces)
        routes = [[(i, i ^ k) for i in range(count)] for k in range(count)]
        return [pieces[0]] + [lax.ppermute(pieces[k], axes, routes[k]) for k in range(1, count)]

    def gather(self, dense, w_in, w_out):
        near = self.number("zl", "y")
        own = pack(self.number("zh", "zl"), self.moved([dense] * 4, "zh", "zl"))
        in_parts, out_parts = pick(near, w_in), pick(near, w_out)
        own, first, second, third, in_parts, out_parts = together(
            own, w_in[:1], w_in[1:2], w_in[2:], in_parts, out_parts
        )
        over_y, over_x, first, second, third, in_parts = together(
            self.swap(own, "y"), self.swap(own, "x"), self.swap(first, "zh"), second, third, in_parts
        )
        firsts = [own, over_y, over_x]
        over_xy = self.swap(over_y, "x")
        second = self.swap(second, "zh")
        theirs, in_parts = together([self.swap(value, "c") for value in firsts], in_parts)
        in_near = self.moved(in_parts, "zl", "y")
        over_xy, second, third = together(over_xy, second, third)
        pieces = [value for pair in zip(firsts, theirs) for value in pair]
        pieces += [over_xy, self.swap(over_xy, "c")]
        third = self.swap(third, "zh")
        full = place(self.place_of("x", "y", "c"), pieces, (0, 2, 3))
        full = full.reshape(32 * dense.shape[0], dense.shape[1])
        full, in_near, out_parts = together(full, in_near, out_parts)
        out_near = self.moved(out_parts, "zl", "y")
        return full, {"in_near": in_near, "in_far": [first, second, third], "out_near": out_near}

    def after_project(self, kept, value):
        near = self.number("zl", "y")
        value, far, out_near = together(value, kept["in_far"], kept["out_near"])
        value, far, out_near = together(value, pick(near, *far), pack(near, out_near))
        kept["in_far"] = self.moved(far, "zl", "y")
        kept["out_near"] = out_near
        kept["out_far"] = [self.swap(out_near[:1], "zh")]
        return value

    def after_middle(self, kept, *values):
        *values, kept["in_far"], near, first = together(
            *values, kept["in_far"], kept["out_near"], kept["out_far"][0]
        )
        kept["out_near"] = near
        kept["out_far"] = [first, self.swap(near[1:3], "zh")]
        return values

    def before_grads(self, kept, *values):
        *values, near, second = together(*values, kept["out_near"], kept["out_far"][1])
        kept["out_near"] = near
        kept["out_far"] = [kept["out_far"][0], second, self.swap(near[3:], "zh")]
        return values

    def joined(self, near, far):
        cores = [self.swap(part, "c") for part in far]
        return join(self.place_of("zh", "c"), near, self.swap(near, "c"), far, cores)

    def expert_in(self, kept):
        near = self.number("zl", "y")
        return self.joined(pack(near, kept["in_near"]), [pack(near, kept["in_far"])])

    def expert_out(self, kept, *values):
        *values, last = together(*values, kept["out_far"][2])
        return *values, self.joined(kept["out_near"], kept["out_far"][:2] + [last])

    def send_slots(self, slots):
        return self.trade(slots, ("x", "zl", "y"))

    def return_slots(self, slots):
        return self.trade(slots, ("x", "zl", "y"))

    def other_core(self, theirs):
        return self.swap(theirs, "c")

    def expert_parts(self, mine, got, counts):
        return add_halves(self.place_of("zh"), mine, got, counts)

    def expert_far(self, parts):
        return parts[0], [self.swap(part, "zh") for part in parts[1:]]

    def expert_pick(self, mine, got):
        return add_pick(self.number("zl", "y"), mine, got)

    def expert_end(self, pieces):
        return pack(self.number("zl", "y"), self.moved(pieces, "zl", "y"), F32)

    def rows_pick(self, *pairs):
        return dense_pick(self.number("x", "y"), pairs)

    def rows_send(self, pieces):
        return self.moved(pieces, "x", "y")

    def rows_turn(self, pieces):
        return turn(self.number("zh", "zl"), pieces)

    def rows_end(self, pieces):
        return sum(piece.astype(F32) for piece in self.moved(pieces, "zh", "zl"))


class AxisLinks:
    def __init__(self, mesh):
        self.mesh = mesh
        self.data = ("dp", "fsdp")
        self.fsdp = "fsdp"
        self.dp = "dp"

    def core(self):
        return jnp.zeros((1,), jnp.int32)

    def gather(self, dense, w_in, w_out):
        full = lax.all_gather(dense, self.data, axis=0, tiled=True)
        return full, {"in": w_in, "out": w_out}

    def after_project(self, kept, value):
        return value

    def after_middle(self, kept, *values):
        return values

    def before_grads(self, kept, *values):
        return values

    def full_rows(self, shard):
        return lax.all_gather(shard, "fsdp", axis=1, tiled=True).reshape(-1, shard.shape[-1])

    def expert_in(self, kept):
        return self.full_rows(kept["in"])

    def expert_out(self, kept, *values):
        return *values, self.full_rows(kept["out"])

    def send_slots(self, slots):
        return lax.all_to_all(slots, "dp", 0, 0, tiled=True)

    def return_slots(self, slots):
        return lax.all_to_all(slots, "dp", 0, 0, tiled=True)

    def other_core(self, theirs):
        return theirs

    def expert_parts(self, mine, got, counts):
        return [jnp.stack([mine, got], axis=2).reshape(1, -1, mine.shape[-1])]

    def expert_far(self, parts):
        return parts[0], []

    def expert_pick(self, mine, got):
        return [mine]

    def expert_end(self, pieces):
        return lax.psum_scatter(pieces[0], "fsdp", scatter_dimension=1, tiled=True).astype(F32)

    def rows_pick(self, *pairs):
        value = jnp.concatenate([jnp.stack(pair, axis=3) for pair in pairs], axis=-1)
        value = value.transpose(0, 2, 1, 3, 4, 5)
        return [value.reshape(-1, value.shape[-1]).astype(F32)]

    def rows_send(self, pieces):
        return [lax.psum_scatter(pieces[0], self.data, scatter_dimension=0, tiled=True)]

    def rows_turn(self, pieces):
        return pieces

    def rows_end(self, pieces):
        return pieces[0]


def per_device(
    links, tokens, gain_attn, w_qkv, w_proj, gain_moe, w_router, w_in, w_out, routes, slot_ids, cotangent
):
    core = links.core()
    small = jnp.concatenate([w_router, gain_attn[:, None], gain_moe[:, None]], axis=1)
    small = jnp.pad(small, ((0, 0), (0, LANES - small.shape[1])))
    own_qkv = by_pair(w_qkv)
    dense, kept = links.gather(
        jnp.concatenate([own_qkv, w_proj, small], axis=1), w_in, w_out
    )
    routes_t = routes.T
    slots_t = slot_ids.T
    targets = jnp.where(slot_ids < CAP, routes * CAP + slot_ids, -1)

    qkv, act_one, table = project(tokens, dense)
    qkv = links.after_project(kept, qkv)
    attended, logs = attention_forward(qkv)
    mid, act_two, columns, gates, rows_sent = middle(
        routes_t, slots_t, tokens, attended, dense, table
    )
    rows_sent, gates = links.after_middle(kept, rows_sent, gates)
    slot_rows = links.send_slots(rows_sent)
    grads_sent = slot_grads(routes_t, slots_t, gates, cotangent)
    expert_in = links.expert_in(kept)
    grads_sent, slot_rows, expert_in = links.before_grads(kept, grads_sent, slot_rows, expert_in)
    grad_slots = links.send_slots(grads_sent)
    held = slot_rows.shape
    expert_rows = slot_rows.reshape(-1, WIDTH)
    hidden, slope = expert_up(expert_rows, expert_in)
    hidden, expert_out = links.expert_out(kept, hidden)
    result, grad_slots, slope = together(expert_down(hidden, expert_out), grad_slots, slope)
    flat_result = links.return_slots(result.reshape(held)).reshape(SLOTS, WIDTH)
    grad_result = grad_slots.reshape(-1, WIDTH)

    out_mine, out_theirs = out_grad(core, hidden, grad_result)
    out_theirs, slope = together(out_theirs, slope)
    out_got = links.other_core(out_theirs)
    grad_pre, grad_rows = expert_back(grad_result, slope, expert_out, expert_in)
    grad_rows, out_got = together(grad_rows, out_got)
    rows_back = links.return_slots(grad_rows.reshape(held)).reshape(SLOTS, WIDTH)
    grad_pre, *out_parts = together(grad_pre, *links.expert_parts(out_mine, out_got, (4,)))
    out_keep, out_far = links.expert_far(out_parts)
    in_mine, in_theirs = in_grad(core, expert_rows, grad_pre)
    in_theirs, flat_result = together(in_theirs, flat_result)
    in_got = links.other_core(in_theirs)
    output, grad_logits = combine_results(routes, targets, columns, mid, cotangent, flat_result)
    grad_logits, rows_back = together(grad_logits, rows_back)
    grad_mid, low, grad_attended, d_gain = middle_back(
        targets, grad_logits, mid, cotangent, rows_back, dense, table
    )
    rest_mine, rest_theirs = proj_grads(core, attended, low, act_two, grad_logits, d_gain)
    rest_theirs, grad_attended = together(rest_theirs, grad_attended)
    grad_qkv = attention_backward(qkv, attended, logs, grad_attended)
    grad_qkv, rest_theirs, out_far, in_got = together(grad_qkv, rest_theirs, out_far, in_got)
    rest_got = links.other_core(rest_theirs)
    in_parts, grad_qkv = together(links.expert_parts(in_mine, in_got, (1, 2, 1)), grad_qkv)
    in_keep, in_first = links.expert_far(in_parts[:2])
    qkv_mine, qkv_theirs = qkv_grads(core, act_one, grad_qkv)
    qkv_theirs, rest_got, in_first, in_later = together(
        qkv_theirs, rest_got, in_first, in_parts[2:]
    )
    qkv_got = links.other_core(qkv_theirs)
    qkv_parts, grad_qkv, out_keep, in_later = together(
        links.rows_pick((qkv_mine, qkv_got), (rest_mine, rest_got)), grad_qkv, out_keep, in_later
    )
    qkv_sent = links.rows_send(qkv_parts)
    _, in_second = links.expert_far([in_keep] + list(in_later[:1]))
    grad_tokens = token_grads(grad_qkv, dense, tokens, grad_mid, table)
    out_pieces = links.expert_pick(out_keep, out_far)
    qkv_sent, grad_tokens, out_pieces, in_second, in_later = together(
        qkv_sent, grad_tokens, out_pieces, in_second, in_later
    )
    turned, out_pieces, in_keep, in_last = together(
        links.rows_turn(qkv_sent), out_pieces, in_keep, in_later[1:]
    )
    _, in_third = links.expert_far([in_keep] + list(in_last))
    d_dense = links.rows_end(turned)
    d_out = links.expert_end(out_pieces)
    d_in = links.expert_end(links.expert_pick(in_keep, in_first + in_second + in_third))
    d_qkv = d_dense[:, : 3 * WIDTH]
    d_rest = d_dense[:, 3 * WIDTH :]
    d_gain_attn = jnp.sum(d_qkv * own_qkv.astype(F32), axis=1) / gain_attn.astype(F32)
    return (
        output,
        grad_tokens,
        d_gain_attn,
        by_part(d_qkv),
        d_rest[:, :WIDTH],
        d_rest[:, WIDTH + GAIN_TWO],
        d_rest[:, WIDTH : WIDTH + EXPERTS],
        d_in,
        d_out,
    )


def solution(mesh):
    pairwise = mesh.shape["dp"] == 2 and mesh.shape["fsdp"] == 16
    links = PairwiseLinks(mesh) if pairwise else AxisLinks(mesh)
    rows = P(links.data, None)
    flat = P(links.data)
    expert = P(links.dp, links.fsdp, None)
    return jax.shard_map(
        lambda *arrays: per_device(links, *arrays),
        mesh=links.mesh,
        in_specs=(rows, flat, rows, rows, flat, rows, expert, expert, rows, rows, rows),
        out_specs=(rows, rows, flat, rows, rows, flat, rows, expert, expert),
        check_vma=False,
    )
```

```python
import math

import jax
import jax.numpy as jnp
from jax import lax
from jax.experimental import pallas as pl
from jax.experimental.pallas import tpu as pltpu
from jax.sharding import Mesh, PartitionSpec as P

HEADS = 12
HEAD_DIM = 64
EXPERTS = 8
SEQ = 576
CAP = 152
SLOTS = EXPERTS * CAP
NORM_EPSILON = 1e-06
SCALE = HEAD_DIM ** (-0.5)
PAIR = 2 * HEAD_DIM
PAIRS = HEADS // 2
WIDTH = HEADS * HEAD_DIM
LANES = 128
GAIN_ONE = EXPERTS
GAIN_TWO = EXPERTS + 1
TOKEN_BLOCK = 192
ROW_BLOCK = 304
F_BLOCK = 512
F32 = jnp.float32
BF16 = jnp.bfloat16
QUICK = pl.CostEstimate(flops=1, bytes_accessed=1, transcendentals=0)


def dot_nn(left, right):
    return jnp.dot(left, right, preferred_element_type=F32)


def dot_nt(left, right):
    return lax.dot_general(left, right, (((1,), (1,)), ((), ())), preferred_element_type=F32)


def dot_tn(left, right):
    return lax.dot_general(left, right, (((0,), (0,)), ((), ())), preferred_element_type=F32)


def scaled(values):
    return values * jnp.asarray(SCALE, BF16)


def norm_parts(values):
    centre = values - jnp.mean(values, axis=-1, keepdims=True)
    inverse = lax.rsqrt(jnp.mean(centre * centre, axis=-1, keepdims=True) + NORM_EPSILON)
    return centre * inverse, inverse


def norm_back(grad_normed, normed, inverse):
    mean_grad = jnp.mean(grad_normed, axis=-1, keepdims=True)
    mean_cross = jnp.mean(grad_normed * normed, axis=-1, keepdims=True)
    return (grad_normed - mean_grad - normed * mean_cross) * inverse


def whole(*shape):
    return pl.BlockSpec(shape, lambda *at: (0,) * len(shape))


def call(name, kernel, grid, in_specs, out_specs, out_shape, scratch=(), scalars=0):
    return pl.pallas_call(
        kernel,
        grid_spec=pltpu.PrefetchScalarGridSpec(
            num_scalar_prefetch=scalars,
            grid=grid,
            in_specs=in_specs,
            out_specs=out_specs,
            scratch_shapes=scratch,
        ),
        out_shape=out_shape,
        cost_estimate=QUICK,
        name=name,
    )


def struct(shape, dtype):
    return jax.ShapeDtypeStruct(shape, dtype)


def attention_kernel(qkv_ref, out_ref, log_ref):
    values_t = qkv_ref[:, 2 * PAIR :].T
    outs = []
    for head in range(2):
        at = head * HEAD_DIM
        queries = scaled(qkv_ref[:, at : at + HEAD_DIM])
        keys = qkv_ref[:, PAIR + at : PAIR + at + HEAD_DIM]
        scores = dot_nt(keys, queries)
        largest = jnp.max(scores, axis=0, keepdims=True)
        powers = jnp.exp(scores - largest)
        totals = jnp.sum(powers, axis=0, keepdims=True)
        mixed = dot_nn(values_t[at : at + HEAD_DIM], powers.astype(BF16))
        outs.append((mixed / totals).astype(BF16))
        log_ref[0, 0, head : head + 1, :] = largest + jnp.log(totals)
    out_ref[...] = jnp.concatenate(outs, axis=0).T


def attention_back_kernel(qkv_ref, out_ref, log_ref, grad_ref, result_ref):
    products = out_ref[...].T.astype(F32) * grad_ref[...].T.astype(F32)
    keys_t = scaled(qkv_ref[:, PAIR : 2 * PAIR]).T
    grad_queries = []
    for head in range(2):
        at = head * HEAD_DIM
        span = slice(at, at + HEAD_DIM)
        queries = scaled(qkv_ref[:, span])
        keys = qkv_ref[:, PAIR + at : PAIR + at + HEAD_DIM]
        values = qkv_ref[:, 2 * PAIR + at : 2 * PAIR + at + HEAD_DIM]
        grads = grad_ref[:, span]
        row_terms = jnp.sum(products[span], axis=0, keepdims=True)
        probs = jnp.exp(dot_nt(keys, queries) - log_ref[0, 0, head : head + 1, :])
        grad_scores = (probs * (dot_nt(values, grads) - row_terms)).astype(BF16)
        grad_values = dot_nn(probs.astype(BF16), grads)
        grad_keys = dot_nn(grad_scores, queries)
        result_ref[:, 2 * PAIR + at : 2 * PAIR + at + HEAD_DIM] = grad_values.astype(BF16)
        result_ref[:, PAIR + at : PAIR + at + HEAD_DIM] = grad_keys.astype(BF16)
        grad_queries.append(dot_nn(keys_t[span], grad_scores).astype(BF16))
    result_ref[:, :PAIR] = jnp.concatenate(grad_queries, axis=0).T


def attention_specs():
    return (
        pl.BlockSpec((SEQ, 3 * PAIR), lambda image, pair: (image, pair)),
        pl.BlockSpec((SEQ, PAIR), lambda image, pair: (image, pair)),
        pl.BlockSpec((1, 1, 2, SEQ), lambda image, pair: (image, pair, 0, 0)),
    )


def attention_forward(qkv):
    rows = qkv.shape[0]
    images = rows // SEQ
    wide, narrow, logs = attention_specs()
    return call(
        "attention_forward",
        attention_kernel,
        (images, PAIRS),
        [wide],
        [narrow, logs],
        [struct((rows, WIDTH), BF16), struct((images, PAIRS, 2, SEQ), F32)],
    )(qkv)


def attention_backward(qkv, attended, logs_saved, grad_attended):
    wide, narrow, logs = attention_specs()
    return call(
        "attention_backward",
        attention_back_kernel,
        (qkv.shape[0] // SEQ, PAIRS),
        [wide, narrow, logs, narrow],
        wide,
        struct(qkv.shape, BF16),
    )(qkv, attended, logs_saved, grad_attended)


QKV_SPEC = pl.BlockSpec((WIDTH, 3 * WIDTH), lambda *at: (0, 0))
PROJ_SPEC = pl.BlockSpec((WIDTH, WIDTH), lambda *at: (0, 3))
SMALL_SPEC = pl.BlockSpec((WIDTH, LANES), lambda *at: (0, 4 * WIDTH // LANES))


def project_kernel(tokens_ref, weight_ref, small_ref, qkv_ref, act_ref, table_ref):
    @pl.when(pl.program_id(0) == 0)
    def _():
        table = small_ref[...].T
        table_ref[...] = table
        gain = table[GAIN_ONE : GAIN_ONE + 1].astype(F32)
        normed, _ = norm_parts(tokens_ref[...].astype(F32))
        act_ref[...] = (normed * gain).astype(BF16)

    qkv_ref[...] = dot_nn(act_ref[...], weight_ref[...]).astype(BF16)


def project(tokens, dense):
    rows = tokens.shape[0]
    return call(
        "project",
        project_kernel,
        (PAIRS,),
        [
            whole(rows, WIDTH),
            pl.BlockSpec((WIDTH, 3 * PAIR), lambda pair: (0, pair)),
            SMALL_SPEC,
        ],
        [
            pl.BlockSpec((rows, 3 * PAIR), lambda pair: (0, pair)),
            whole(rows, WIDTH),
            whole(LANES, WIDTH),
        ],
        [
            struct((rows, 3 * WIDTH), BF16),
            struct((rows, WIDTH), BF16),
            struct((LANES, WIDTH), BF16),
        ],
    )(tokens, dense, dense)


def slot_hits(routes_ref, slots_ref):
    rows = routes_ref.shape[1]
    places = lax.broadcasted_iota(jnp.int32, (CAP, rows), 0)
    expert = pl.program_id(0)
    return [
        (routes_ref[k : k + 1, :] == expert) & (slots_ref[k : k + 1, :] == places)
        for k in range(2)
    ]


def middle_kernel(
    routes_ref, slots_ref, tokens_ref, attended_ref, proj_ref, table_ref,
    mid_ref, act_ref, columns_ref, gates_ref, slot_rows_ref,
):
    @pl.when(pl.program_id(0) == 0)
    def _():
        mid = tokens_ref[...].astype(F32) + dot_nn(attended_ref[...], proj_ref[...])
        mid_ref[...] = mid
        normed, _ = norm_parts(mid)
        gain = table_ref[GAIN_TWO : GAIN_TWO + 1, :].astype(F32)
        act = (normed * gain).astype(BF16)
        act_ref[...] = act
        logits = dot_nt(table_ref[:16, :], act)[:EXPERTS]
        powers = jnp.exp(logits - jnp.max(logits, axis=0, keepdims=True))
        router = powers / jnp.sum(powers, axis=0, keepdims=True)
        names = lax.broadcasted_iota(jnp.int32, router.shape, 0)
        gates = [
            jnp.sum(jnp.where(names == routes_ref[k : k + 1, :], router, 0.0), axis=0, keepdims=True)
            .astype(BF16)
            .astype(F32)
            for k in range(2)
        ]
        rows = router.shape[1]
        gates = jnp.concatenate(gates + [jnp.zeros((EXPERTS - 2, rows), F32)], axis=0)
        gates_ref[...] = gates
        spare = jnp.zeros((LANES - 2 * EXPERTS, rows), F32)
        columns_ref[...] = jnp.concatenate([router, gates, spare], axis=0).T

    first, second = slot_hits(routes_ref, slots_ref)
    dispatch = jnp.where(first | second, 1.0, 0.0).astype(BF16)
    slot_rows_ref[0] = dot_nn(dispatch, act_ref[...]).astype(BF16)


def middle(routes_t, slots_t, tokens, attended, dense, table):
    rows = tokens.shape[0]
    return call(
        "middle",
        middle_kernel,
        (EXPERTS,),
        [
            whole(2, rows),
            whole(2, rows),
            whole(rows, WIDTH),
            whole(rows, WIDTH),
            PROJ_SPEC,
            whole(LANES, WIDTH),
        ],
        [
            whole(rows, WIDTH),
            whole(rows, WIDTH),
            whole(rows, LANES),
            whole(EXPERTS, rows),
            pl.BlockSpec((1, CAP, WIDTH), lambda expert: (expert, 0, 0)),
        ],
        [
            struct((rows, WIDTH), F32),
            struct((rows, WIDTH), BF16),
            struct((rows, LANES), F32),
            struct((EXPERTS, rows), F32),
            struct((EXPERTS, CAP, WIDTH), BF16),
        ],
    )(routes_t, slots_t, tokens, attended, dense, table)


def slot_grads_kernel(routes_ref, slots_ref, gates_ref, grad_ref, result_ref):
    first, second = slot_hits(routes_ref, slots_ref)
    combine = jnp.where(first, gates_ref[0:1, :], jnp.where(second, gates_ref[1:2, :], 0.0))
    result_ref[0] = dot_nn(combine.astype(BF16), grad_ref[...]).astype(BF16)


def slot_grads(routes_t, slots_t, gates, cotangent):
    rows = cotangent.shape[0]
    return call(
        "slot_grads",
        slot_grads_kernel,
        (EXPERTS,),
        [whole(2, rows), whole(2, rows), whole(EXPERTS, rows), whole(rows, WIDTH)],
        pl.BlockSpec((1, CAP, WIDTH), lambda expert: (expert, 0, 0)),
        struct((EXPERTS, CAP, WIDTH), BF16),
    )(routes_t, slots_t, gates, cotangent)


def expert_up_kernel(rows_ref, weight_ref, hidden_ref, slope_ref):
    root = math.sqrt(2.0 / math.pi)
    value = dot_nn(rows_ref[...], weight_ref[...])
    square = value * value
    curve = jnp.tanh(value * (root + (root * 0.044715) * square))
    upper = 0.5 + 0.5 * curve
    hidden_ref[...] = (value * upper).astype(BF16)
    inner = value * (root + (3.0 * root * 0.044715) * square)
    slope_ref[...] = (upper + (0.5 - 0.5 * curve * curve) * inner).astype(BF16)


def expert_up(rows, weight):
    count, depth = rows.shape[0], weight.shape[1]
    wide = pl.BlockSpec((count, F_BLOCK), lambda f: (0, f))
    return call(
        "expert_up",
        expert_up_kernel,
        (depth // F_BLOCK,),
        [whole(count, WIDTH), pl.BlockSpec((WIDTH, F_BLOCK), lambda f: (0, f))],
        [wide, wide],
        [struct((count, depth), BF16)] * 2,
    )(rows, weight)


def expert_down_kernel(hidden_ref, weight_ref, result_ref):
    result_ref[...] = dot_nn(hidden_ref[...], weight_ref[...]).astype(BF16)


def expert_down(hidden, weight):
    count, depth = hidden.shape
    return call(
        "expert_down",
        expert_down_kernel,
        (count // ROW_BLOCK,),
        [pl.BlockSpec((ROW_BLOCK, depth), lambda r: (r, 0)), whole(depth, WIDTH)],
        pl.BlockSpec((ROW_BLOCK, WIDTH), lambda r: (r, 0)),
        struct((count, WIDTH), BF16),
    )(hidden, weight)


def expert_back_kernel(grad_ref, slope_ref, out_ref, in_ref, grad_pre_ref, grad_rows_ref):
    grad_hidden = dot_nt(grad_ref[...], out_ref[...])
    grad_pre = (grad_hidden * slope_ref[...].astype(F32)).astype(BF16)
    grad_pre_ref[...] = grad_pre
    grad_rows_ref[...] = dot_nt(grad_pre, in_ref[...]).astype(BF16)


def expert_back(grad_result, slope, weight_out, weight_in):
    count, depth = slope.shape
    wide = pl.BlockSpec((ROW_BLOCK, depth), lambda r: (r, 0))
    narrow = pl.BlockSpec((ROW_BLOCK, WIDTH), lambda r: (r, 0))
    return call(
        "expert_back",
        expert_back_kernel,
        (count // ROW_BLOCK,),
        [narrow, wide, whole(depth, WIDTH), whole(WIDTH, depth)],
        [wide, narrow],
        [struct((count, depth), BF16), struct((count, WIDTH), BF16)],
    )(grad_result, slope, weight_out, weight_in)


def out_grad_kernel(me_ref, hidden_ref, grad_ref, mine_ref, theirs_ref):
    value = dot_tn(hidden_ref[...], grad_ref[...]).astype(BF16)
    half = value.shape[0] // 2
    first = me_ref[0] == 0
    mine_ref[0, 0] = jnp.where(first, value[:half], value[half:])
    theirs_ref[0, 0] = jnp.where(first, value[half:], value[:half])


def out_grad(me, hidden, grad_result):
    count, depth = hidden.shape
    rest = depth // 16
    half = pl.BlockSpec((1, 1, rest, WIDTH), lambda f, me: (f // 4, lax.rem(f, 4), 0, 0))
    return call(
        "out_grad",
        out_grad_kernel,
        (8,),
        [pl.BlockSpec((count, 2 * rest), lambda f, me: (0, f)), whole(count, WIDTH)],
        [half, half],
        [struct((2, 4, rest, WIDTH), BF16)] * 2,
        scalars=1,
    )(me, hidden, grad_result)


def in_grad_kernel(me_ref, rows_ref, grad_ref, mine_ref, theirs_ref, turned_ref):
    @pl.when(pl.program_id(0) == 0)
    def _():
        turned_ref[...] = rows_ref[...].T

    value = dot_nn(turned_ref[...], grad_ref[...]).astype(BF16)
    value = value.reshape(8, 2, WIDTH // 16, F_BLOCK)
    first = me_ref[0] == 0
    shape = mine_ref.shape
    mine_ref[...] = jnp.where(first, value[:, 0], value[:, 1]).reshape(shape)
    theirs_ref[...] = jnp.where(first, value[:, 1], value[:, 0]).reshape(shape)


def in_grad(me, rows, grad_pre):
    count, depth = grad_pre.shape
    rest = WIDTH // 16
    half = pl.BlockSpec((2, 4, rest, F_BLOCK), lambda f, me: (0, 0, 0, f))
    return call(
        "in_grad",
        in_grad_kernel,
        (depth // F_BLOCK,),
        [whole(count, WIDTH), pl.BlockSpec((count, F_BLOCK), lambda f, me: (0, f))],
        [half, half],
        [struct((2, 4, rest, depth), BF16)] * 2,
        scratch=[pltpu.VMEM((WIDTH, count), BF16)],
        scalars=1,
    )(me, rows, grad_pre)


def token_hits(targets_ref):
    columns = lax.broadcasted_iota(jnp.int32, (targets_ref.shape[0], SLOTS), 1)
    return [targets_ref[:, k : k + 1] == columns for k in range(2)]


def combine_kernel(
    routes_ref, targets_ref, columns_ref, mid_ref, grad_ref, result_ref, output_ref, logits_ref
):
    first, second = token_hits(targets_ref)
    gates = columns_ref[:, EXPERTS : EXPERTS + 2]
    combine = jnp.where(first, gates[:, 0:1], jnp.where(second, gates[:, 1:2], 0.0)).astype(BF16)
    output_ref[...] = (mid_ref[...] + dot_nn(combine, result_ref[...])).astype(BF16)
    crossed = dot_nt(grad_ref[...], result_ref[...])
    lanes = lax.broadcasted_iota(jnp.int32, columns_ref.shape, 1)
    grad_router = jnp.zeros(columns_ref.shape, F32)
    for k, hits in enumerate((first, second)):
        grad_gate = jnp.sum(jnp.where(hits, crossed, 0.0), axis=1, keepdims=True)
        grad_router += jnp.where(lanes == routes_ref[:, k : k + 1], grad_gate, 0.0)
    router = jnp.where(lanes < EXPERTS, columns_ref[...], 0.0)
    total = jnp.sum(router * grad_router, axis=1, keepdims=True)
    logits_ref[...] = (router * (grad_router - total)).astype(BF16)


def token_spec(columns):
    return pl.BlockSpec((TOKEN_BLOCK, columns), lambda t: (t, 0))


def combine_results(routes, targets, columns, mid, cotangent, result):
    rows = mid.shape[0]
    return call(
        "combine",
        combine_kernel,
        (rows // TOKEN_BLOCK,),
        [
            token_spec(2),
            token_spec(2),
            token_spec(LANES),
            token_spec(WIDTH),
            token_spec(WIDTH),
            whole(SLOTS, WIDTH),
        ],
        [token_spec(WIDTH), token_spec(LANES)],
        [struct((rows, WIDTH), BF16), struct((rows, LANES), BF16)],
    )(routes, targets, columns, mid, cotangent, result)


def middle_back_kernel(
    targets_ref, logits_ref, mid_ref, grad_ref, rows_ref, proj_ref, table_ref,
    grad_mid_ref, low_ref, attended_ref, gain_ref,
):
    first, second = token_hits(targets_ref)
    dispatch = jnp.where(first | second, 1.0, 0.0).astype(BF16)
    grad_act = dot_nn(dispatch, rows_ref[...]) + dot_nn(logits_ref[...], table_ref[...])
    normed, inverse = norm_parts(mid_ref[...])
    gain = table_ref[GAIN_TWO : GAIN_TWO + 1, :].astype(F32)
    part = jnp.sum(grad_act * normed, axis=0, keepdims=True)

    @pl.when(pl.program_id(0) == 0)
    def _():
        gain_ref[...] = jnp.zeros_like(gain_ref)

    gain_ref[0:1, :] += part
    grad_mid = grad_ref[...].astype(F32) + norm_back(grad_act * gain, normed, inverse)
    grad_mid_ref[...] = grad_mid
    low = grad_mid.astype(BF16)
    low_ref[...] = low
    attended_ref[...] = dot_nt(low, proj_ref[...]).astype(BF16)


def middle_back(targets, logits, mid, cotangent, grad_rows, dense, table):
    rows = mid.shape[0]
    return call(
        "middle_back",
        middle_back_kernel,
        (rows // TOKEN_BLOCK,),
        [
            token_spec(2),
            token_spec(LANES),
            token_spec(WIDTH),
            token_spec(WIDTH),
            whole(SLOTS, WIDTH),
            PROJ_SPEC,
            whole(LANES, WIDTH),
        ],
        [token_spec(WIDTH), token_spec(WIDTH), token_spec(WIDTH), whole(8, WIDTH)],
        [
            struct((rows, WIDTH), F32),
            struct((rows, WIDTH), BF16),
            struct((rows, WIDTH), BF16),
            struct((8, WIDTH), F32),
        ],
    )(targets, logits, mid, cotangent, grad_rows, dense, table)


def write_halves(value, first, mine_ref, theirs_ref):
    value = value.reshape(2, 4, 2, 2, value.shape[0] // 32, value.shape[1])
    for x, y, z in ((x, y, z) for x in range(2) for y in range(2) for z in range(4)):
        low, high = value[x, z, y, 0], value[x, z, y, 1]
        mine_ref[x, y, z] = jnp.where(first, low, high).astype(BF16)
        theirs_ref[x, y, z] = jnp.where(first, high, low).astype(BF16)


def proj_grads_kernel(
    me_ref, attended_ref, low_ref, act_ref, logits_ref, gain_ref, mine_ref, theirs_ref
):
    wide = dot_tn(attended_ref[...], low_ref[...])
    small = dot_tn(act_ref[...], logits_ref[...])
    lanes = lax.broadcasted_iota(jnp.int32, small.shape, 1)
    gain = gain_ref[...].T[:, 0:1]
    value = jnp.concatenate([wide, jnp.where(lanes == GAIN_TWO, gain, small)], axis=1)
    write_halves(value, me_ref[0] == 0, mine_ref, theirs_ref)


def proj_grads(me, attended, low, act_two, logits, gain):
    rows = low.shape[0]
    half = (2, 2, 4, WIDTH // 32, WIDTH + LANES)
    return call(
        "proj_grads",
        proj_grads_kernel,
        (1,),
        [whole(rows, WIDTH)] * 3 + [whole(rows, LANES), whole(8, WIDTH)],
        [whole(*half)] * 2,
        [struct(half, BF16)] * 2,
        scalars=1,
    )(me, attended, low, act_two, logits, gain)


def qkv_grads_kernel(me_ref, act_ref, grad_ref, mine_ref, theirs_ref, turned_ref):
    @pl.when(pl.program_id(0) == 0)
    def _():
        turned_ref[...] = act_ref[...].T

    value = dot_nn(turned_ref[...], grad_ref[...])
    write_halves(value, me_ref[0] == 0, mine_ref, theirs_ref)


def qkv_grads(me, act_one, grad_qkv):
    rows = act_one.shape[0]
    half = (2, 2, 4, WIDTH // 32)
    spec = pl.BlockSpec(half + (3 * PAIR,), lambda pair, me: (0, 0, 0, 0, pair))
    return call(
        "qkv_grads",
        qkv_grads_kernel,
        (PAIRS,),
        [whole(rows, WIDTH), pl.BlockSpec((rows, 3 * PAIR), lambda pair, me: (0, pair))],
        [spec, spec],
        [struct(half + (3 * WIDTH,), BF16)] * 2,
        scratch=[pltpu.VMEM((WIDTH, rows), BF16)],
        scalars=1,
    )(me, act_one, grad_qkv)


def token_grads_kernel(grad_ref, weight_ref, tokens_ref, grad_mid_ref, table_ref, result_ref):
    grad_act = dot_nt(grad_ref[...], weight_ref[...])
    normed, inverse = norm_parts(tokens_ref[...].astype(F32))
    gain = table_ref[GAIN_ONE : GAIN_ONE + 1, :].astype(F32)
    result_ref[...] = grad_mid_ref[...] + norm_back(grad_act * gain, normed, inverse)


def token_grads(grad_qkv, dense, tokens, grad_mid, table):
    rows = tokens.shape[0]
    return call(
        "token_grads",
        token_grads_kernel,
        (rows // TOKEN_BLOCK,),
        [token_spec(3 * WIDTH), QKV_SPEC, token_spec(WIDTH), token_spec(WIDTH), whole(LANES, WIDTH)],
        token_spec(WIDTH),
        struct((rows, WIDTH), F32),
    )(grad_qkv, dense, tokens, grad_mid, table)


def by_pair(columns):
    rows = columns.shape[0]
    return columns.reshape(rows, 3, PAIRS, PAIR).transpose(0, 2, 1, 3).reshape(rows, -1)


def by_part(columns):
    rows = columns.shape[0]
    return columns.reshape(rows, PAIRS, 3, PAIR).transpose(0, 2, 1, 3).reshape(rows, -1)


def place_kernel(count, me_ref, *refs):
    pieces, result_ref = refs[:-1], refs[-1]
    at = 0
    for axis in range(count):
        at = 2 * at + lax.rem(pl.program_id(axis) + me_ref[axis], 2)
    for index, piece in enumerate(pieces):

        @pl.when(at == index)
        def _():
            result_ref[...] = piece[...].reshape(result_ref.shape)


def place(me, pieces, axes):
    count = len(axes)
    shape = list(pieces[0].shape)
    for axis in axes:
        shape.insert(axis, 2)
    block = [1 if axis in axes else size for axis, size in enumerate(shape)]

    def index(*at):
        return tuple(at[axes.index(a)] if a in axes else 0 for a in range(len(shape)))

    return call(
        "place",
        lambda *refs: place_kernel(count, *refs),
        (2,) * count,
        [whole(*piece.shape) for piece in pieces],
        pl.BlockSpec(tuple(block), index),
        struct(tuple(shape), pieces[0].dtype),
        scalars=1,
    )(me, *pieces)


def join_kernel(bounds, me_ref, near_ref, near_core_ref, *refs):
    zh, core = me_ref[0], me_ref[1]
    result_ref = refs[-1]
    result_ref[zh, 0, core] = near_ref[0]
    result_ref[zh, 0, 1 - core] = near_core_ref[0]
    for part, (begin, end) in enumerate(bounds):

        @pl.when((pl.program_id(0) >= begin) & (pl.program_id(0) < end))
        def _():
            result_ref[1 - zh, 0, core] = refs[part][0]
            result_ref[1 - zh, 0, 1 - core] = refs[len(bounds) + part][0]


def join(me, near, near_core, far, far_core):
    blocks, rest, columns = near.shape
    bounds, end = [], 0
    for part in far:
        bounds.append((end, end + part.shape[0]))
        end += part.shape[0]

    def piece(begin, end):
        return pl.BlockSpec(
            (1, rest, columns), lambda b, me: (jnp.clip(b - begin, 0, end - begin - 1), 0, 0)
        )

    return call(
        "join",
        lambda *refs: join_kernel(bounds, *refs),
        (blocks,),
        [piece(0, blocks)] * 2 + [piece(*at) for at in bounds] * 2,
        pl.BlockSpec((2, 1, 2, rest, columns), lambda b, me: (0, b, 0, 0, 0)),
        struct((2, blocks, 2, rest, columns), near.dtype),
        scalars=1,
    )(me, near, near_core, *far, *far_core).reshape(-1, columns)


def parts_of(columns):
    return 3 if columns % (3 * LANES) == 0 else 1


def columns_of(shape):
    block = tuple(shape[:-1]) + (shape[-1] // parts_of(shape[-1]),)
    return pl.BlockSpec(block, lambda i, me: (0,) * (len(shape) - 1) + (i,))


def pick_kernel(count, me_ref, *refs):
    parts, outs = refs[:-count], refs[-count:]
    places = [(ref, at) for ref in parts for at in range(ref.shape[0])]
    for place_at, (part, at) in enumerate(places):
        for k, ref in enumerate(outs):

            @pl.when((me_ref[0] ^ k) == place_at)
            def _():
                ref[...] = part[at]


def pick(me, *parts):
    count, shape = sum(part.shape[0] for part in parts), parts[0].shape[1:]
    return call(
        "pick",
        lambda *refs: pick_kernel(count, *refs),
        (parts_of(shape[-1]),),
        [columns_of(part.shape) for part in parts],
        [columns_of(shape)] * count,
        [struct(shape, BF16)] * count,
        scalars=1,
    )(me, *parts)


def pack_kernel(me_ref, *refs):
    for k, ref in enumerate(refs[:-1]):
        refs[-1][me_ref[0] ^ k] = ref[...].astype(refs[-1].dtype)


def pack(me, pieces, dtype=BF16):
    shape = (len(pieces),) + pieces[0].shape
    return call(
        "pack",
        pack_kernel,
        (parts_of(shape[-1]),),
        [columns_of(shape[1:])] * len(pieces),
        columns_of(shape),
        struct(shape, dtype),
        scalars=1,
    )(me, *pieces)


def add_halves_kernel(me_ref, mine_ref, got_ref, keep_ref, *send_refs):
    def total(at):
        return (mine_ref[at].astype(F32) + got_ref[at].astype(F32)).astype(BF16)

    keep_ref[...] = total(me_ref[0])
    send = total(1 - me_ref[0])
    begin = 0
    for ref in send_refs:
        ref[...] = send[begin : begin + ref.shape[0]]
        begin += ref.shape[0]


def add_halves(me, mine, got, counts):
    shapes = [(count,) + mine.shape[2:] for count in (mine.shape[1],) + counts]
    return call(
        "add_halves",
        add_halves_kernel,
        (parts_of(mine.shape[-1]),),
        [columns_of(mine.shape)] * 2,
        [columns_of(shape) for shape in shapes],
        [struct(shape, BF16) for shape in shapes],
        scalars=1,
    )(me, mine, got)


def add_pick_kernel(me_ref, mine_ref, *refs):
    gots, outs = refs[: -mine_ref.shape[0]], refs[-mine_ref.shape[0] :]
    got = jnp.concatenate([ref[...] for ref in gots], axis=0).astype(F32)
    for at in range(mine_ref.shape[0]):
        value = (mine_ref[at].astype(F32) + got[at]).astype(BF16)
        for k, ref in enumerate(outs):

            @pl.when((me_ref[0] ^ k) == at)
            def _():
                ref[...] = value


def add_pick(me, mine, gots):
    count, shape = mine.shape[0], mine.shape[1:]
    return call(
        "add_pick",
        add_pick_kernel,
        (parts_of(shape[-1]),),
        [columns_of(mine.shape)] + [columns_of(got.shape) for got in gots],
        [columns_of(shape)] * count,
        [struct(shape, BF16)] * count,
        scalars=1,
    )(me, mine, *gots)


def dense_pick_kernel(me_ref, *refs):
    outs = refs[-4:]
    begin = 0
    for mine_ref, got_ref in zip(refs[:-4:2], refs[1:-4:2]):
        end = begin + mine_ref.shape[-1]
        for at in range(4):
            value = (mine_ref[at].astype(F32) + got_ref[at].astype(F32)).astype(BF16)
            for k, ref in enumerate(outs):

                @pl.when((me_ref[0] ^ k) == at)
                def _():
                    ref[:, begin:end] = value

        begin = end


def dense_pick(me, pairs):
    arrays = [array.reshape(4, -1, array.shape[-1]) for pair in pairs for array in pair]
    shape = (arrays[0].shape[1], sum(array.shape[-1] for array in arrays[::2]))
    half = shape[0] // 2
    return call(
        "dense_pick",
        dense_pick_kernel,
        (2,),
        [pl.BlockSpec((4, half, array.shape[-1]), lambda i, me: (0, i, 0)) for array in arrays],
        [pl.BlockSpec((half, shape[1]), lambda i, me: (i, 0))] * 4,
        [struct(shape, BF16)] * 4,
        scalars=1,
    )(me, *arrays)


def turn_kernel(me_ref, *refs):
    outs = refs[-4:]
    total = sum(ref[...].astype(F32) for ref in refs[:-4])
    total = total.reshape(4, total.shape[0] // 4, total.shape[1])
    for at in range(4):
        value = total[at].astype(BF16)
        for k, ref in enumerate(outs):

            @pl.when((me_ref[0] ^ k) == at)
            def _():
                ref[...] = value


def turn(me, pieces):
    shape = (pieces[0].shape[0] // 4, pieces[0].shape[1])
    return call(
        "turn",
        turn_kernel,
        (1,),
        [whole(*piece.shape) for piece in pieces],
        [whole(*shape)] * 4,
        [struct(shape, BF16)] * 4,
        scalars=1,
    )(me, *pieces)


def together(*values):
    return lax.optimization_barrier(values)


def add(mine, got):
    return (mine.astype(F32) + got.astype(F32)).astype(BF16)


class PairwiseLinks:
    def __init__(self, mesh):
        self.mesh = Mesh(mesh.devices.reshape(2, 2, 2, 2, 2), ("x", "zh", "zl", "y", "c"))
        self.data = ("x", "zh", "zl", "y", "c")
        self.fsdp = ("zh", "zl", "y", "c")
        self.dp = "x"

    def swap(self, value, axis):
        return lax.ppermute(value, axis, [(0, 1), (1, 0)])

    def trade(self, value, axes):
        return lax.all_to_all(value, axes, 0, 0, tiled=True)

    def place_of(self, *axes):
        return jnp.stack([lax.axis_index(axis) for axis in axes]).astype(jnp.int32)

    def core(self):
        return self.place_of("c")

    def number(self, *axes):
        index = 0
        for axis in axes:
            index = 2 * index + lax.axis_index(axis)
        return index.astype(jnp.int32)[None]

    def moved(self, pieces, *axes):
        count = len(pieces)
        routes = [[(i, i ^ k) for i in range(count)] for k in range(count)]
        return [pieces[0]] + [lax.ppermute(pieces[k], axes, routes[k]) for k in range(1, count)]

    def gather(self, dense, w_in, w_out):
        near = self.number("zl", "y")
        own = pack(self.number("zh", "zl"), self.moved([dense] * 4, "zh", "zl"))
        in_parts, out_parts = pick(near, w_in), pick(near, w_out)
        own, first, second, third, in_parts, out_parts = together(
            own, w_in[:1], w_in[1:2], w_in[2:], in_parts, out_parts
        )
        over_y, over_x, first, second, third, in_parts = together(
            self.swap(own, "y"), self.swap(own, "x"), self.swap(first, "zh"), second, third, in_parts
        )
        firsts = [own, over_y, over_x]
        over_xy = self.swap(over_y, "x")
        second = self.swap(second, "zh")
        theirs, in_parts = together([self.swap(value, "c") for value in firsts], in_parts)
        in_near = self.moved(in_parts, "zl", "y")
        over_xy, second, third, in_near, out_parts = together(
            over_xy, second, third, in_near, out_parts
        )
        pieces = [value for pair in zip(firsts, theirs) for value in pair]
        pieces += [over_xy, self.swap(over_xy, "c")]
        third = self.swap(third, "zh")
        out_near = self.moved(out_parts, "zl", "y")
        full = place(self.place_of("x", "y", "c"), pieces, (0, 2, 3))
        full = full.reshape(32 * dense.shape[0], dense.shape[1])
        return full, {"in_near": in_near, "in_far": [first, second, third], "out_near": out_near}

    def after_project(self, kept, value):
        near = self.number("zl", "y")
        value, far, out_near = together(value, kept["in_far"], kept["out_near"])
        value, far, out_near = together(value, pick(near, *far), pack(near, out_near))
        kept["in_far"] = self.moved(far, "zl", "y")
        kept["out_near"] = out_near
        kept["out_far"] = [self.swap(out_near[:2], "zh")]
        return value

    def after_middle(self, kept, *values):
        *values, kept["in_far"], near, first = together(
            *values, kept["in_far"], kept["out_near"], kept["out_far"][0]
        )
        kept["out_near"] = near
        kept["out_far"] = [first, self.swap(near[2:3], "zh")]
        return values

    def before_grads(self, kept, *values):
        *values, near, second = together(*values, kept["out_near"], kept["out_far"][1])
        kept["out_near"] = near
        kept["out_far"] = [kept["out_far"][0], second, self.swap(near[3:], "zh")]
        return values

    def joined(self, near, far):
        cores = [self.swap(part, "c") for part in far]
        return join(self.place_of("zh", "c"), near, self.swap(near, "c"), far, cores)

    def expert_in(self, kept):
        near = self.number("zl", "y")
        return self.joined(pack(near, kept["in_near"]), [pack(near, kept["in_far"])])

    def expert_out(self, kept, *values):
        *values, last = together(*values, kept["out_far"][2])
        return *values, self.joined(kept["out_near"], kept["out_far"][:2] + [last])

    def send_slots(self, slots):
        return self.trade(slots, ("x", "zl", "y"))

    def return_slots(self, slots):
        return self.trade(slots, ("x", "zl", "y"))

    def other_core(self, theirs):
        return self.swap(theirs, "c")

    def expert_parts(self, mine, got, counts):
        return add_halves(self.place_of("zh"), mine, got, counts)

    def expert_far(self, parts):
        return parts[0], [self.swap(part, "zh") for part in parts[1:]]

    def expert_pick(self, mine, got):
        return add_pick(self.number("zl", "y"), mine, got)

    def expert_end(self, pieces):
        return pack(self.number("zl", "y"), self.moved(pieces, "zl", "y"), F32)

    def rows_pick(self, *pairs):
        return dense_pick(self.number("x", "y"), pairs)

    def rows_send(self, pieces):
        return self.moved(pieces, "x", "y")

    def rows_turn(self, pieces):
        return turn(self.number("zh", "zl"), pieces)

    def rows_end(self, pieces):
        return sum(piece.astype(F32) for piece in self.moved(pieces, "zh", "zl"))


class AxisLinks:
    def __init__(self, mesh):
        self.mesh = mesh
        self.data = ("dp", "fsdp")
        self.fsdp = "fsdp"
        self.dp = "dp"

    def core(self):
        return jnp.zeros((1,), jnp.int32)

    def gather(self, dense, w_in, w_out):
        full = lax.all_gather(dense, self.data, axis=0, tiled=True)
        return full, {"in": w_in, "out": w_out}

    def after_project(self, kept, value):
        return value

    def after_middle(self, kept, *values):
        return values

    def before_grads(self, kept, *values):
        return values

    def full_rows(self, shard):
        return lax.all_gather(shard, "fsdp", axis=1, tiled=True).reshape(-1, shard.shape[-1])

    def expert_in(self, kept):
        return self.full_rows(kept["in"])

    def expert_out(self, kept, *values):
        return *values, self.full_rows(kept["out"])

    def send_slots(self, slots):
        return lax.all_to_all(slots, "dp", 0, 0, tiled=True)

    def return_slots(self, slots):
        return lax.all_to_all(slots, "dp", 0, 0, tiled=True)

    def other_core(self, theirs):
        return theirs

    def expert_parts(self, mine, got, counts):
        return [jnp.stack([mine, got], axis=2).reshape(1, -1, mine.shape[-1])]

    def expert_far(self, parts):
        return parts[0], []

    def expert_pick(self, mine, got):
        return [mine]

    def expert_end(self, pieces):
        return lax.psum_scatter(pieces[0], "fsdp", scatter_dimension=1, tiled=True).astype(F32)

    def rows_pick(self, *pairs):
        value = jnp.concatenate([jnp.stack(pair, axis=3) for pair in pairs], axis=-1)
        value = value.transpose(0, 2, 1, 3, 4, 5)
        return [value.reshape(-1, value.shape[-1]).astype(F32)]

    def rows_send(self, pieces):
        return [lax.psum_scatter(pieces[0], self.data, scatter_dimension=0, tiled=True)]

    def rows_turn(self, pieces):
        return pieces

    def rows_end(self, pieces):
        return pieces[0]


def per_device(
    links, tokens, gain_attn, w_qkv, w_proj, gain_moe, w_router, w_in, w_out, routes, slot_ids, cotangent
):
    core = links.core()
    small = jnp.concatenate([w_router, gain_attn[:, None], gain_moe[:, None]], axis=1)
    small = jnp.pad(small, ((0, 0), (0, LANES - small.shape[1])))
    own_qkv = by_pair(w_qkv)
    dense, kept = links.gather(
        jnp.concatenate([own_qkv, w_proj, small], axis=1), w_in, w_out
    )
    routes_t = routes.T
    slots_t = slot_ids.T
    targets = jnp.where(slot_ids < CAP, routes * CAP + slot_ids, -1)

    qkv, act_one, table = project(tokens, dense)
    qkv = links.after_project(kept, qkv)
    attended, logs = attention_forward(qkv)
    mid, act_two, columns, gates, rows_sent = middle(
        routes_t, slots_t, tokens, attended, dense, table
    )
    rows_sent, gates = links.after_middle(kept, rows_sent, gates)
    slot_rows = links.send_slots(rows_sent)
    grads_sent = slot_grads(routes_t, slots_t, gates, cotangent)
    expert_in = links.expert_in(kept)
    grads_sent, slot_rows, expert_in = links.before_grads(kept, grads_sent, slot_rows, expert_in)
    grad_slots = links.send_slots(grads_sent)
    held = slot_rows.shape
    expert_rows = slot_rows.reshape(-1, WIDTH)
    hidden, slope = expert_up(expert_rows, expert_in)
    hidden, expert_out = links.expert_out(kept, hidden)
    result, grad_slots, slope = together(expert_down(hidden, expert_out), grad_slots, slope)
    flat_result = links.return_slots(result.reshape(held)).reshape(SLOTS, WIDTH)
    grad_result = grad_slots.reshape(-1, WIDTH)

    grad_pre, grad_rows = expert_back(grad_result, slope, expert_out, expert_in)
    grad_rows, grad_pre, hidden = together(grad_rows, grad_pre, hidden)
    rows_back = links.return_slots(grad_rows.reshape(held)).reshape(SLOTS, WIDTH)
    out_mine, out_theirs = out_grad(core, hidden, grad_result)
    out_theirs, grad_pre = together(out_theirs, grad_pre)
    out_got = links.other_core(out_theirs)
    in_mine, in_theirs = in_grad(core, expert_rows, grad_pre)
    in_theirs, out_got = together(in_theirs, out_got)
    in_got = links.other_core(in_theirs)
    flat_result, out_parts = together(flat_result, links.expert_parts(out_mine, out_got, (4,)))
    out_keep, out_far = links.expert_far(out_parts)
    output, grad_logits = combine_results(routes, targets, columns, mid, cotangent, flat_result)
    grad_logits, rows_back = together(grad_logits, rows_back)
    grad_mid, low, grad_attended, d_gain = middle_back(
        targets, grad_logits, mid, cotangent, rows_back, dense, table
    )
    rest_mine, rest_theirs = proj_grads(core, attended, low, act_two, grad_logits, d_gain)
    rest_theirs, grad_attended = together(rest_theirs, grad_attended)
    grad_qkv = attention_backward(qkv, attended, logs, grad_attended)
    qkv_mine, qkv_theirs = qkv_grads(core, act_one, grad_qkv)
    qkv_theirs, rest_theirs, grad_qkv, out_far, in_got = together(
        qkv_theirs, rest_theirs, grad_qkv, out_far, in_got
    )
    rest_got = links.other_core(rest_theirs)
    qkv_got = links.other_core(qkv_theirs)
    qkv_got, in_parts = together(qkv_got, links.expert_parts(in_mine, in_got, (4,)))
    qkv_parts, grad_qkv, out_keep, in_parts = together(
        links.rows_pick((qkv_mine, qkv_got), (rest_mine, rest_got)), grad_qkv, out_keep, in_parts
    )
    qkv_sent = links.rows_send(qkv_parts)
    in_keep, in_far = links.expert_far(in_parts)
    grad_tokens = token_grads(grad_qkv, dense, tokens, grad_mid, table)
    out_pieces = links.expert_pick(out_keep, out_far)
    qkv_sent, grad_tokens, out_pieces, in_far = together(
        qkv_sent, grad_tokens, out_pieces, in_far
    )
    turned, out_pieces, in_keep = together(links.rows_turn(qkv_sent), out_pieces, in_keep)
    d_dense = links.rows_end(turned)
    d_out = links.expert_end(out_pieces)
    d_in = links.expert_end(links.expert_pick(in_keep, in_far))
    d_qkv = d_dense[:, : 3 * WIDTH]
    d_rest = d_dense[:, 3 * WIDTH :]
    d_gain_attn = jnp.sum(d_qkv * own_qkv.astype(F32), axis=1) / gain_attn.astype(F32)
    return (
        output,
        grad_tokens,
        d_gain_attn,
        by_part(d_qkv),
        d_rest[:, :WIDTH],
        d_rest[:, WIDTH + GAIN_TWO],
        d_rest[:, WIDTH : WIDTH + EXPERTS],
        d_in,
        d_out,
    )


def solution(mesh):
    pairwise = mesh.shape["dp"] == 2 and mesh.shape["fsdp"] == 16
    links = PairwiseLinks(mesh) if pairwise else AxisLinks(mesh)
    rows = P(links.data, None)
    flat = P(links.data)
    expert = P(links.dp, links.fsdp, None)
    return jax.shard_map(
        lambda *arrays: per_device(links, *arrays),
        mesh=links.mesh,
        in_specs=(rows, flat, rows, rows, flat, rows, expert, expert, rows, rows, rows),
        out_specs=(rows, rows, flat, rows, rows, flat, rows, expert, expert),
        check_vma=False,
    )
```

```python
import math

import jax
import jax.numpy as jnp
from jax import lax
from jax.experimental import pallas as pl
from jax.experimental.pallas import tpu as pltpu
from jax.sharding import Mesh, PartitionSpec as P

HEADS = 12
HEAD_DIM = 64
EXPERTS = 8
SEQ = 576
CAP = 152
SLOTS = EXPERTS * CAP
NORM_EPSILON = 1e-06
SCALE = HEAD_DIM ** (-0.5)
PAIR = 2 * HEAD_DIM
PAIRS = HEADS // 2
WIDTH = HEADS * HEAD_DIM
LANES = 128
GAIN_ONE = EXPERTS
GAIN_TWO = EXPERTS + 1
TOKEN_BLOCK = 192
ROW_BLOCK = 304
F_BLOCK = 512
F32 = jnp.float32
BF16 = jnp.bfloat16
QUICK = pl.CostEstimate(flops=1, bytes_accessed=1, transcendentals=0)


def dot_nn(left, right):
    return jnp.dot(left, right, preferred_element_type=F32)


def dot_nt(left, right):
    return lax.dot_general(left, right, (((1,), (1,)), ((), ())), preferred_element_type=F32)


def dot_tn(left, right):
    return lax.dot_general(left, right, (((0,), (0,)), ((), ())), preferred_element_type=F32)


def scaled(values):
    return values * jnp.asarray(SCALE, BF16)


def norm_parts(values):
    centre = values - jnp.mean(values, axis=-1, keepdims=True)
    inverse = lax.rsqrt(jnp.mean(centre * centre, axis=-1, keepdims=True) + NORM_EPSILON)
    return centre * inverse, inverse


def norm_back(grad_normed, normed, inverse):
    mean_grad = jnp.mean(grad_normed, axis=-1, keepdims=True)
    mean_cross = jnp.mean(grad_normed * normed, axis=-1, keepdims=True)
    return (grad_normed - mean_grad - normed * mean_cross) * inverse


def whole(*shape):
    return pl.BlockSpec(shape, lambda *at: (0,) * len(shape))


def call(name, kernel, grid, in_specs, out_specs, out_shape, scratch=(), scalars=0):
    return pl.pallas_call(
        kernel,
        grid_spec=pltpu.PrefetchScalarGridSpec(
            num_scalar_prefetch=scalars,
            grid=grid,
            in_specs=in_specs,
            out_specs=out_specs,
            scratch_shapes=scratch,
        ),
        out_shape=out_shape,
        cost_estimate=QUICK,
        name=name,
    )


def struct(shape, dtype):
    return jax.ShapeDtypeStruct(shape, dtype)


def attention_kernel(qkv_ref, out_ref, log_ref):
    values_t = qkv_ref[:, 2 * PAIR :].T
    outs = []
    for head in range(2):
        at = head * HEAD_DIM
        queries = scaled(qkv_ref[:, at : at + HEAD_DIM])
        keys = qkv_ref[:, PAIR + at : PAIR + at + HEAD_DIM]
        scores = dot_nt(keys, queries)
        largest = jnp.max(scores, axis=0, keepdims=True)
        powers = jnp.exp(scores - largest)
        totals = jnp.sum(powers, axis=0, keepdims=True)
        mixed = dot_nn(values_t[at : at + HEAD_DIM], powers.astype(BF16))
        outs.append((mixed / totals).astype(BF16))
        log_ref[0, 0, head : head + 1, :] = largest + jnp.log(totals)
    out_ref[...] = jnp.concatenate(outs, axis=0).T


def attention_back_kernel(qkv_ref, out_ref, log_ref, grad_ref, result_ref):
    products = out_ref[...].T.astype(F32) * grad_ref[...].T.astype(F32)
    keys_t = scaled(qkv_ref[:, PAIR : 2 * PAIR]).T
    grad_queries = []
    for head in range(2):
        at = head * HEAD_DIM
        span = slice(at, at + HEAD_DIM)
        queries = scaled(qkv_ref[:, span])
        keys = qkv_ref[:, PAIR + at : PAIR + at + HEAD_DIM]
        values = qkv_ref[:, 2 * PAIR + at : 2 * PAIR + at + HEAD_DIM]
        grads = grad_ref[:, span]
        row_terms = jnp.sum(products[span], axis=0, keepdims=True)
        probs = jnp.exp(dot_nt(keys, queries) - log_ref[0, 0, head : head + 1, :])
        grad_scores = (probs * (dot_nt(values, grads) - row_terms)).astype(BF16)
        grad_values = dot_nn(probs.astype(BF16), grads)
        grad_keys = dot_nn(grad_scores, queries)
        result_ref[:, 2 * PAIR + at : 2 * PAIR + at + HEAD_DIM] = grad_values.astype(BF16)
        result_ref[:, PAIR + at : PAIR + at + HEAD_DIM] = grad_keys.astype(BF16)
        grad_queries.append(dot_nn(keys_t[span], grad_scores).astype(BF16))
    result_ref[:, :PAIR] = jnp.concatenate(grad_queries, axis=0).T


def attention_specs():
    return (
        pl.BlockSpec((SEQ, 3 * PAIR), lambda image, pair: (image, pair)),
        pl.BlockSpec((SEQ, PAIR), lambda image, pair: (image, pair)),
        pl.BlockSpec((1, 1, 2, SEQ), lambda image, pair: (image, pair, 0, 0)),
    )


def attention_forward(qkv):
    rows = qkv.shape[0]
    images = rows // SEQ
    wide, narrow, logs = attention_specs()
    return call(
        "attention_forward",
        attention_kernel,
        (images, PAIRS),
        [wide],
        [narrow, logs],
        [struct((rows, WIDTH), BF16), struct((images, PAIRS, 2, SEQ), F32)],
    )(qkv)


def attention_backward(qkv, attended, logs_saved, grad_attended):
    wide, narrow, logs = attention_specs()
    return call(
        "attention_backward",
        attention_back_kernel,
        (qkv.shape[0] // SEQ, PAIRS),
        [wide, narrow, logs, narrow],
        wide,
        struct(qkv.shape, BF16),
    )(qkv, attended, logs_saved, grad_attended)


QKV_SPEC = pl.BlockSpec((WIDTH, 3 * WIDTH), lambda *at: (0, 0))
PROJ_SPEC = pl.BlockSpec((WIDTH, WIDTH), lambda *at: (0, 3))
SMALL_SPEC = pl.BlockSpec((WIDTH, LANES), lambda *at: (0, 4 * WIDTH // LANES))


def project_kernel(tokens_ref, weight_ref, small_ref, qkv_ref, act_ref, table_ref):
    @pl.when(pl.program_id(0) == 0)
    def _():
        table = small_ref[...].T
        table_ref[...] = table
        gain = table[GAIN_ONE : GAIN_ONE + 1].astype(F32)
        normed, _ = norm_parts(tokens_ref[...].astype(F32))
        act_ref[...] = (normed * gain).astype(BF16)

    qkv_ref[...] = dot_nn(act_ref[...], weight_ref[...]).astype(BF16)


def project(tokens, dense):
    rows = tokens.shape[0]
    return call(
        "project",
        project_kernel,
        (PAIRS,),
        [
            whole(rows, WIDTH),
            pl.BlockSpec((WIDTH, 3 * PAIR), lambda pair: (0, pair)),
            SMALL_SPEC,
        ],
        [
            pl.BlockSpec((rows, 3 * PAIR), lambda pair: (0, pair)),
            whole(rows, WIDTH),
            whole(LANES, WIDTH),
        ],
        [
            struct((rows, 3 * WIDTH), BF16),
            struct((rows, WIDTH), BF16),
            struct((LANES, WIDTH), BF16),
        ],
    )(tokens, dense, dense)


def slot_hits(routes_ref, slots_ref):
    rows = routes_ref.shape[1]
    places = lax.broadcasted_iota(jnp.int32, (CAP, rows), 0)
    expert = pl.program_id(0)
    return [
        (routes_ref[k : k + 1, :] == expert) & (slots_ref[k : k + 1, :] == places)
        for k in range(2)
    ]


def middle_kernel(
    routes_ref, slots_ref, tokens_ref, attended_ref, proj_ref, table_ref,
    mid_ref, act_ref, columns_ref, gates_ref, slot_rows_ref,
):
    @pl.when(pl.program_id(0) == 0)
    def _():
        mid = tokens_ref[...].astype(F32) + dot_nn(attended_ref[...], proj_ref[...])
        mid_ref[...] = mid
        normed, _ = norm_parts(mid)
        gain = table_ref[GAIN_TWO : GAIN_TWO + 1, :].astype(F32)
        act = (normed * gain).astype(BF16)
        act_ref[...] = act
        logits = dot_nt(table_ref[:16, :], act)[:EXPERTS]
        powers = jnp.exp(logits - jnp.max(logits, axis=0, keepdims=True))
        router = powers / jnp.sum(powers, axis=0, keepdims=True)
        names = lax.broadcasted_iota(jnp.int32, router.shape, 0)
        gates = [
            jnp.sum(jnp.where(names == routes_ref[k : k + 1, :], router, 0.0), axis=0, keepdims=True)
            .astype(BF16)
            .astype(F32)
            for k in range(2)
        ]
        rows = router.shape[1]
        gates = jnp.concatenate(gates + [jnp.zeros((EXPERTS - 2, rows), F32)], axis=0)
        gates_ref[...] = gates
        spare = jnp.zeros((LANES - 2 * EXPERTS, rows), F32)
        columns_ref[...] = jnp.concatenate([router, gates, spare], axis=0).T

    first, second = slot_hits(routes_ref, slots_ref)
    dispatch = jnp.where(first | second, 1.0, 0.0).astype(BF16)
    slot_rows_ref[0] = dot_nn(dispatch, act_ref[...]).astype(BF16)


def middle(routes_t, slots_t, tokens, attended, dense, table):
    rows = tokens.shape[0]
    return call(
        "middle",
        middle_kernel,
        (EXPERTS,),
        [
            whole(2, rows),
            whole(2, rows),
            whole(rows, WIDTH),
            whole(rows, WIDTH),
            PROJ_SPEC,
            whole(LANES, WIDTH),
        ],
        [
            whole(rows, WIDTH),
            whole(rows, WIDTH),
            whole(rows, LANES),
            whole(EXPERTS, rows),
            pl.BlockSpec((1, CAP, WIDTH), lambda expert: (expert, 0, 0)),
        ],
        [
            struct((rows, WIDTH), F32),
            struct((rows, WIDTH), BF16),
            struct((rows, LANES), F32),
            struct((EXPERTS, rows), F32),
            struct((EXPERTS, CAP, WIDTH), BF16),
        ],
    )(routes_t, slots_t, tokens, attended, dense, table)


def slot_grads_kernel(routes_ref, slots_ref, gates_ref, grad_ref, result_ref):
    first, second = slot_hits(routes_ref, slots_ref)
    combine = jnp.where(first, gates_ref[0:1, :], jnp.where(second, gates_ref[1:2, :], 0.0))
    result_ref[0] = dot_nn(combine.astype(BF16), grad_ref[...]).astype(BF16)


def slot_grads(routes_t, slots_t, gates, cotangent):
    rows = cotangent.shape[0]
    return call(
        "slot_grads",
        slot_grads_kernel,
        (EXPERTS,),
        [whole(2, rows), whole(2, rows), whole(EXPERTS, rows), whole(rows, WIDTH)],
        pl.BlockSpec((1, CAP, WIDTH), lambda expert: (expert, 0, 0)),
        struct((EXPERTS, CAP, WIDTH), BF16),
    )(routes_t, slots_t, gates, cotangent)


def expert_up_kernel(rows_ref, weight_ref, hidden_ref, slope_ref):
    root = math.sqrt(2.0 / math.pi)
    value = dot_nn(rows_ref[...], weight_ref[...])
    square = value * value
    curve = jnp.tanh(value * (root + (root * 0.044715) * square))
    upper = 0.5 + 0.5 * curve
    hidden_ref[...] = (value * upper).astype(BF16)
    inner = value * (root + (3.0 * root * 0.044715) * square)
    slope_ref[...] = (upper + (0.5 - 0.5 * curve * curve) * inner).astype(BF16)


def expert_up(rows, weight):
    count, depth = rows.shape[0], weight.shape[1]
    wide = pl.BlockSpec((count, F_BLOCK), lambda f: (0, f))
    return call(
        "expert_up",
        expert_up_kernel,
        (depth // F_BLOCK,),
        [whole(count, WIDTH), pl.BlockSpec((WIDTH, F_BLOCK), lambda f: (0, f))],
        [wide, wide],
        [struct((count, depth), BF16)] * 2,
    )(rows, weight)


def expert_down_kernel(hidden_ref, weight_ref, result_ref):
    result_ref[...] = dot_nn(hidden_ref[...], weight_ref[...]).astype(BF16)


def expert_down(hidden, weight):
    count, depth = hidden.shape
    return call(
        "expert_down",
        expert_down_kernel,
        (count // ROW_BLOCK,),
        [pl.BlockSpec((ROW_BLOCK, depth), lambda r: (r, 0)), whole(depth, WIDTH)],
        pl.BlockSpec((ROW_BLOCK, WIDTH), lambda r: (r, 0)),
        struct((count, WIDTH), BF16),
    )(hidden, weight)


def expert_back_kernel(grad_ref, slope_ref, out_ref, in_ref, grad_pre_ref, grad_rows_ref):
    grad_hidden = dot_nt(grad_ref[...], out_ref[...])
    grad_pre = (grad_hidden * slope_ref[...].astype(F32)).astype(BF16)
    grad_pre_ref[...] = grad_pre
    grad_rows_ref[...] = dot_nt(grad_pre, in_ref[...]).astype(BF16)


def expert_back(grad_result, slope, weight_out, weight_in):
    count, depth = slope.shape
    wide = pl.BlockSpec((ROW_BLOCK, depth), lambda r: (r, 0))
    narrow = pl.BlockSpec((ROW_BLOCK, WIDTH), lambda r: (r, 0))
    return call(
        "expert_back",
        expert_back_kernel,
        (count // ROW_BLOCK,),
        [narrow, wide, whole(depth, WIDTH), whole(WIDTH, depth)],
        [wide, narrow],
        [struct((count, depth), BF16), struct((count, WIDTH), BF16)],
    )(grad_result, slope, weight_out, weight_in)


def out_grad_kernel(me_ref, hidden_ref, grad_ref, mine_ref, theirs_ref):
    value = dot_tn(hidden_ref[...], grad_ref[...]).astype(BF16)
    half = value.shape[0] // 2
    first = me_ref[0] == 0
    mine_ref[0, 0] = jnp.where(first, value[:half], value[half:])
    theirs_ref[0, 0] = jnp.where(first, value[half:], value[:half])


def out_grad(me, hidden, grad_result):
    count, depth = hidden.shape
    rest = depth // 16
    half = pl.BlockSpec((1, 1, rest, WIDTH), lambda f, me: (f // 4, lax.rem(f, 4), 0, 0))
    return call(
        "out_grad",
        out_grad_kernel,
        (8,),
        [pl.BlockSpec((count, 2 * rest), lambda f, me: (0, f)), whole(count, WIDTH)],
        [half, half],
        [struct((2, 4, rest, WIDTH), BF16)] * 2,
        scalars=1,
    )(me, hidden, grad_result)


def in_grad_kernel(me_ref, rows_ref, grad_ref, mine_ref, theirs_ref, turned_ref):
    @pl.when(pl.program_id(0) == 0)
    def _():
        turned_ref[...] = rows_ref[...].T

    value = dot_nn(turned_ref[...], grad_ref[...]).astype(BF16)
    value = value.reshape(8, 2, WIDTH // 16, F_BLOCK)
    first = me_ref[0] == 0
    shape = mine_ref.shape
    mine_ref[...] = jnp.where(first, value[:, 0], value[:, 1]).reshape(shape)
    theirs_ref[...] = jnp.where(first, value[:, 1], value[:, 0]).reshape(shape)


def in_grad(me, rows, grad_pre):
    count, depth = grad_pre.shape
    rest = WIDTH // 16
    half = pl.BlockSpec((2, 4, rest, F_BLOCK), lambda f, me: (0, 0, 0, f))
    return call(
        "in_grad",
        in_grad_kernel,
        (depth // F_BLOCK,),
        [whole(count, WIDTH), pl.BlockSpec((count, F_BLOCK), lambda f, me: (0, f))],
        [half, half],
        [struct((2, 4, rest, depth), BF16)] * 2,
        scratch=[pltpu.VMEM((WIDTH, count), BF16)],
        scalars=1,
    )(me, rows, grad_pre)


def token_hits(targets_ref):
    columns = lax.broadcasted_iota(jnp.int32, (targets_ref.shape[0], SLOTS), 1)
    return [targets_ref[:, k : k + 1] == columns for k in range(2)]


def combine_kernel(
    routes_ref, targets_ref, columns_ref, mid_ref, grad_ref, result_ref, output_ref, logits_ref
):
    first, second = token_hits(targets_ref)
    gates = columns_ref[:, EXPERTS : EXPERTS + 2]
    combine = jnp.where(first, gates[:, 0:1], jnp.where(second, gates[:, 1:2], 0.0)).astype(BF16)
    output_ref[...] = (mid_ref[...] + dot_nn(combine, result_ref[...])).astype(BF16)
    crossed = dot_nt(grad_ref[...], result_ref[...])
    lanes = lax.broadcasted_iota(jnp.int32, columns_ref.shape, 1)
    grad_router = jnp.zeros(columns_ref.shape, F32)
    for k, hits in enumerate((first, second)):
        grad_gate = jnp.sum(jnp.where(hits, crossed, 0.0), axis=1, keepdims=True)
        grad_router += jnp.where(lanes == routes_ref[:, k : k + 1], grad_gate, 0.0)
    router = jnp.where(lanes < EXPERTS, columns_ref[...], 0.0)
    total = jnp.sum(router * grad_router, axis=1, keepdims=True)
    logits_ref[...] = (router * (grad_router - total)).astype(BF16)


def token_spec(columns):
    return pl.BlockSpec((TOKEN_BLOCK, columns), lambda t: (t, 0))


def combine_results(routes, targets, columns, mid, cotangent, result):
    rows = mid.shape[0]
    return call(
        "combine",
        combine_kernel,
        (rows // TOKEN_BLOCK,),
        [
            token_spec(2),
            token_spec(2),
            token_spec(LANES),
            token_spec(WIDTH),
            token_spec(WIDTH),
            whole(SLOTS, WIDTH),
        ],
        [token_spec(WIDTH), token_spec(LANES)],
        [struct((rows, WIDTH), BF16), struct((rows, LANES), BF16)],
    )(routes, targets, columns, mid, cotangent, result)


def middle_back_kernel(
    targets_ref, logits_ref, mid_ref, grad_ref, rows_ref, proj_ref, table_ref,
    grad_mid_ref, low_ref, attended_ref, gain_ref,
):
    first, second = token_hits(targets_ref)
    dispatch = jnp.where(first | second, 1.0, 0.0).astype(BF16)
    grad_act = dot_nn(dispatch, rows_ref[...]) + dot_nn(logits_ref[...], table_ref[...])
    normed, inverse = norm_parts(mid_ref[...])
    gain = table_ref[GAIN_TWO : GAIN_TWO + 1, :].astype(F32)
    part = jnp.sum(grad_act * normed, axis=0, keepdims=True)

    @pl.when(pl.program_id(0) == 0)
    def _():
        gain_ref[...] = jnp.zeros_like(gain_ref)

    gain_ref[0:1, :] += part
    grad_mid = grad_ref[...].astype(F32) + norm_back(grad_act * gain, normed, inverse)
    grad_mid_ref[...] = grad_mid
    low = grad_mid.astype(BF16)
    low_ref[...] = low
    attended_ref[...] = dot_nt(low, proj_ref[...]).astype(BF16)


def middle_back(targets, logits, mid, cotangent, grad_rows, dense, table):
    rows = mid.shape[0]
    return call(
        "middle_back",
        middle_back_kernel,
        (rows // TOKEN_BLOCK,),
        [
            token_spec(2),
            token_spec(LANES),
            token_spec(WIDTH),
            token_spec(WIDTH),
            whole(SLOTS, WIDTH),
            PROJ_SPEC,
            whole(LANES, WIDTH),
        ],
        [token_spec(WIDTH), token_spec(WIDTH), token_spec(WIDTH), whole(8, WIDTH)],
        [
            struct((rows, WIDTH), F32),
            struct((rows, WIDTH), BF16),
            struct((rows, WIDTH), BF16),
            struct((8, WIDTH), F32),
        ],
    )(targets, logits, mid, cotangent, grad_rows, dense, table)


def write_halves(value, first, mine_ref, theirs_ref):
    value = value.reshape(2, 4, 2, 2, value.shape[0] // 32, value.shape[1])
    for x, y, z in ((x, y, z) for x in range(2) for y in range(2) for z in range(4)):
        low, high = value[x, z, y, 0], value[x, z, y, 1]
        mine_ref[x, y, z] = jnp.where(first, low, high).astype(BF16)
        theirs_ref[x, y, z] = jnp.where(first, high, low).astype(BF16)


def proj_grads_kernel(
    me_ref, attended_ref, low_ref, act_ref, logits_ref, gain_ref, mine_ref, theirs_ref
):
    wide = dot_tn(attended_ref[...], low_ref[...])
    small = dot_tn(act_ref[...], logits_ref[...])
    lanes = lax.broadcasted_iota(jnp.int32, small.shape, 1)
    gain = gain_ref[...].T[:, 0:1]
    value = jnp.concatenate([wide, jnp.where(lanes == GAIN_TWO, gain, small)], axis=1)
    write_halves(value, me_ref[0] == 0, mine_ref, theirs_ref)


def proj_grads(me, attended, low, act_two, logits, gain):
    rows = low.shape[0]
    half = (2, 2, 4, WIDTH // 32, WIDTH + LANES)
    return call(
        "proj_grads",
        proj_grads_kernel,
        (1,),
        [whole(rows, WIDTH)] * 3 + [whole(rows, LANES), whole(8, WIDTH)],
        [whole(*half)] * 2,
        [struct(half, BF16)] * 2,
        scalars=1,
    )(me, attended, low, act_two, logits, gain)


def qkv_grads_kernel(me_ref, act_ref, grad_ref, mine_ref, theirs_ref, turned_ref):
    @pl.when(pl.program_id(0) == 0)
    def _():
        turned_ref[...] = act_ref[...].T

    value = dot_nn(turned_ref[...], grad_ref[...])
    write_halves(value, me_ref[0] == 0, mine_ref, theirs_ref)


def qkv_grads(me, act_one, grad_qkv):
    rows = act_one.shape[0]
    half = (2, 2, 4, WIDTH // 32)
    spec = pl.BlockSpec(half + (3 * PAIR,), lambda pair, me: (0, 0, 0, 0, pair))
    return call(
        "qkv_grads",
        qkv_grads_kernel,
        (PAIRS,),
        [whole(rows, WIDTH), pl.BlockSpec((rows, 3 * PAIR), lambda pair, me: (0, pair))],
        [spec, spec],
        [struct(half + (3 * WIDTH,), BF16)] * 2,
        scratch=[pltpu.VMEM((WIDTH, rows), BF16)],
        scalars=1,
    )(me, act_one, grad_qkv)


def token_grads_kernel(grad_ref, weight_ref, tokens_ref, grad_mid_ref, table_ref, result_ref):
    grad_act = dot_nt(grad_ref[...], weight_ref[...])
    normed, inverse = norm_parts(tokens_ref[...].astype(F32))
    gain = table_ref[GAIN_ONE : GAIN_ONE + 1, :].astype(F32)
    result_ref[...] = grad_mid_ref[...] + norm_back(grad_act * gain, normed, inverse)


def token_grads(grad_qkv, dense, tokens, grad_mid, table):
    rows = tokens.shape[0]
    return call(
        "token_grads",
        token_grads_kernel,
        (rows // TOKEN_BLOCK,),
        [token_spec(3 * WIDTH), QKV_SPEC, token_spec(WIDTH), token_spec(WIDTH), whole(LANES, WIDTH)],
        token_spec(WIDTH),
        struct((rows, WIDTH), F32),
    )(grad_qkv, dense, tokens, grad_mid, table)


def by_pair(columns):
    rows = columns.shape[0]
    return columns.reshape(rows, 3, PAIRS, PAIR).transpose(0, 2, 1, 3).reshape(rows, -1)


def by_part(columns):
    rows = columns.shape[0]
    return columns.reshape(rows, PAIRS, 3, PAIR).transpose(0, 2, 1, 3).reshape(rows, -1)


def place_kernel(count, me_ref, *refs):
    pieces, result_ref = refs[:-1], refs[-1]
    at = 0
    for axis in range(count):
        at = 2 * at + lax.rem(pl.program_id(axis) + me_ref[axis], 2)
    for index, piece in enumerate(pieces):

        @pl.when(at == index)
        def _():
            result_ref[...] = piece[...].reshape(result_ref.shape)


def place(me, pieces, axes):
    count = len(axes)
    shape = list(pieces[0].shape)
    for axis in axes:
        shape.insert(axis, 2)
    block = [1 if axis in axes else size for axis, size in enumerate(shape)]

    def index(*at):
        return tuple(at[axes.index(a)] if a in axes else 0 for a in range(len(shape)))

    return call(
        "place",
        lambda *refs: place_kernel(count, *refs),
        (2,) * count,
        [whole(*piece.shape) for piece in pieces],
        pl.BlockSpec(tuple(block), index),
        struct(tuple(shape), pieces[0].dtype),
        scalars=1,
    )(me, *pieces)


def join_kernel(bounds, me_ref, near_ref, near_core_ref, *refs):
    zh, core = me_ref[0], me_ref[1]
    result_ref = refs[-1]
    result_ref[zh, 0, core] = near_ref[0]
    result_ref[zh, 0, 1 - core] = near_core_ref[0]
    for part, (begin, end) in enumerate(bounds):

        @pl.when((pl.program_id(0) >= begin) & (pl.program_id(0) < end))
        def _():
            result_ref[1 - zh, 0, core] = refs[part][0]
            result_ref[1 - zh, 0, 1 - core] = refs[len(bounds) + part][0]


def join(me, near, near_core, far, far_core):
    blocks, rest, columns = near.shape
    bounds, end = [], 0
    for part in far:
        bounds.append((end, end + part.shape[0]))
        end += part.shape[0]

    def piece(begin, end):
        return pl.BlockSpec(
            (1, rest, columns), lambda b, me: (jnp.clip(b - begin, 0, end - begin - 1), 0, 0)
        )

    return call(
        "join",
        lambda *refs: join_kernel(bounds, *refs),
        (blocks,),
        [piece(0, blocks)] * 2 + [piece(*at) for at in bounds] * 2,
        pl.BlockSpec((2, 1, 2, rest, columns), lambda b, me: (0, b, 0, 0, 0)),
        struct((2, blocks, 2, rest, columns), near.dtype),
        scalars=1,
    )(me, near, near_core, *far, *far_core).reshape(-1, columns)


def parts_of(columns):
    return 3 if columns % (3 * LANES) == 0 else 1


def columns_of(shape):
    block = tuple(shape[:-1]) + (shape[-1] // parts_of(shape[-1]),)
    return pl.BlockSpec(block, lambda i, me: (0,) * (len(shape) - 1) + (i,))


def pick_kernel(count, me_ref, *refs):
    parts, outs = refs[:-count], refs[-count:]
    places = [(ref, at) for ref in parts for at in range(ref.shape[0])]
    for place_at, (part, at) in enumerate(places):
        for k, ref in enumerate(outs):

            @pl.when((me_ref[0] ^ k) == place_at)
            def _():
                ref[...] = part[at]


def pick(me, *parts):
    count, shape = sum(part.shape[0] for part in parts), parts[0].shape[1:]
    return call(
        "pick",
        lambda *refs: pick_kernel(count, *refs),
        (parts_of(shape[-1]),),
        [columns_of(part.shape) for part in parts],
        [columns_of(shape)] * count,
        [struct(shape, BF16)] * count,
        scalars=1,
    )(me, *parts)


def pack_kernel(me_ref, *refs):
    for k, ref in enumerate(refs[:-1]):
        refs[-1][me_ref[0] ^ k] = ref[...].astype(refs[-1].dtype)


def pack(me, pieces, dtype=BF16):
    shape = (len(pieces),) + pieces[0].shape
    return call(
        "pack",
        pack_kernel,
        (parts_of(shape[-1]),),
        [columns_of(shape[1:])] * len(pieces),
        columns_of(shape),
        struct(shape, dtype),
        scalars=1,
    )(me, *pieces)


def add_halves_kernel(me_ref, mine_ref, got_ref, keep_ref, *send_refs):
    def total(at):
        return (mine_ref[at].astype(F32) + got_ref[at].astype(F32)).astype(BF16)

    keep_ref[...] = total(me_ref[0])
    send = total(1 - me_ref[0])
    begin = 0
    for ref in send_refs:
        ref[...] = send[begin : begin + ref.shape[0]]
        begin += ref.shape[0]


def add_halves(me, mine, got, counts):
    shapes = [(count,) + mine.shape[2:] for count in (mine.shape[1],) + counts]
    return call(
        "add_halves",
        add_halves_kernel,
        (parts_of(mine.shape[-1]),),
        [columns_of(mine.shape)] * 2,
        [columns_of(shape) for shape in shapes],
        [struct(shape, BF16) for shape in shapes],
        scalars=1,
    )(me, mine, got)


def add_pick_kernel(me_ref, mine_ref, *refs):
    gots, outs = refs[: -mine_ref.shape[0]], refs[-mine_ref.shape[0] :]
    got = jnp.concatenate([ref[...] for ref in gots], axis=0).astype(F32)
    for at in range(mine_ref.shape[0]):
        value = (mine_ref[at].astype(F32) + got[at]).astype(BF16)
        for k, ref in enumerate(outs):

            @pl.when((me_ref[0] ^ k) == at)
            def _():
                ref[...] = value


def add_pick(me, mine, gots):
    count, shape = mine.shape[0], mine.shape[1:]
    return call(
        "add_pick",
        add_pick_kernel,
        (parts_of(shape[-1]),),
        [columns_of(mine.shape)] + [columns_of(got.shape) for got in gots],
        [columns_of(shape)] * count,
        [struct(shape, BF16)] * count,
        scalars=1,
    )(me, mine, *gots)


def dense_pick_kernel(me_ref, *refs):
    outs = refs[-4:]
    begin = 0
    for mine_ref, got_ref in zip(refs[:-4:2], refs[1:-4:2]):
        end = begin + mine_ref.shape[-1]
        for at in range(4):
            value = (mine_ref[at].astype(F32) + got_ref[at].astype(F32)).astype(BF16)
            for k, ref in enumerate(outs):

                @pl.when((me_ref[0] ^ k) == at)
                def _():
                    ref[:, begin:end] = value

        begin = end


def dense_pick(me, pairs):
    arrays = [array.reshape(4, -1, array.shape[-1]) for pair in pairs for array in pair]
    shape = (arrays[0].shape[1], sum(array.shape[-1] for array in arrays[::2]))
    half = shape[0] // 2
    return call(
        "dense_pick",
        dense_pick_kernel,
        (2,),
        [pl.BlockSpec((4, half, array.shape[-1]), lambda i, me: (0, i, 0)) for array in arrays],
        [pl.BlockSpec((half, shape[1]), lambda i, me: (i, 0))] * 4,
        [struct(shape, BF16)] * 4,
        scalars=1,
    )(me, *arrays)


def turn_kernel(me_ref, *refs):
    outs = refs[-4:]
    total = sum(ref[...].astype(F32) for ref in refs[:-4])
    total = total.reshape(4, total.shape[0] // 4, total.shape[1])
    for at in range(4):
        value = total[at].astype(BF16)
        for k, ref in enumerate(outs):

            @pl.when((me_ref[0] ^ k) == at)
            def _():
                ref[...] = value


def turn(me, pieces):
    shape = (pieces[0].shape[0] // 4, pieces[0].shape[1])
    return call(
        "turn",
        turn_kernel,
        (1,),
        [whole(*piece.shape) for piece in pieces],
        [whole(*shape)] * 4,
        [struct(shape, BF16)] * 4,
        scalars=1,
    )(me, *pieces)


def together(*values):
    return lax.optimization_barrier(values)


def add(mine, got):
    return (mine.astype(F32) + got.astype(F32)).astype(BF16)


class PairwiseLinks:
    def __init__(self, mesh):
        self.mesh = Mesh(mesh.devices.reshape(2, 2, 2, 2, 2), ("x", "zh", "zl", "y", "c"))
        self.data = ("x", "zh", "zl", "y", "c")
        self.fsdp = ("zh", "zl", "y", "c")
        self.dp = "x"

    def swap(self, value, axis):
        return lax.ppermute(value, axis, [(0, 1), (1, 0)])

    def trade(self, value, axes):
        return lax.all_to_all(value, axes, 0, 0, tiled=True)

    def place_of(self, *axes):
        return jnp.stack([lax.axis_index(axis) for axis in axes]).astype(jnp.int32)

    def core(self):
        return self.place_of("c")

    def number(self, *axes):
        index = 0
        for axis in axes:
            index = 2 * index + lax.axis_index(axis)
        return index.astype(jnp.int32)[None]

    def moved(self, pieces, *axes):
        count = len(pieces)
        routes = [[(i, i ^ k) for i in range(count)] for k in range(count)]
        return [pieces[0]] + [lax.ppermute(pieces[k], axes, routes[k]) for k in range(1, count)]

    def gather(self, dense, w_in, w_out):
        near = ("zl", "y")
        own = pack(self.number("zh", "zl"), self.moved([dense] * 4, "zh", "zl"))
        own, first, second, third, w_in, w_out = together(
            own, w_in[:1], w_in[1:3], w_in[3:], w_in, w_out
        )
        over_y, over_x, first, second, third, w_in = together(
            self.swap(own, "y"), self.swap(own, "x"), self.swap(first, "zh"), second, third, w_in
        )
        firsts = [own, over_y, over_x]
        over_xy = self.swap(over_y, "x")
        second = self.swap(second, "zh")
        in_near = self.trade(w_in, near)
        theirs = [self.swap(value, "c") for value in firsts]
        over_xy, second, third, in_near, w_out = together(over_xy, second, third, in_near, w_out)
        pieces = [value for pair in zip(firsts, theirs) for value in pair]
        pieces += [over_xy, self.swap(over_xy, "c")]
        third = self.swap(third, "zh")
        out_near = self.trade(w_out, near)
        full = place(self.place_of("x", "y", "c"), pieces, (0, 2, 3))
        full = full.reshape(32 * dense.shape[0], dense.shape[1])
        return full, {"in_near": in_near, "in_far": [first, second, third], "out_near": out_near}

    def after_project(self, kept, value):
        value, far, out_near = together(value, kept["in_far"], kept["out_near"])
        kept["in_far"] = self.trade(jnp.concatenate(far, axis=0), ("zl", "y"))
        kept["out_near"] = out_near
        kept["out_far"] = [self.swap(out_near[:2], "zh")]
        return value

    def after_middle(self, kept, *values):
        *values, kept["in_far"], near, first = together(
            *values, kept["in_far"], kept["out_near"], kept["out_far"][0]
        )
        kept["out_near"] = near
        kept["out_far"] = [first, self.swap(near[2:3], "zh")]
        return values

    def before_grads(self, kept, *values):
        *values, near, second = together(*values, kept["out_near"], kept["out_far"][1])
        kept["out_near"] = near
        kept["out_far"] = [kept["out_far"][0], second, self.swap(near[3:], "zh")]
        return values

    def joined(self, near, far):
        cores = [self.swap(part, "c") for part in far]
        return join(self.place_of("zh", "c"), near, self.swap(near, "c"), far, cores)

    def expert_in(self, kept):
        return self.joined(kept["in_near"], [kept["in_far"]])

    def expert_out(self, kept, *values):
        *values, last = together(*values, kept["out_far"][2])
        return *values, self.joined(kept["out_near"], kept["out_far"][:2] + [last])

    def send_slots(self, slots):
        return self.trade(slots, ("x", "zl", "y"))

    def return_slots(self, slots):
        return self.trade(slots, ("x", "zl", "y"))

    def other_core(self, theirs):
        return self.swap(theirs, "c")

    def expert_parts(self, mine, got, counts):
        return add_halves(self.place_of("zh"), mine, got, counts)

    def expert_far(self, parts):
        return parts[0], [self.swap(part, "zh") for part in parts[1:]]

    def expert_pick(self, mine, got):
        return add_pick(self.number("zl", "y"), mine, got)

    def expert_end(self, pieces):
        return pack(self.number("zl", "y"), self.moved(pieces, "zl", "y"), F32)

    def rows_pick(self, *pairs):
        return dense_pick(self.number("x", "y"), pairs)

    def rows_send(self, pieces):
        return self.moved(pieces, "x", "y")

    def rows_turn(self, pieces):
        return turn(self.number("zh", "zl"), pieces)

    def rows_end(self, pieces):
        return sum(piece.astype(F32) for piece in self.moved(pieces, "zh", "zl"))


class AxisLinks:
    def __init__(self, mesh):
        self.mesh = mesh
        self.data = ("dp", "fsdp")
        self.fsdp = "fsdp"
        self.dp = "dp"

    def core(self):
        return jnp.zeros((1,), jnp.int32)

    def gather(self, dense, w_in, w_out):
        full = lax.all_gather(dense, self.data, axis=0, tiled=True)
        return full, {"in": w_in, "out": w_out}

    def after_project(self, kept, value):
        return value

    def after_middle(self, kept, *values):
        return values

    def before_grads(self, kept, *values):
        return values

    def full_rows(self, shard):
        return lax.all_gather(shard, "fsdp", axis=1, tiled=True).reshape(-1, shard.shape[-1])

    def expert_in(self, kept):
        return self.full_rows(kept["in"])

    def expert_out(self, kept, *values):
        return *values, self.full_rows(kept["out"])

    def send_slots(self, slots):
        return lax.all_to_all(slots, "dp", 0, 0, tiled=True)

    def return_slots(self, slots):
        return lax.all_to_all(slots, "dp", 0, 0, tiled=True)

    def other_core(self, theirs):
        return theirs

    def expert_parts(self, mine, got, counts):
        return [jnp.stack([mine, got], axis=2).reshape(1, -1, mine.shape[-1])]

    def expert_far(self, parts):
        return parts[0], []

    def expert_pick(self, mine, got):
        return [mine]

    def expert_end(self, pieces):
        return lax.psum_scatter(pieces[0], "fsdp", scatter_dimension=1, tiled=True).astype(F32)

    def rows_pick(self, *pairs):
        value = jnp.concatenate([jnp.stack(pair, axis=3) for pair in pairs], axis=-1)
        value = value.transpose(0, 2, 1, 3, 4, 5)
        return [value.reshape(-1, value.shape[-1]).astype(F32)]

    def rows_send(self, pieces):
        return [lax.psum_scatter(pieces[0], self.data, scatter_dimension=0, tiled=True)]

    def rows_turn(self, pieces):
        return pieces

    def rows_end(self, pieces):
        return pieces[0]


def per_device(
    links, tokens, gain_attn, w_qkv, w_proj, gain_moe, w_router, w_in, w_out, routes, slot_ids, cotangent
):
    core = links.core()
    small = jnp.concatenate([w_router, gain_attn[:, None], gain_moe[:, None]], axis=1)
    small = jnp.pad(small, ((0, 0), (0, LANES - small.shape[1])))
    own_qkv = by_pair(w_qkv)
    dense, kept = links.gather(
        jnp.concatenate([own_qkv, w_proj, small], axis=1), w_in, w_out
    )
    routes_t = routes.T
    slots_t = slot_ids.T
    targets = jnp.where(slot_ids < CAP, routes * CAP + slot_ids, -1)

    qkv, act_one, table = project(tokens, dense)
    qkv = links.after_project(kept, qkv)
    attended, logs = attention_forward(qkv)
    mid, act_two, columns, gates, rows_sent = middle(
        routes_t, slots_t, tokens, attended, dense, table
    )
    rows_sent, gates = links.after_middle(kept, rows_sent, gates)
    slot_rows = links.send_slots(rows_sent)
    grads_sent = slot_grads(routes_t, slots_t, gates, cotangent)
    expert_in = links.expert_in(kept)
    grads_sent, slot_rows, expert_in = links.before_grads(kept, grads_sent, slot_rows, expert_in)
    grad_slots = links.send_slots(grads_sent)
    held = slot_rows.shape
    expert_rows = slot_rows.reshape(-1, WIDTH)
    hidden, slope = expert_up(expert_rows, expert_in)
    hidden, expert_out = links.expert_out(kept, hidden)
    result, grad_slots, slope = together(expert_down(hidden, expert_out), grad_slots, slope)
    flat_result = links.return_slots(result.reshape(held)).reshape(SLOTS, WIDTH)
    grad_result = grad_slots.reshape(-1, WIDTH)

    grad_pre, grad_rows = expert_back(grad_result, slope, expert_out, expert_in)
    grad_rows, grad_pre, hidden = together(grad_rows, grad_pre, hidden)
    rows_back = links.return_slots(grad_rows.reshape(held)).reshape(SLOTS, WIDTH)
    out_mine, out_theirs = out_grad(core, hidden, grad_result)
    out_theirs, grad_pre = together(out_theirs, grad_pre)
    out_got = links.other_core(out_theirs)
    in_mine, in_theirs = in_grad(core, expert_rows, grad_pre)
    in_theirs, out_got = together(in_theirs, out_got)
    in_got = links.other_core(in_theirs)
    flat_result, out_parts = together(flat_result, links.expert_parts(out_mine, out_got, (4,)))
    out_keep, out_far = links.expert_far(out_parts)
    output, grad_logits = combine_results(routes, targets, columns, mid, cotangent, flat_result)
    grad_logits, rows_back = together(grad_logits, rows_back)
    grad_mid, low, grad_attended, d_gain = middle_back(
        targets, grad_logits, mid, cotangent, rows_back, dense, table
    )
    rest_mine, rest_theirs = proj_grads(core, attended, low, act_two, grad_logits, d_gain)
    rest_theirs, grad_attended, in_got = together(rest_theirs, grad_attended, in_got)
    in_parts, grad_attended = together(
        links.expert_parts(in_mine, in_got, (1, 3)), grad_attended
    )
    grad_qkv = attention_backward(qkv, attended, logs, grad_attended)
    qkv_mine, qkv_theirs = qkv_grads(core, act_one, grad_qkv)
    qkv_theirs, rest_theirs, grad_qkv, out_far, in_parts = together(
        qkv_theirs, rest_theirs, grad_qkv, out_far, in_parts
    )
    in_keep, in_first = links.expert_far(in_parts[:2])
    rest_got = links.other_core(rest_theirs)
    qkv_got = links.other_core(qkv_theirs)
    qkv_got, rest_got, in_first, in_later = together(qkv_got, rest_got, in_first, in_parts[2:])
    qkv_parts, grad_qkv, out_keep, in_later = together(
        links.rows_pick((qkv_mine, qkv_got), (rest_mine, rest_got)), grad_qkv, out_keep, in_later
    )
    qkv_sent = links.rows_send(qkv_parts)
    _, in_second = links.expert_far([in_keep] + list(in_later))
    grad_tokens = token_grads(grad_qkv, dense, tokens, grad_mid, table)
    out_pieces = links.expert_pick(out_keep, out_far)
    qkv_sent, grad_tokens, out_pieces = together(qkv_sent, grad_tokens, out_pieces)
    turned, out_pieces, in_keep, in_second = together(
        links.rows_turn(qkv_sent), out_pieces, in_keep, in_second
    )
    d_dense = links.rows_end(turned)
    d_out = links.expert_end(out_pieces)
    d_in = links.expert_end(links.expert_pick(in_keep, in_first + in_second))
    d_qkv = d_dense[:, : 3 * WIDTH]
    d_rest = d_dense[:, 3 * WIDTH :]
    d_gain_attn = jnp.sum(d_qkv * own_qkv.astype(F32), axis=1) / gain_attn.astype(F32)
    return (
        output,
        grad_tokens,
        d_gain_attn,
        by_part(d_qkv),
        d_rest[:, :WIDTH],
        d_rest[:, WIDTH + GAIN_TWO],
        d_rest[:, WIDTH : WIDTH + EXPERTS],
        d_in,
        d_out,
    )


def solution(mesh):
    pairwise = mesh.shape["dp"] == 2 and mesh.shape["fsdp"] == 16
    links = PairwiseLinks(mesh) if pairwise else AxisLinks(mesh)
    rows = P(links.data, None)
    flat = P(links.data)
    expert = P(links.dp, links.fsdp, None)
    return jax.shard_map(
        lambda *arrays: per_device(links, *arrays),
        mesh=links.mesh,
        in_specs=(rows, flat, rows, rows, flat, rows, expert, expert, rows, rows, rows),
        out_specs=(rows, rows, flat, rows, rows, flat, rows, expert, expert),
        check_vma=False,
    )
```

```python
import math

import jax
import jax.numpy as jnp
from jax import lax
from jax.experimental import pallas as pl
from jax.experimental.pallas import tpu as pltpu
from jax.sharding import Mesh, PartitionSpec as P

HEADS = 12
HEAD_DIM = 64
EXPERTS = 8
SEQ = 576
CAP = 152
SLOTS = EXPERTS * CAP
NORM_EPSILON = 1e-06
SCALE = HEAD_DIM ** (-0.5)
PAIR = 2 * HEAD_DIM
PAIRS = HEADS // 2
WIDTH = HEADS * HEAD_DIM
LANES = 128
GAIN_ONE = EXPERTS
GAIN_TWO = EXPERTS + 1
TOKEN_BLOCK = 192
ROW_BLOCK = 304
F_BLOCK = 512
F32 = jnp.float32
BF16 = jnp.bfloat16
QUICK = pl.CostEstimate(flops=1, bytes_accessed=1, transcendentals=0)


def dot_nn(left, right):
    return jnp.dot(left, right, preferred_element_type=F32)


def dot_nt(left, right):
    return lax.dot_general(left, right, (((1,), (1,)), ((), ())), preferred_element_type=F32)


def dot_tn(left, right):
    return lax.dot_general(left, right, (((0,), (0,)), ((), ())), preferred_element_type=F32)


def scaled(values):
    return values * jnp.asarray(SCALE, BF16)


def norm_parts(values):
    centre = values - jnp.mean(values, axis=-1, keepdims=True)
    inverse = lax.rsqrt(jnp.mean(centre * centre, axis=-1, keepdims=True) + NORM_EPSILON)
    return centre * inverse, inverse


def norm_back(grad_normed, normed, inverse):
    mean_grad = jnp.mean(grad_normed, axis=-1, keepdims=True)
    mean_cross = jnp.mean(grad_normed * normed, axis=-1, keepdims=True)
    return (grad_normed - mean_grad - normed * mean_cross) * inverse


def whole(*shape):
    return pl.BlockSpec(shape, lambda *at: (0,) * len(shape))


def call(name, kernel, grid, in_specs, out_specs, out_shape, scratch=(), scalars=0):
    return pl.pallas_call(
        kernel,
        grid_spec=pltpu.PrefetchScalarGridSpec(
            num_scalar_prefetch=scalars,
            grid=grid,
            in_specs=in_specs,
            out_specs=out_specs,
            scratch_shapes=scratch,
        ),
        out_shape=out_shape,
        cost_estimate=QUICK,
        name=name,
    )


def struct(shape, dtype):
    return jax.ShapeDtypeStruct(shape, dtype)


def attention_kernel(qkv_ref, out_ref, log_ref):
    values_t = qkv_ref[:, 2 * PAIR :].T
    outs = []
    for head in range(2):
        at = head * HEAD_DIM
        queries = scaled(qkv_ref[:, at : at + HEAD_DIM])
        keys = qkv_ref[:, PAIR + at : PAIR + at + HEAD_DIM]
        scores = dot_nt(keys, queries)
        largest = jnp.max(scores, axis=0, keepdims=True)
        powers = jnp.exp(scores - largest)
        totals = jnp.sum(powers, axis=0, keepdims=True)
        mixed = dot_nn(values_t[at : at + HEAD_DIM], powers.astype(BF16))
        outs.append((mixed / totals).astype(BF16))
        log_ref[0, 0, head : head + 1, :] = largest + jnp.log(totals)
    out_ref[...] = jnp.concatenate(outs, axis=0).T


def attention_back_kernel(qkv_ref, out_ref, log_ref, grad_ref, result_ref):
    products = out_ref[...].T.astype(F32) * grad_ref[...].T.astype(F32)
    keys_t = scaled(qkv_ref[:, PAIR : 2 * PAIR]).T
    grad_queries = []
    for head in range(2):
        at = head * HEAD_DIM
        span = slice(at, at + HEAD_DIM)
        queries = scaled(qkv_ref[:, span])
        keys = qkv_ref[:, PAIR + at : PAIR + at + HEAD_DIM]
        values = qkv_ref[:, 2 * PAIR + at : 2 * PAIR + at + HEAD_DIM]
        grads = grad_ref[:, span]
        row_terms = jnp.sum(products[span], axis=0, keepdims=True)
        probs = jnp.exp(dot_nt(keys, queries) - log_ref[0, 0, head : head + 1, :])
        grad_scores = (probs * (dot_nt(values, grads) - row_terms)).astype(BF16)
        grad_values = dot_nn(probs.astype(BF16), grads)
        grad_keys = dot_nn(grad_scores, queries)
        result_ref[:, 2 * PAIR + at : 2 * PAIR + at + HEAD_DIM] = grad_values.astype(BF16)
        result_ref[:, PAIR + at : PAIR + at + HEAD_DIM] = grad_keys.astype(BF16)
        grad_queries.append(dot_nn(keys_t[span], grad_scores).astype(BF16))
    result_ref[:, :PAIR] = jnp.concatenate(grad_queries, axis=0).T


def attention_specs():
    return (
        pl.BlockSpec((SEQ, 3 * PAIR), lambda image, pair: (image, pair)),
        pl.BlockSpec((SEQ, PAIR), lambda image, pair: (image, pair)),
        pl.BlockSpec((1, 1, 2, SEQ), lambda image, pair: (image, pair, 0, 0)),
    )


def attention_forward(qkv):
    rows = qkv.shape[0]
    images = rows // SEQ
    wide, narrow, logs = attention_specs()
    return call(
        "attention_forward",
        attention_kernel,
        (images, PAIRS),
        [wide],
        [narrow, logs],
        [struct((rows, WIDTH), BF16), struct((images, PAIRS, 2, SEQ), F32)],
    )(qkv)


def attention_backward(qkv, attended, logs_saved, grad_attended):
    wide, narrow, logs = attention_specs()
    return call(
        "attention_backward",
        attention_back_kernel,
        (qkv.shape[0] // SEQ, PAIRS),
        [wide, narrow, logs, narrow],
        wide,
        struct(qkv.shape, BF16),
    )(qkv, attended, logs_saved, grad_attended)


QKV_SPEC = pl.BlockSpec((WIDTH, 3 * WIDTH), lambda *at: (0, 0))
PROJ_SPEC = pl.BlockSpec((WIDTH, WIDTH), lambda *at: (0, 3))
SMALL_SPEC = pl.BlockSpec((WIDTH, LANES), lambda *at: (0, 4 * WIDTH // LANES))


def project_kernel(tokens_ref, weight_ref, small_ref, qkv_ref, act_ref, table_ref):
    @pl.when(pl.program_id(0) == 0)
    def _():
        table = small_ref[...].T
        table_ref[...] = table
        gain = table[GAIN_ONE : GAIN_ONE + 1].astype(F32)
        normed, _ = norm_parts(tokens_ref[...].astype(F32))
        act_ref[...] = (normed * gain).astype(BF16)

    qkv_ref[...] = dot_nn(act_ref[...], weight_ref[...]).astype(BF16)


def project(tokens, dense):
    rows = tokens.shape[0]
    return call(
        "project",
        project_kernel,
        (PAIRS,),
        [
            whole(rows, WIDTH),
            pl.BlockSpec((WIDTH, 3 * PAIR), lambda pair: (0, pair)),
            SMALL_SPEC,
        ],
        [
            pl.BlockSpec((rows, 3 * PAIR), lambda pair: (0, pair)),
            whole(rows, WIDTH),
            whole(LANES, WIDTH),
        ],
        [
            struct((rows, 3 * WIDTH), BF16),
            struct((rows, WIDTH), BF16),
            struct((LANES, WIDTH), BF16),
        ],
    )(tokens, dense, dense)


def slot_hits(routes_ref, slots_ref):
    rows = routes_ref.shape[1]
    places = lax.broadcasted_iota(jnp.int32, (CAP, rows), 0)
    expert = pl.program_id(0)
    return [
        (routes_ref[k : k + 1, :] == expert) & (slots_ref[k : k + 1, :] == places)
        for k in range(2)
    ]


def middle_kernel(
    routes_ref, slots_ref, tokens_ref, attended_ref, proj_ref, table_ref,
    mid_ref, act_ref, columns_ref, gates_ref, slot_rows_ref,
):
    @pl.when(pl.program_id(0) == 0)
    def _():
        mid = tokens_ref[...].astype(F32) + dot_nn(attended_ref[...], proj_ref[...])
        mid_ref[...] = mid
        normed, _ = norm_parts(mid)
        gain = table_ref[GAIN_TWO : GAIN_TWO + 1, :].astype(F32)
        act = (normed * gain).astype(BF16)
        act_ref[...] = act
        logits = dot_nt(table_ref[:16, :], act)[:EXPERTS]
        powers = jnp.exp(logits - jnp.max(logits, axis=0, keepdims=True))
        router = powers / jnp.sum(powers, axis=0, keepdims=True)
        names = lax.broadcasted_iota(jnp.int32, router.shape, 0)
        gates = [
            jnp.sum(jnp.where(names == routes_ref[k : k + 1, :], router, 0.0), axis=0, keepdims=True)
            .astype(BF16)
            .astype(F32)
            for k in range(2)
        ]
        rows = router.shape[1]
        gates = jnp.concatenate(gates + [jnp.zeros((EXPERTS - 2, rows), F32)], axis=0)
        gates_ref[...] = gates
        spare = jnp.zeros((LANES - 2 * EXPERTS, rows), F32)
        columns_ref[...] = jnp.concatenate([router, gates, spare], axis=0).T

    first, second = slot_hits(routes_ref, slots_ref)
    dispatch = jnp.where(first | second, 1.0, 0.0).astype(BF16)
    slot_rows_ref[0] = dot_nn(dispatch, act_ref[...]).astype(BF16)


def middle(routes_t, slots_t, tokens, attended, dense, table):
    rows = tokens.shape[0]
    return call(
        "middle",
        middle_kernel,
        (EXPERTS,),
        [
            whole(2, rows),
            whole(2, rows),
            whole(rows, WIDTH),
            whole(rows, WIDTH),
            PROJ_SPEC,
            whole(LANES, WIDTH),
        ],
        [
            whole(rows, WIDTH),
            whole(rows, WIDTH),
            whole(rows, LANES),
            whole(EXPERTS, rows),
            pl.BlockSpec((1, CAP, WIDTH), lambda expert: (expert, 0, 0)),
        ],
        [
            struct((rows, WIDTH), F32),
            struct((rows, WIDTH), BF16),
            struct((rows, LANES), F32),
            struct((EXPERTS, rows), F32),
            struct((EXPERTS, CAP, WIDTH), BF16),
        ],
    )(routes_t, slots_t, tokens, attended, dense, table)


def slot_grads_kernel(routes_ref, slots_ref, gates_ref, grad_ref, result_ref):
    first, second = slot_hits(routes_ref, slots_ref)
    combine = jnp.where(first, gates_ref[0:1, :], jnp.where(second, gates_ref[1:2, :], 0.0))
    result_ref[0] = dot_nn(combine.astype(BF16), grad_ref[...]).astype(BF16)


def slot_grads(routes_t, slots_t, gates, cotangent):
    rows = cotangent.shape[0]
    return call(
        "slot_grads",
        slot_grads_kernel,
        (EXPERTS,),
        [whole(2, rows), whole(2, rows), whole(EXPERTS, rows), whole(rows, WIDTH)],
        pl.BlockSpec((1, CAP, WIDTH), lambda expert: (expert, 0, 0)),
        struct((EXPERTS, CAP, WIDTH), BF16),
    )(routes_t, slots_t, gates, cotangent)


def expert_up_kernel(rows_ref, weight_ref, hidden_ref, slope_ref):
    root = math.sqrt(2.0 / math.pi)
    value = dot_nn(rows_ref[...], weight_ref[...])
    square = value * value
    curve = jnp.tanh(value * (root + (root * 0.044715) * square))
    upper = 0.5 + 0.5 * curve
    hidden_ref[...] = (value * upper).astype(BF16)
    inner = value * (root + (3.0 * root * 0.044715) * square)
    slope_ref[...] = (upper + (0.5 - 0.5 * curve * curve) * inner).astype(BF16)


def expert_up(rows, weight):
    count, depth = rows.shape[0], weight.shape[1]
    wide = pl.BlockSpec((count, F_BLOCK), lambda f: (0, f))
    return call(
        "expert_up",
        expert_up_kernel,
        (depth // F_BLOCK,),
        [whole(count, WIDTH), pl.BlockSpec((WIDTH, F_BLOCK), lambda f: (0, f))],
        [wide, wide],
        [struct((count, depth), BF16)] * 2,
    )(rows, weight)


def expert_down_kernel(hidden_ref, weight_ref, result_ref):
    result_ref[...] = dot_nn(hidden_ref[...], weight_ref[...]).astype(BF16)


def expert_down(hidden, weight):
    count, depth = hidden.shape
    return call(
        "expert_down",
        expert_down_kernel,
        (count // ROW_BLOCK,),
        [pl.BlockSpec((ROW_BLOCK, depth), lambda r: (r, 0)), whole(depth, WIDTH)],
        pl.BlockSpec((ROW_BLOCK, WIDTH), lambda r: (r, 0)),
        struct((count, WIDTH), BF16),
    )(hidden, weight)


def expert_back_kernel(grad_ref, slope_ref, out_ref, in_ref, grad_pre_ref, grad_rows_ref):
    grad_hidden = dot_nt(grad_ref[...], out_ref[...])
    grad_pre = (grad_hidden * slope_ref[...].astype(F32)).astype(BF16)
    grad_pre_ref[...] = grad_pre
    grad_rows_ref[...] = dot_nt(grad_pre, in_ref[...]).astype(BF16)


def expert_back(grad_result, slope, weight_out, weight_in):
    count, depth = slope.shape
    wide = pl.BlockSpec((ROW_BLOCK, depth), lambda r: (r, 0))
    narrow = pl.BlockSpec((ROW_BLOCK, WIDTH), lambda r: (r, 0))
    return call(
        "expert_back",
        expert_back_kernel,
        (count // ROW_BLOCK,),
        [narrow, wide, whole(depth, WIDTH), whole(WIDTH, depth)],
        [wide, narrow],
        [struct((count, depth), BF16), struct((count, WIDTH), BF16)],
    )(grad_result, slope, weight_out, weight_in)


def out_grad_kernel(me_ref, hidden_ref, grad_ref, mine_ref, theirs_ref):
    value = dot_tn(hidden_ref[...], grad_ref[...]).astype(BF16)
    half = value.shape[0] // 2
    first = me_ref[0] == 0
    mine_ref[0, 0] = jnp.where(first, value[:half], value[half:])
    theirs_ref[0, 0] = jnp.where(first, value[half:], value[:half])


def out_grad(me, hidden, grad_result):
    count, depth = hidden.shape
    rest = depth // 16
    half = pl.BlockSpec((1, 1, rest, WIDTH), lambda f, me: (f // 4, lax.rem(f, 4), 0, 0))
    return call(
        "out_grad",
        out_grad_kernel,
        (8,),
        [pl.BlockSpec((count, 2 * rest), lambda f, me: (0, f)), whole(count, WIDTH)],
        [half, half],
        [struct((2, 4, rest, WIDTH), BF16)] * 2,
        scalars=1,
    )(me, hidden, grad_result)


def in_grad_kernel(me_ref, rows_ref, grad_ref, mine_ref, theirs_ref, turned_ref):
    @pl.when(pl.program_id(0) == 0)
    def _():
        turned_ref[...] = rows_ref[...].T

    value = dot_nn(turned_ref[...], grad_ref[...]).astype(BF16)
    value = value.reshape(8, 2, WIDTH // 16, F_BLOCK)
    first = me_ref[0] == 0
    shape = mine_ref.shape
    mine_ref[...] = jnp.where(first, value[:, 0], value[:, 1]).reshape(shape)
    theirs_ref[...] = jnp.where(first, value[:, 1], value[:, 0]).reshape(shape)


def in_grad(me, rows, grad_pre):
    count, depth = grad_pre.shape
    rest = WIDTH // 16
    half = pl.BlockSpec((2, 4, rest, F_BLOCK), lambda f, me: (0, 0, 0, f))
    return call(
        "in_grad",
        in_grad_kernel,
        (depth // F_BLOCK,),
        [whole(count, WIDTH), pl.BlockSpec((count, F_BLOCK), lambda f, me: (0, f))],
        [half, half],
        [struct((2, 4, rest, depth), BF16)] * 2,
        scratch=[pltpu.VMEM((WIDTH, count), BF16)],
        scalars=1,
    )(me, rows, grad_pre)


def token_hits(targets_ref):
    columns = lax.broadcasted_iota(jnp.int32, (targets_ref.shape[0], SLOTS), 1)
    return [targets_ref[:, k : k + 1] == columns for k in range(2)]


def combine_kernel(
    routes_ref, targets_ref, columns_ref, mid_ref, grad_ref, result_ref, output_ref, logits_ref
):
    first, second = token_hits(targets_ref)
    gates = columns_ref[:, EXPERTS : EXPERTS + 2]
    combine = jnp.where(first, gates[:, 0:1], jnp.where(second, gates[:, 1:2], 0.0)).astype(BF16)
    output_ref[...] = (mid_ref[...] + dot_nn(combine, result_ref[...])).astype(BF16)
    crossed = dot_nt(grad_ref[...], result_ref[...])
    lanes = lax.broadcasted_iota(jnp.int32, columns_ref.shape, 1)
    grad_router = jnp.zeros(columns_ref.shape, F32)
    for k, hits in enumerate((first, second)):
        grad_gate = jnp.sum(jnp.where(hits, crossed, 0.0), axis=1, keepdims=True)
        grad_router += jnp.where(lanes == routes_ref[:, k : k + 1], grad_gate, 0.0)
    router = jnp.where(lanes < EXPERTS, columns_ref[...], 0.0)
    total = jnp.sum(router * grad_router, axis=1, keepdims=True)
    logits_ref[...] = (router * (grad_router - total)).astype(BF16)


def token_spec(columns):
    return pl.BlockSpec((TOKEN_BLOCK, columns), lambda t: (t, 0))


def combine_results(routes, targets, columns, mid, cotangent, result):
    rows = mid.shape[0]
    return call(
        "combine",
        combine_kernel,
        (rows // TOKEN_BLOCK,),
        [
            token_spec(2),
            token_spec(2),
            token_spec(LANES),
            token_spec(WIDTH),
            token_spec(WIDTH),
            whole(SLOTS, WIDTH),
        ],
        [token_spec(WIDTH), token_spec(LANES)],
        [struct((rows, WIDTH), BF16), struct((rows, LANES), BF16)],
    )(routes, targets, columns, mid, cotangent, result)


def middle_back_kernel(
    targets_ref, logits_ref, mid_ref, grad_ref, rows_ref, proj_ref, table_ref,
    grad_mid_ref, low_ref, attended_ref, gain_ref,
):
    first, second = token_hits(targets_ref)
    dispatch = jnp.where(first | second, 1.0, 0.0).astype(BF16)
    grad_act = dot_nn(dispatch, rows_ref[...]) + dot_nn(logits_ref[...], table_ref[...])
    normed, inverse = norm_parts(mid_ref[...])
    gain = table_ref[GAIN_TWO : GAIN_TWO + 1, :].astype(F32)
    part = jnp.sum(grad_act * normed, axis=0, keepdims=True)

    @pl.when(pl.program_id(0) == 0)
    def _():
        gain_ref[...] = jnp.zeros_like(gain_ref)

    gain_ref[0:1, :] += part
    grad_mid = grad_ref[...].astype(F32) + norm_back(grad_act * gain, normed, inverse)
    grad_mid_ref[...] = grad_mid
    low = grad_mid.astype(BF16)
    low_ref[...] = low
    attended_ref[...] = dot_nt(low, proj_ref[...]).astype(BF16)


def middle_back(targets, logits, mid, cotangent, grad_rows, dense, table):
    rows = mid.shape[0]
    return call(
        "middle_back",
        middle_back_kernel,
        (rows // TOKEN_BLOCK,),
        [
            token_spec(2),
            token_spec(LANES),
            token_spec(WIDTH),
            token_spec(WIDTH),
            whole(SLOTS, WIDTH),
            PROJ_SPEC,
            whole(LANES, WIDTH),
        ],
        [token_spec(WIDTH), token_spec(WIDTH), token_spec(WIDTH), whole(8, WIDTH)],
        [
            struct((rows, WIDTH), F32),
            struct((rows, WIDTH), BF16),
            struct((rows, WIDTH), BF16),
            struct((8, WIDTH), F32),
        ],
    )(targets, logits, mid, cotangent, grad_rows, dense, table)


def write_halves(value, first, mine_ref, theirs_ref):
    value = value.reshape(2, 4, 2, 2, value.shape[0] // 32, value.shape[1])
    for x, y, z in ((x, y, z) for x in range(2) for y in range(2) for z in range(4)):
        low, high = value[x, z, y, 0], value[x, z, y, 1]
        mine_ref[x, y, z] = jnp.where(first, low, high).astype(BF16)
        theirs_ref[x, y, z] = jnp.where(first, high, low).astype(BF16)


def proj_grads_kernel(
    me_ref, attended_ref, low_ref, act_ref, logits_ref, gain_ref, mine_ref, theirs_ref
):
    wide = dot_tn(attended_ref[...], low_ref[...])
    small = dot_tn(act_ref[...], logits_ref[...])
    lanes = lax.broadcasted_iota(jnp.int32, small.shape, 1)
    gain = gain_ref[...].T[:, 0:1]
    value = jnp.concatenate([wide, jnp.where(lanes == GAIN_TWO, gain, small)], axis=1)
    write_halves(value, me_ref[0] == 0, mine_ref, theirs_ref)


def proj_grads(me, attended, low, act_two, logits, gain):
    rows = low.shape[0]
    half = (2, 2, 4, WIDTH // 32, WIDTH + LANES)
    return call(
        "proj_grads",
        proj_grads_kernel,
        (1,),
        [whole(rows, WIDTH)] * 3 + [whole(rows, LANES), whole(8, WIDTH)],
        [whole(*half)] * 2,
        [struct(half, BF16)] * 2,
        scalars=1,
    )(me, attended, low, act_two, logits, gain)


def qkv_grads_kernel(me_ref, act_ref, grad_ref, mine_ref, theirs_ref, turned_ref):
    @pl.when(pl.program_id(0) == 0)
    def _():
        turned_ref[...] = act_ref[...].T

    value = dot_nn(turned_ref[...], grad_ref[...])
    write_halves(value, me_ref[0] == 0, mine_ref, theirs_ref)


def qkv_grads(me, act_one, grad_qkv):
    rows = act_one.shape[0]
    half = (2, 2, 4, WIDTH // 32)
    spec = pl.BlockSpec(half + (3 * PAIR,), lambda pair, me: (0, 0, 0, 0, pair))
    return call(
        "qkv_grads",
        qkv_grads_kernel,
        (PAIRS,),
        [whole(rows, WIDTH), pl.BlockSpec((rows, 3 * PAIR), lambda pair, me: (0, pair))],
        [spec, spec],
        [struct(half + (3 * WIDTH,), BF16)] * 2,
        scratch=[pltpu.VMEM((WIDTH, rows), BF16)],
        scalars=1,
    )(me, act_one, grad_qkv)


def token_grads_kernel(grad_ref, weight_ref, tokens_ref, grad_mid_ref, table_ref, result_ref):
    grad_act = dot_nt(grad_ref[...], weight_ref[...])
    normed, inverse = norm_parts(tokens_ref[...].astype(F32))
    gain = table_ref[GAIN_ONE : GAIN_ONE + 1, :].astype(F32)
    result_ref[...] = grad_mid_ref[...] + norm_back(grad_act * gain, normed, inverse)


def token_grads(grad_qkv, dense, tokens, grad_mid, table):
    rows = tokens.shape[0]
    return call(
        "token_grads",
        token_grads_kernel,
        (rows // TOKEN_BLOCK,),
        [token_spec(3 * WIDTH), QKV_SPEC, token_spec(WIDTH), token_spec(WIDTH), whole(LANES, WIDTH)],
        token_spec(WIDTH),
        struct((rows, WIDTH), F32),
    )(grad_qkv, dense, tokens, grad_mid, table)


def by_pair(columns):
    rows = columns.shape[0]
    return columns.reshape(rows, 3, PAIRS, PAIR).transpose(0, 2, 1, 3).reshape(rows, -1)


def by_part(columns):
    rows = columns.shape[0]
    return columns.reshape(rows, PAIRS, 3, PAIR).transpose(0, 2, 1, 3).reshape(rows, -1)


def place_kernel(count, me_ref, *refs):
    pieces, result_ref = refs[:-1], refs[-1]
    at = 0
    for axis in range(count):
        at = 2 * at + lax.rem(pl.program_id(axis) + me_ref[axis], 2)
    for index, piece in enumerate(pieces):

        @pl.when(at == index)
        def _():
            result_ref[...] = piece[...].reshape(result_ref.shape)


def place(me, pieces, axes):
    count = len(axes)
    shape = list(pieces[0].shape)
    for axis in axes:
        shape.insert(axis, 2)
    block = [1 if axis in axes else size for axis, size in enumerate(shape)]

    def index(*at):
        return tuple(at[axes.index(a)] if a in axes else 0 for a in range(len(shape)))

    return call(
        "place",
        lambda *refs: place_kernel(count, *refs),
        (2,) * count,
        [whole(*piece.shape) for piece in pieces],
        pl.BlockSpec(tuple(block), index),
        struct(tuple(shape), pieces[0].dtype),
        scalars=1,
    )(me, *pieces)


def join_kernel(bounds, me_ref, near_ref, near_core_ref, *refs):
    zh, core = me_ref[0], me_ref[1]
    result_ref = refs[-1]
    result_ref[zh, 0, core] = near_ref[0]
    result_ref[zh, 0, 1 - core] = near_core_ref[0]
    for part, (begin, end) in enumerate(bounds):

        @pl.when((pl.program_id(0) >= begin) & (pl.program_id(0) < end))
        def _():
            result_ref[1 - zh, 0, core] = refs[part][0]
            result_ref[1 - zh, 0, 1 - core] = refs[len(bounds) + part][0]


def join(me, near, near_core, far, far_core):
    blocks, rest, columns = near.shape
    bounds, end = [], 0
    for part in far:
        bounds.append((end, end + part.shape[0]))
        end += part.shape[0]

    def piece(begin, end):
        return pl.BlockSpec(
            (1, rest, columns), lambda b, me: (jnp.clip(b - begin, 0, end - begin - 1), 0, 0)
        )

    return call(
        "join",
        lambda *refs: join_kernel(bounds, *refs),
        (blocks,),
        [piece(0, blocks)] * 2 + [piece(*at) for at in bounds] * 2,
        pl.BlockSpec((2, 1, 2, rest, columns), lambda b, me: (0, b, 0, 0, 0)),
        struct((2, blocks, 2, rest, columns), near.dtype),
        scalars=1,
    )(me, near, near_core, *far, *far_core).reshape(-1, columns)


def parts_of(columns):
    return 3 if columns % (3 * LANES) == 0 else 1


def columns_of(shape):
    block = tuple(shape[:-1]) + (shape[-1] // parts_of(shape[-1]),)
    return pl.BlockSpec(block, lambda i, me: (0,) * (len(shape) - 1) + (i,))


def pick_kernel(count, me_ref, *refs):
    parts, outs = refs[:-count], refs[-count:]
    places = [(ref, at) for ref in parts for at in range(ref.shape[0])]
    for place_at, (part, at) in enumerate(places):
        for k, ref in enumerate(outs):

            @pl.when((me_ref[0] ^ k) == place_at)
            def _():
                ref[...] = part[at]


def pick(me, *parts):
    count, shape = sum(part.shape[0] for part in parts), parts[0].shape[1:]
    return call(
        "pick",
        lambda *refs: pick_kernel(count, *refs),
        (parts_of(shape[-1]),),
        [columns_of(part.shape) for part in parts],
        [columns_of(shape)] * count,
        [struct(shape, BF16)] * count,
        scalars=1,
    )(me, *parts)


def pack_kernel(me_ref, *refs):
    for k, ref in enumerate(refs[:-1]):
        refs[-1][me_ref[0] ^ k] = ref[...].astype(refs[-1].dtype)


def pack(me, pieces, dtype=BF16):
    shape = (len(pieces),) + pieces[0].shape
    return call(
        "pack",
        pack_kernel,
        (parts_of(shape[-1]),),
        [columns_of(shape[1:])] * len(pieces),
        columns_of(shape),
        struct(shape, dtype),
        scalars=1,
    )(me, *pieces)


def add_halves_kernel(me_ref, mine_ref, got_ref, keep_ref, *send_refs):
    def total(at):
        return (mine_ref[at].astype(F32) + got_ref[at].astype(F32)).astype(BF16)

    keep_ref[...] = total(me_ref[0])
    send = total(1 - me_ref[0])
    begin = 0
    for ref in send_refs:
        ref[...] = send[begin : begin + ref.shape[0]]
        begin += ref.shape[0]


def add_halves(me, mine, got, counts):
    shapes = [(count,) + mine.shape[2:] for count in (mine.shape[1],) + counts]
    return call(
        "add_halves",
        add_halves_kernel,
        (parts_of(mine.shape[-1]),),
        [columns_of(mine.shape)] * 2,
        [columns_of(shape) for shape in shapes],
        [struct(shape, BF16) for shape in shapes],
        scalars=1,
    )(me, mine, got)


def add_pick_kernel(me_ref, mine_ref, *refs):
    gots, outs = refs[: -mine_ref.shape[0]], refs[-mine_ref.shape[0] :]
    got = jnp.concatenate([ref[...] for ref in gots], axis=0).astype(F32)
    for at in range(mine_ref.shape[0]):
        value = (mine_ref[at].astype(F32) + got[at]).astype(BF16)
        for k, ref in enumerate(outs):

            @pl.when((me_ref[0] ^ k) == at)
            def _():
                ref[...] = value


def add_pick(me, mine, gots):
    count, shape = mine.shape[0], mine.shape[1:]
    return call(
        "add_pick",
        add_pick_kernel,
        (parts_of(shape[-1]),),
        [columns_of(mine.shape)] + [columns_of(got.shape) for got in gots],
        [columns_of(shape)] * count,
        [struct(shape, BF16)] * count,
        scalars=1,
    )(me, mine, *gots)


def dense_pick_kernel(me_ref, *refs):
    outs = refs[-4:]
    begin = 0
    for mine_ref, got_ref in zip(refs[:-4:2], refs[1:-4:2]):
        end = begin + mine_ref.shape[-1]
        for at in range(4):
            value = (mine_ref[at].astype(F32) + got_ref[at].astype(F32)).astype(BF16)
            for k, ref in enumerate(outs):

                @pl.when((me_ref[0] ^ k) == at)
                def _():
                    ref[:, begin:end] = value

        begin = end


def dense_pick(me, pairs):
    arrays = [array.reshape(4, -1, array.shape[-1]) for pair in pairs for array in pair]
    shape = (arrays[0].shape[1], sum(array.shape[-1] for array in arrays[::2]))
    half = shape[0] // 2
    return call(
        "dense_pick",
        dense_pick_kernel,
        (2,),
        [pl.BlockSpec((4, half, array.shape[-1]), lambda i, me: (0, i, 0)) for array in arrays],
        [pl.BlockSpec((half, shape[1]), lambda i, me: (i, 0))] * 4,
        [struct(shape, BF16)] * 4,
        scalars=1,
    )(me, *arrays)


def turn_kernel(me_ref, *refs):
    outs = refs[-4:]
    total = sum(ref[...].astype(F32) for ref in refs[:-4])
    total = total.reshape(4, total.shape[0] // 4, total.shape[1])
    for at in range(4):
        value = total[at].astype(BF16)
        for k, ref in enumerate(outs):

            @pl.when((me_ref[0] ^ k) == at)
            def _():
                ref[...] = value


def turn(me, pieces):
    shape = (pieces[0].shape[0] // 4, pieces[0].shape[1])
    return call(
        "turn",
        turn_kernel,
        (1,),
        [whole(*piece.shape) for piece in pieces],
        [whole(*shape)] * 4,
        [struct(shape, BF16)] * 4,
        scalars=1,
    )(me, *pieces)


def together(*values):
    return lax.optimization_barrier(values)


def add(mine, got):
    return (mine.astype(F32) + got.astype(F32)).astype(BF16)


class PairwiseLinks:
    def __init__(self, mesh):
        self.mesh = Mesh(mesh.devices.reshape(2, 2, 2, 2, 2), ("x", "zh", "zl", "y", "c"))
        self.data = ("x", "zh", "zl", "y", "c")
        self.fsdp = ("zh", "zl", "y", "c")
        self.dp = "x"

    def swap(self, value, axis):
        return lax.ppermute(value, axis, [(0, 1), (1, 0)])

    def trade(self, value, axes):
        return lax.all_to_all(value, axes, 0, 0, tiled=True)

    def place_of(self, *axes):
        return jnp.stack([lax.axis_index(axis) for axis in axes]).astype(jnp.int32)

    def core(self):
        return self.place_of("c")

    def number(self, *axes):
        index = 0
        for axis in axes:
            index = 2 * index + lax.axis_index(axis)
        return index.astype(jnp.int32)[None]

    def moved(self, pieces, *axes):
        count = len(pieces)
        routes = [[(i, i ^ k) for i in range(count)] for k in range(count)]
        return [pieces[0]] + [lax.ppermute(pieces[k], axes, routes[k]) for k in range(1, count)]

    def gather(self, dense, w_in, w_out):
        near = ("zl", "y")
        own = pack(self.number("zh", "zl"), self.moved([dense] * 4, "zh", "zl"))
        own, first, second, third, w_in, w_out = together(
            own, w_in[:1], w_in[1:3], w_in[3:], w_in, w_out
        )
        over_y, over_x, first, second, third, w_in = together(
            self.swap(own, "y"), self.swap(own, "x"), self.swap(first, "zh"), second, third, w_in
        )
        firsts = [own, over_y, over_x]
        over_xy = self.swap(over_y, "x")
        second = self.swap(second, "zh")
        in_near = self.trade(w_in, near)
        theirs = [self.swap(value, "c") for value in firsts]
        over_xy, second, third, in_near, w_out = together(over_xy, second, third, in_near, w_out)
        pieces = [value for pair in zip(firsts, theirs) for value in pair]
        pieces += [over_xy, self.swap(over_xy, "c")]
        third = self.swap(third, "zh")
        out_near = self.trade(w_out, near)
        full = place(self.place_of("x", "y", "c"), pieces, (0, 2, 3))
        full = full.reshape(32 * dense.shape[0], dense.shape[1])
        return full, {"in_near": in_near, "in_far": [first, second, third], "out_near": out_near}

    def after_project(self, kept, value):
        value, far, out_near = together(value, kept["in_far"], kept["out_near"])
        kept["in_far"] = self.trade(jnp.concatenate(far, axis=0), ("zl", "y"))
        kept["out_near"] = out_near
        kept["out_far"] = [self.swap(out_near[:2], "zh")]
        return value

    def after_middle(self, kept, *values):
        *values, kept["in_far"], near, first = together(
            *values, kept["in_far"], kept["out_near"], kept["out_far"][0]
        )
        kept["out_near"] = near
        kept["out_far"] = [first, self.swap(near[2:3], "zh")]
        return values

    def before_grads(self, kept, *values):
        *values, near, second = together(*values, kept["out_near"], kept["out_far"][1])
        kept["out_near"] = near
        kept["out_far"] = [kept["out_far"][0], second, self.swap(near[3:], "zh")]
        return values

    def joined(self, near, far):
        cores = [self.swap(part, "c") for part in far]
        return join(self.place_of("zh", "c"), near, self.swap(near, "c"), far, cores)

    def expert_in(self, kept):
        return self.joined(kept["in_near"], [kept["in_far"]])

    def expert_out(self, kept, *values):
        *values, last = together(*values, kept["out_far"][2])
        return *values, self.joined(kept["out_near"], kept["out_far"][:2] + [last])

    def send_slots(self, slots):
        return self.trade(slots, ("x", "zl", "y"))

    def return_slots(self, slots):
        return self.trade(slots, ("x", "zl", "y"))

    def other_core(self, theirs):
        return self.swap(theirs, "c")

    def expert_parts(self, mine, got, counts):
        return add_halves(self.place_of("zh"), mine, got, counts)

    def expert_far(self, parts):
        return parts[0], [self.swap(part, "zh") for part in parts[1:]]

    def expert_pick(self, mine, got):
        return add_pick(self.number("zl", "y"), mine, got)

    def expert_end(self, pieces):
        return pack(self.number("zl", "y"), self.moved(pieces, "zl", "y"), F32)

    def rows_pick(self, *pairs):
        return dense_pick(self.number("x", "y"), pairs)

    def rows_send(self, pieces):
        return self.moved(pieces, "x", "y")

    def rows_turn(self, pieces):
        return turn(self.number("zh", "zl"), pieces)

    def rows_last(self, pieces):
        return self.moved(pieces, "zh", "zl")

    def rows_end(self, pieces):
        return sum(piece.astype(F32) for piece in pieces)


class AxisLinks:
    def __init__(self, mesh):
        self.mesh = mesh
        self.data = ("dp", "fsdp")
        self.fsdp = "fsdp"
        self.dp = "dp"

    def core(self):
        return jnp.zeros((1,), jnp.int32)

    def gather(self, dense, w_in, w_out):
        full = lax.all_gather(dense, self.data, axis=0, tiled=True)
        return full, {"in": w_in, "out": w_out}

    def after_project(self, kept, value):
        return value

    def after_middle(self, kept, *values):
        return values

    def before_grads(self, kept, *values):
        return values

    def full_rows(self, shard):
        return lax.all_gather(shard, "fsdp", axis=1, tiled=True).reshape(-1, shard.shape[-1])

    def expert_in(self, kept):
        return self.full_rows(kept["in"])

    def expert_out(self, kept, *values):
        return *values, self.full_rows(kept["out"])

    def send_slots(self, slots):
        return lax.all_to_all(slots, "dp", 0, 0, tiled=True)

    def return_slots(self, slots):
        return lax.all_to_all(slots, "dp", 0, 0, tiled=True)

    def other_core(self, theirs):
        return theirs

    def expert_parts(self, mine, got, counts):
        return [jnp.stack([mine, got], axis=2).reshape(1, -1, mine.shape[-1])]

    def expert_far(self, parts):
        return parts[0], []

    def expert_pick(self, mine, got):
        return [mine]

    def expert_end(self, pieces):
        return lax.psum_scatter(pieces[0], "fsdp", scatter_dimension=1, tiled=True).astype(F32)

    def rows_pick(self, *pairs):
        value = jnp.concatenate([jnp.stack(pair, axis=3) for pair in pairs], axis=-1)
        value = value.transpose(0, 2, 1, 3, 4, 5)
        return [value.reshape(-1, value.shape[-1]).astype(F32)]

    def rows_send(self, pieces):
        return [lax.psum_scatter(pieces[0], self.data, scatter_dimension=0, tiled=True)]

    def rows_turn(self, pieces):
        return pieces

    def rows_last(self, pieces):
        return pieces

    def rows_end(self, pieces):
        return pieces[0]


def per_device(
    links, tokens, gain_attn, w_qkv, w_proj, gain_moe, w_router, w_in, w_out, routes, slot_ids, cotangent
):
    core = links.core()
    small = jnp.concatenate([w_router, gain_attn[:, None], gain_moe[:, None]], axis=1)
    small = jnp.pad(small, ((0, 0), (0, LANES - small.shape[1])))
    own_qkv = by_pair(w_qkv)
    dense, kept = links.gather(
        jnp.concatenate([own_qkv, w_proj, small], axis=1), w_in, w_out
    )
    routes_t = routes.T
    slots_t = slot_ids.T
    targets = jnp.where(slot_ids < CAP, routes * CAP + slot_ids, -1)

    qkv, act_one, table = project(tokens, dense)
    qkv = links.after_project(kept, qkv)
    attended, logs = attention_forward(qkv)
    mid, act_two, columns, gates, rows_sent = middle(
        routes_t, slots_t, tokens, attended, dense, table
    )
    rows_sent, gates = links.after_middle(kept, rows_sent, gates)
    slot_rows = links.send_slots(rows_sent)
    grads_sent = slot_grads(routes_t, slots_t, gates, cotangent)
    expert_in = links.expert_in(kept)
    grads_sent, slot_rows, expert_in = links.before_grads(kept, grads_sent, slot_rows, expert_in)
    grad_slots = links.send_slots(grads_sent)
    held = slot_rows.shape
    expert_rows = slot_rows.reshape(-1, WIDTH)
    hidden, slope = expert_up(expert_rows, expert_in)
    hidden, expert_out = links.expert_out(kept, hidden)
    result, grad_slots, slope = together(expert_down(hidden, expert_out), grad_slots, slope)
    flat_result = links.return_slots(result.reshape(held)).reshape(SLOTS, WIDTH)
    grad_result = grad_slots.reshape(-1, WIDTH)

    grad_pre, grad_rows = expert_back(grad_result, slope, expert_out, expert_in)
    grad_rows, grad_pre, hidden = together(grad_rows, grad_pre, hidden)
    rows_back = links.return_slots(grad_rows.reshape(held)).reshape(SLOTS, WIDTH)
    out_mine, out_theirs = out_grad(core, hidden, grad_result)
    out_theirs, grad_pre = together(out_theirs, grad_pre)
    out_got = links.other_core(out_theirs)
    in_mine, in_theirs = in_grad(core, expert_rows, grad_pre)
    in_theirs, out_got = together(in_theirs, out_got)
    in_got = links.other_core(in_theirs)
    flat_result, out_parts = together(flat_result, links.expert_parts(out_mine, out_got, (4,)))
    out_keep, out_far = links.expert_far(out_parts)
    output, grad_logits = combine_results(routes, targets, columns, mid, cotangent, flat_result)
    grad_logits, rows_back = together(grad_logits, rows_back)
    grad_mid, low, grad_attended, d_gain = middle_back(
        targets, grad_logits, mid, cotangent, rows_back, dense, table
    )
    rest_mine, rest_theirs = proj_grads(core, attended, low, act_two, grad_logits, d_gain)
    rest_theirs, grad_attended, in_got = together(rest_theirs, grad_attended, in_got)
    in_parts, grad_attended = together(
        links.expert_parts(in_mine, in_got, (1, 3)), grad_attended
    )
    grad_qkv = attention_backward(qkv, attended, logs, grad_attended)
    qkv_mine, qkv_theirs = qkv_grads(core, act_one, grad_qkv)
    qkv_theirs, rest_theirs, grad_qkv, out_far, in_parts = together(
        qkv_theirs, rest_theirs, grad_qkv, out_far, in_parts
    )
    in_keep, in_first = links.expert_far(in_parts[:2])
    rest_got = links.other_core(rest_theirs)
    qkv_got = links.other_core(qkv_theirs)
    qkv_got, rest_got, in_first, in_later = together(qkv_got, rest_got, in_first, in_parts[2:])
    qkv_parts, grad_qkv, out_keep, in_later = together(
        links.rows_pick((qkv_mine, qkv_got), (rest_mine, rest_got)), grad_qkv, out_keep, in_later
    )
    qkv_sent = links.rows_send(qkv_parts)
    _, in_second = links.expert_far([in_keep] + list(in_later))
    grad_tokens = token_grads(grad_qkv, dense, tokens, grad_mid, table)
    out_pieces = links.expert_pick(out_keep, out_far)
    qkv_sent, grad_tokens, out_pieces = together(qkv_sent, grad_tokens, out_pieces)
    turned, out_pieces, in_keep, in_second = together(
        links.rows_turn(qkv_sent), out_pieces, in_keep, in_second
    )
    dense_pieces, out_pieces = together(links.rows_last(turned), out_pieces)
    d_dense = links.rows_end(dense_pieces)
    d_out = links.expert_end(out_pieces)
    d_in = links.expert_end(links.expert_pick(in_keep, in_first + in_second))
    d_qkv = d_dense[:, : 3 * WIDTH]
    d_rest = d_dense[:, 3 * WIDTH :]
    d_gain_attn = jnp.sum(d_qkv * own_qkv.astype(F32), axis=1) / gain_attn.astype(F32)
    return (
        output,
        grad_tokens,
        d_gain_attn,
        by_part(d_qkv),
        d_rest[:, :WIDTH],
        d_rest[:, WIDTH + GAIN_TWO],
        d_rest[:, WIDTH : WIDTH + EXPERTS],
        d_in,
        d_out,
    )


def solution(mesh):
    pairwise = mesh.shape["dp"] == 2 and mesh.shape["fsdp"] == 16
    links = PairwiseLinks(mesh) if pairwise else AxisLinks(mesh)
    rows = P(links.data, None)
    flat = P(links.data)
    expert = P(links.dp, links.fsdp, None)
    return jax.shard_map(
        lambda *arrays: per_device(links, *arrays),
        mesh=links.mesh,
        in_specs=(rows, flat, rows, rows, flat, rows, expert, expert, rows, rows, rows),
        out_specs=(rows, rows, flat, rows, rows, flat, rows, expert, expert),
        check_vma=False,
    )
```
